32 devices in a mesh: parts: 2 (over y), leaf: 4 (over z), top: 4 (over x, core).
Axes of the slice: x: 2, y: 2, z: 4, core: 2. Of those that a mesh axis runs over, the one named last changes fastest.
Arguments:
- right_side: float32 [8, 2560, 256], P(('parts', 'top'), 'leaf'), parts along dimension 0, may hold values from -6 to 6
- leaf_inverse: bfloat16 [8, 2560, 640], P(('parts', 'top'), 'leaf'), parts along dimension 0, as said below
- left_basis: bfloat16 [2, 8, 2560, 128], P(None, ('parts', 'top'), 'leaf'), parts along dimension 1, may hold values from -0.1875 to 0.1875
- right_basis: bfloat16 [2, 8, 2560, 128], P(None, ('parts', 'top'), 'leaf'), parts along dimension 1, may hold values from -6 to 6
- level_caps: bfloat16 [2, 8, 512, 256], P(None, ('parts', 'top'), 'leaf'), parts along dimension 1, may hold values from -0.375 to 0.375
- top_left: bfloat16 [8, 2560, 128], P(('parts', 'top'), 'leaf'), parts along dimension 0, may hold values from -0.1875 to 0.1875
- top_right: bfloat16 [8, 2560, 128], P(('parts', 'top'), 'leaf'), parts along dimension 0, may hold values from -6 to 6
- top_caps: bfloat16 [1024, 512], P(('parts', 'top')), parts along dimension 0, may hold values from -0.25 to 0.25
Outputs:
- solution: float32 [8, 2560, 256], P(('parts', 'top'), 'leaf'), parts along dimension 0
The draws below stay inside these ranges and needn't reach their ends.
There are 2 independent parts, one for each index of `parts`. The reference program is written for one: setup_inputs(seed, part) draws one part's arguments, and reference() takes and returns one part's arrays. A program takes and returns all parts, laid end to end along the dimension named above; each array names one. Nothing has to cross between parts.
Inputs may be any that keep to these rules, and one draw needn't show every extreme that they name: Each leaf block of leaf_inverse is lower triangular with a positive diagonal.
All inputs are finite; a program needn't handle non-finite values.
Results may differ from the reference program's by a relative error of at most 0.0075.
Values may be sent and summed in bfloat16 or wider, within the bound.
No kernel may reach another device: no remote copies, remote signals or barrier semaphores. Data moves between devices by JAX's collectives and lax.ppermute only.
A program may use at most 64 MiB of HBM per device.

```python
import math
import jax
import jax.numpy as jnp
from jax import lax

LEAF = 640
R = 128
S = 256
LEVELS = 2
LEAVES = 4
TOPS = 4
ROWS = 2560
TOP_RANK = 512


def draw_leaf_inverse(key, part):
    key_lower = jax.random.fold_in(key, 11)
    key_diagonal = jax.random.fold_in(key, 12)
    block_shape = (TOPS, LEAVES, LEAF, LEAF)
    strict_part = 0.5 * jax.random.normal(key_lower, block_shape, jnp.float32) / math.sqrt(LEAF)
    diagonal_values = jax.random.uniform(key_diagonal, (TOPS, LEAVES, LEAF), jnp.float32, 0.5, 1.5)
    row_ids = lax.broadcasted_iota(jnp.int32, (LEAF, LEAF), 0)
    col_ids = lax.broadcasted_iota(jnp.int32, (LEAF, LEAF), 1)
    matrix = jnp.where(row_ids > col_ids, strict_part, 0.0)
    matrix = matrix + jnp.where(row_ids == col_ids, 1.0, 0.0) * diagonal_values[..., :, None]
    return matrix.reshape(TOPS, LEAVES * LEAF, LEAF).astype(jnp.bfloat16)


def level_of(rng, dims, shards, smallest, top_value):
    factor_of = 1.0
    for position, parts in shards:
        heights = jax.random.uniform(jax.random.fold_in(jax.random.fold_in(rng, 6), position), (parts,), jnp.float32, smallest / len(shards), top_value / len(shards))
        factor_of = factor_of * jnp.repeat(jnp.exp(heights), dims[position] // parts).reshape((-1,) + (1,) * (len(dims) - 1 - position))
    return factor_of


def gaussian(key, dims, width, most, shards=(), held_as=jnp.bfloat16):
    level = level_of(key, dims, shards, -0.22, 0.18) if shards else 1.0
    result = jax.random.normal(key, dims, jnp.float32) * width * level
    return jnp.minimum(jnp.maximum(result, -most), most).astype(held_as)


def setup_inputs(seed: int = 0, part: int = 0) -> dict:
    key_list = jax.random.split(jax.random.key(seed), 9)
    own_keys = jax.random.split(jax.random.fold_in(key_list[8], part), 9)
    right_side = gaussian(own_keys[0], (TOPS, ROWS, S), 1.0, 6.0, ((0, 4), (1, 4)), jnp.float32)
    leaf_inverse = draw_leaf_inverse(jax.random.fold_in(jax.random.fold_in(key_list[8], part), 71), part)
    left_basis = gaussian(own_keys[2], (LEVELS, TOPS, ROWS, R), (8 * R) ** -0.5, 0.1875, ((1, 4), (2, 4)))
    right_basis = gaussian(own_keys[3], (LEVELS, TOPS, ROWS, R), 1.0, 6.0, ((1, 4), (2, 4)))
    level_caps = gaussian(own_keys[4], (LEVELS, TOPS, LEAVES * R, 2 * R), (2 * R) ** -0.5, 0.375, ((1, 4), (2, 4)))
    top_left = gaussian(own_keys[5], (TOPS, ROWS, R), (8 * R) ** -0.5, 0.1875, ((0, 4), (1, 4)))
    top_right = gaussian(own_keys[6], (TOPS, ROWS, R), 1.0, 6.0, ((0, 4), (1, 4)))
    top_caps = gaussian(own_keys[7], (TOP_RANK, TOP_RANK), TOP_RANK ** -0.5, 0.25, ((0, 4),))
    return dict(right_side=right_side, leaf_inverse=leaf_inverse, left_basis=left_basis, right_basis=right_basis, level_caps=level_caps, top_left=top_left, top_right=top_right, top_caps=top_caps)


def rounded(values):
    return lax.optimization_barrier(values.astype(jnp.bfloat16)).astype(jnp.float32)

def project_blocks(basis, current):
    return jnp.einsum('tdlr,tdls->tdrs', basis.astype(jnp.float32), rounded(current), precision=lax.Precision.HIGHEST)

def level_update(current, project_basis, update_basis, caps_rows, level_num):
    top_count, leaf_count, leaf_rows, columns = current.shape
    half_size = 2 ** (level_num - 1)
    node_count = leaf_count // (2 * half_size)
    partial_value = project_blocks(project_basis, current) * (1.0 / math.sqrt(leaf_rows * half_size))
    half_sums = partial_value.reshape(top_count, node_count, 2, half_size, R, columns).sum(axis=3)
    stacked = rounded(half_sums.reshape(top_count, node_count, 2 * R, columns))
    stacked = jnp.repeat(stacked, 2 * half_size, axis=1)
    weights = rounded(jnp.einsum('tdqp,tdps->tdqs', caps_rows.astype(jnp.float32), stacked, precision=lax.Precision.HIGHEST))
    return current - jnp.einsum('tdlq,tdqs->tdls', update_basis.astype(jnp.float32), weights, precision=lax.Precision.HIGHEST)

def top_update(current, project_basis, update_basis, caps_matrix):
    top_count, leaf_count, leaf_rows, columns = current.shape
    partial_value = project_blocks(project_basis, current) * (1.0 / math.sqrt(leaf_count * leaf_rows))
    stacked = rounded(partial_value.sum(axis=1).reshape(top_count * R, columns))
    weights = rounded(jnp.dot(caps_matrix.astype(jnp.float32), stacked, precision=lax.Precision.HIGHEST))
    weights = weights.reshape(top_count, R, columns)
    return current - jnp.einsum('tdlq,tqs->tdls', update_basis.astype(jnp.float32), weights, precision=lax.Precision.HIGHEST)

def reference(right_side, leaf_inverse, left_basis, right_basis, level_caps, top_left, top_right, top_caps):
    inverse_blocks = leaf_inverse.reshape(TOPS, LEAVES, LEAF, LEAF).astype(jnp.float32)
    lefts = left_basis.reshape(LEVELS, TOPS, LEAVES, LEAF, R)
    rights = right_basis.reshape(LEVELS, TOPS, LEAVES, LEAF, R)
    caps_blocks = level_caps.reshape(LEVELS, TOPS, LEAVES, R, 2 * R)
    top_lefts = top_left.reshape(TOPS, LEAVES, LEAF, R)
    top_rights = top_right.reshape(TOPS, LEAVES, LEAF, R)
    current = jnp.einsum('tdij,tdjs->tdis', inverse_blocks, rounded(right_side.reshape(TOPS, LEAVES, LEAF, S)), precision=lax.Precision.HIGHEST)
    for level_num in range(1, LEVELS + 1):
        current = level_update(current, rights[level_num - 1], lefts[level_num - 1], caps_blocks[level_num - 1], level_num)
    current = top_update(current, top_rights, top_lefts, top_caps)
    current = top_update(current, top_lefts, top_rights, top_caps)
    for level_num in range(LEVELS, 0, -1):
        current = level_update(current, lefts[level_num - 1], rights[level_num - 1], caps_blocks[level_num - 1], level_num)
    current = jnp.einsum('tdji,tdjs->tdis', inverse_blocks, rounded(current), precision=lax.Precision.HIGHEST)
    return current.reshape(TOPS, LEAVES * LEAF, S)
```

```python
import math

import jax
import jax.numpy as jnp
from jax import lax
from jax.sharding import PartitionSpec as P

BF = jnp.bfloat16


def swap(value, axis, mask):
    pairs = [(source, source ^ mask) for source in range(lax.axis_size(axis))]
    return lax.ppermute(value, axis, pairs)


def dot(a, b):
    return jnp.dot(a, b, preferred_element_type=jnp.float32)


def dot_t(a, b):
    return lax.dot_general(a, b, (((0,), (0,)), ((), ())), preferred_element_type=jnp.float32)


def level_step(current, project_basis, update_basis, caps_rows, level_num):
    leaf_rows = current.shape[0]
    shift_bits = level_num - 1
    partial_value = dot_t(project_basis, current.astype(BF)) * (
        1.0 / math.sqrt(leaf_rows * 2**shift_bits)
    )
    for bit_index in range(shift_bits):
        partial_value = partial_value + swap(partial_value, "leaf", 2**bit_index)
    own = partial_value.astype(BF)
    other = swap(own, "leaf", 2**shift_bits)
    upper_side = (lax.axis_index("leaf") >> shift_bits) & 1 == 1
    stacked = ordered(upper_side, own, other)
    weights = dot(caps_rows, stacked).astype(BF)
    return current - dot(update_basis, weights)


def top_step(current, project_basis, update_basis, caps_rows):
    leaf_count = lax.axis_size("leaf")
    partial_value = dot_t(project_basis, current.astype(BF)) * (
        1.0 / math.sqrt(leaf_count * current.shape[0])
    )
    column_total = lax.psum(partial_value, "leaf")
    stacked = lax.all_gather(column_total.astype(BF), "top", axis=0, tiled=True)
    weights = dot(caps_rows, stacked).astype(BF)
    return current - dot(update_basis, weights)


def step_by_step(rhs, inverse, lefts, rights, caps, top_left, top_right, top_caps):
    levels = len(lefts)
    current = dot(inverse, rhs.astype(BF))
    for k in range(levels):
        current = level_step(current, rights[k], lefts[k], caps[k], k + 1)
    current = top_step(current, top_right, top_left, top_caps)
    current = top_step(current, top_left, top_right, top_caps)
    for k in reversed(range(levels)):
        current = level_step(current, lefts[k], rights[k], caps[k], k + 1)
    return dot_t(inverse, current.astype(BF))


def ordered(upper_side, own, other):
    return jnp.where(
        upper_side, jnp.concatenate([other, own], 0), jnp.concatenate([own, other], 0)
    )


def halves(upper_side, value):
    width = value.shape[1] // 2
    low, high = value[:, :width], value[:, width:]
    return jnp.where(upper_side, high, low), jnp.where(upper_side, low, high)


def gather_top(value):
    count = lax.axis_size("top")
    if count != 4:
        return lax.all_gather(value, "top")
    index = lax.axis_index("top")
    far = swap(value, "top", 2)
    near = swap(value, "top", 1)
    far_near = swap(far, "top", 1)
    odd, high = index & 1 == 1, index & 2 == 2
    pair = jnp.where(odd, jnp.stack([near, value]), jnp.stack([value, near]))
    far_pair = jnp.where(odd, jnp.stack([far_near, far]), jnp.stack([far, far_near]))
    return jnp.where(
        high, jnp.concatenate([far_pair, pair], 0), jnp.concatenate([pair, far_pair], 0)
    )


def two_levels(rhs, inverse, lefts, rights, caps, top_left, top_right, top_caps):
    leaf_rows = rhs.shape[0]
    rank = top_left.shape[1]
    s1 = 1.0 / math.sqrt(leaf_rows)
    s2 = 1.0 / math.sqrt(leaf_rows * 2)
    st = 1.0 / math.sqrt(leaf_rows * 4)
    leaf = lax.axis_index("leaf")
    odd, high = leaf & 1 == 1, leaf & 2 == 2
    left1, left2 = lefts
    right1, right2 = rights
    caps1, caps2 = caps

    def cat(*values):
        return jnp.concatenate([v.astype(BF) for v in values], 1)

    def cut(value, *widths):
        out, at = [], 0
        for w in widths:
            out.append(value[:, at * rank : (at + w) * rank])
            at += w
        return out

    start = dot(inverse, rhs.astype(BF))
    proj1 = (dot_t(right1, start.astype(BF)) * s1).astype(BF)
    proj1_sib = swap(proj1, "leaf", 1)

    gram_rl = (dot_t(top_right, left2) * st).astype(BF)
    gram_ll = (dot_t(top_left, left2) * st).astype(BF)
    gram_top = dot_t(top_left, top_left) * st
    next3, next4 = dot(gram_rl, caps2), dot(gram_ll, caps2)
    down5 = cat(dot_t(left2, top_left) * s2, dot_t(left2, top_right) * s2)
    down6 = cat(
        dot_t(left1, top_left) * s1, dot_t(left1, top_right) * s1, dot_t(left1, right2) * s1
    )
    early = swap(cat(next3, next4, gram_top), "leaf", 1)
    all_caps = gather_top(top_caps)
    next3_sib, next4_sib, gram_sib = cut(early, 2, 2, 1)
    next3, next4, gram_top = next3 + next3_sib, next4 + next4_sib, gram_top + gram_sib
    next3_own, next3_send = halves(high, next3)
    next4_own, next4_send = halves(high, next4)
    cross = swap(cat(next3_send, next4_send, gram_top), "leaf", 2)
    next3_far, next4_far, gram_far = cut(cross, 1, 1, 1)
    gram_top = gram_top + gram_far

    coef1 = dot(caps1, ordered(odd, proj1, proj1_sib)).astype(BF)
    state1 = start - dot(left1, coef1)
    state1_b = state1.astype(BF)
    proj2 = dot_t(right2, state1_b) * s2
    proj3 = dot_t(top_right, state1_b) * st
    proj4 = dot_t(top_left, state1_b) * st
    keep3, send3 = halves(odd, proj3)
    keep4, send4 = halves(odd, proj4)
    pair_in = swap(cat(proj2, send3, send4), "leaf", 1)
    in2, in3, in4 = cut(pair_in, 2, 1, 1)
    half2 = (proj2 + in2).astype(BF)
    half2_keep, _ = halves(odd, half2)
    half3 = keep3 + in3 - dot(next3_own.astype(BF), half2_keep)
    half4 = keep4 + in4 - dot(next4_own.astype(BF), half2_keep)
    cross_in = swap(cat(half2, half3, half4), "leaf", 2)
    far2, far3, far4 = cut(cross_in, 2, 1, 1)
    far2_keep, _ = halves(odd, far2)
    column3 = (
        half3 + far3 - dot(next3_send.astype(BF), far2_keep) - dot(next3_far, half2_keep)
    )
    column4 = (
        half4 + far4 - dot(next4_send.astype(BF), far2_keep) - dot(next4_far, half2_keep)
    )
    top_in = gather_top(cat(column3, column4, gram_top))

    late = swap(cat(down5, down6, caps2), "leaf", 1)
    down5_sib, down6_sib, caps2_sib = cut(late, 2, 3, 2)
    down5 = (down5.astype(jnp.float32) + down5_sib).astype(BF)
    down5_far = swap(down5, "leaf", 2)

    coef2 = dot(caps2, ordered(high, half2, far2)).astype(BF)
    state2 = state1 - dot(left2, coef2)
    state2_b = state2.astype(BF)
    down_proj5 = dot_t(left2, state2_b) * s2
    down_proj6 = dot_t(left1, state2_b) * s1
    down_in = swap(cat(down_proj5, down_proj6), "leaf", 1)
    down5_in, down6_in = cut(down_in, 2, 2)
    down_half5 = down_proj5 + down5_in
    down_far5 = swap(down_half5.astype(BF), "leaf", 2)

    stack3 = top_in[:, :, :rank].reshape(-1, rank)
    top_coef_all = dot(all_caps.reshape(-1, all_caps.shape[-1]), stack3).astype(BF)
    turn = lax.dot_general(
        top_in[:, :, 2 * rank :],
        top_coef_all.reshape(-1, rank, rank),
        (((2,), (1,)), ((0,), (0,))),
        preferred_element_type=jnp.float32,
    )
    stack4 = (top_in[:, :, rank : 2 * rank] - turn).astype(BF).reshape(-1, rank)
    up_coef = dot(top_caps, stack3).astype(BF)
    down_coef = dot(top_caps, stack4).astype(BF)
    back = swap(cat(up_coef, down_coef), "leaf", 1)
    up_sib, down_sib = cut(back, 1, 1)

    def columns(own, other):
        return jnp.where(
            odd, jnp.concatenate([other, own], 1), jnp.concatenate([own, other], 1)
        )

    up_coef, down_coef = columns(up_coef, up_sib), columns(down_coef, down_sib)
    both = jnp.concatenate([up_coef, down_coef], 0)
    state4 = state2 - dot(jnp.concatenate([top_left, top_right], 1), both)
    half5 = (down_half5 - dot(down5, both)).astype(BF)
    far5 = (down_far5 - dot(down5_far, both)).astype(BF)
    stack5 = ordered(high, half5, far5)
    coef5 = dot(caps2, stack5).astype(BF)
    coef5_sib = dot(caps2_sib, stack5).astype(BF)
    state5 = state4 - dot(right2, coef5)
    proj6 = (dot_t(left1, state5.astype(BF)) * s1).astype(BF)
    proj6_sib = (down6_in - dot(down6_sib, jnp.concatenate([both, coef5_sib], 0))).astype(BF)
    coef6 = dot(caps1, ordered(odd, proj6, proj6_sib)).astype(BF)
    state6 = state5 - dot(right1, coef6)
    return dot_t(inverse, state6.astype(BF))


def on_device(
    right_side, leaf_inverse, left_basis, right_basis, level_caps, top_left, top_right, top_caps
):
    levels = left_basis.shape[0]
    run = two_levels if levels == 2 and lax.axis_size("leaf") == 4 else step_by_step
    out = run(
        right_side[0],
        leaf_inverse[0],
        [left_basis[k, 0] for k in range(levels)],
        [right_basis[k, 0] for k in range(levels)],
        [level_caps[k, 0] for k in range(levels)],
        top_left[0],
        top_right[0],
        top_caps,
    )
    return out[None]


def solution(mesh):
    rows = P(("parts", "top"), "leaf", None)
    level_rows = P(None, ("parts", "top"), "leaf", None)
    return jax.shard_map(
        on_device,
        mesh=mesh,
        in_specs=(
            rows,
            rows,
            level_rows,
            level_rows,
            level_rows,
            rows,
            rows,
            P(("parts", "top"), None),
        ),
        out_specs=rows,
        check_vma=False,
    )
```

```python
import math

import jax
import jax.numpy as jnp
from jax import lax
from jax.experimental import pallas as pl
from jax.experimental.pallas import tpu as pltpu
from jax.sharding import PartitionSpec as P

BF = jnp.bfloat16


def swap(value, axis, mask):
    pairs = [(source, source ^ mask) for source in range(lax.axis_size(axis))]
    return lax.ppermute(value, axis, pairs)


def dot(a, b):
    return jnp.dot(a, b, preferred_element_type=jnp.float32)


def dot_t(a, b):
    return lax.dot_general(a, b, (((0,), (0,)), ((), ())), preferred_element_type=jnp.float32)


def ordered(upper_side, own, other):
    return jnp.where(
        upper_side, jnp.concatenate([other, own], 0), jnp.concatenate([own, other], 0)
    )


def level_step(current, project_basis, update_basis, caps_rows, level_num):
    leaf_rows = current.shape[0]
    shift_bits = level_num - 1
    partial_value = dot_t(project_basis, current.astype(BF)) * (
        1.0 / math.sqrt(leaf_rows * 2**shift_bits)
    )
    for bit_index in range(shift_bits):
        partial_value = partial_value + swap(partial_value, "leaf", 2**bit_index)
    own = partial_value.astype(BF)
    other = swap(own, "leaf", 2**shift_bits)
    upper_side = (lax.axis_index("leaf") >> shift_bits) & 1 == 1
    stacked = ordered(upper_side, own, other)
    weights = dot(caps_rows, stacked).astype(BF)
    return current - dot(update_basis, weights)


def top_step(current, project_basis, update_basis, caps_rows):
    leaf_count = lax.axis_size("leaf")
    partial_value = dot_t(project_basis, current.astype(BF)) * (
        1.0 / math.sqrt(leaf_count * current.shape[0])
    )
    column_total = lax.psum(partial_value, "leaf")
    stacked = lax.all_gather(column_total.astype(BF), "top", axis=0, tiled=True)
    weights = dot(caps_rows, stacked).astype(BF)
    return current - dot(update_basis, weights)


def step_by_step(
    right_side, leaf_inverse, left_basis, right_basis, level_caps, top_left, top_right, top_caps
):
    levels = left_basis.shape[0]
    lefts = [left_basis[k, 0] for k in range(levels)]
    rights = [right_basis[k, 0] for k in range(levels)]
    current = dot(leaf_inverse[0], right_side[0].astype(BF))
    for k in range(levels):
        current = level_step(current, rights[k], lefts[k], level_caps[k, 0], k + 1)
    current = top_step(current, top_right[0], top_left[0], top_caps)
    current = top_step(current, top_left[0], top_right[0], top_caps)
    for k in reversed(range(levels)):
        current = level_step(current, lefts[k], rights[k], level_caps[k, 0], k + 1)
    return dot_t(leaf_inverse[0], current.astype(BF))[None]


def call(body, outs, *args, scratch=(), hbm=()):
    vmem = pl.BlockSpec(memory_space=pltpu.VMEM)
    anywhere = pl.BlockSpec(memory_space=pl.ANY)
    return pl.pallas_call(
        body,
        out_shape=[jax.ShapeDtypeStruct(shape, dtype) for shape, dtype in outs],
        in_specs=[anywhere if i in hbm else vmem for i in range(len(args))],
        out_specs=[vmem] * len(outs),
        scratch_shapes=list(scratch),
    )(*args)


def side(bit):
    return (lax.axis_index("leaf") >> bit) & 1


def block(index, width):
    return pl.ds(pl.multiple_of(index * width, width), width)


def put_ordered(scratch, upper, own, other):
    rows = own.shape[0]
    scratch[block(upper, rows), :] = own
    scratch[block(1 - upper, rows), :] = other


def two_levels(
    right_side, leaf_inverse, left_basis, right_basis, level_caps, top_left, top_right, top_caps
):
    rows, cols = right_side.shape[1:]
    rank = top_left.shape[2]
    half = cols // 2
    f32 = jnp.float32
    s1 = 1.0 / math.sqrt(rows)
    s2 = 1.0 / math.sqrt(rows * 2)
    st = 1.0 / math.sqrt(rows * 4)
    blocks = rows // rank
    square, wide = (rank, rank), (rank, cols)

    def span(i, n=1):
        return slice(i * rank, (i + n) * rank)

    def start_body(rhs_hbm, inv_hbm, rb_hbm, x_ref, inv_ref, p_ref, rhs_v, rb_v, sems):
        copies = []
        for i in range(blocks):
            copies.append(
                (
                    pltpu.make_async_copy(
                        rhs_hbm.at[0, span(i), :], rhs_v.at[span(i), :], sems.at[0, i]
                    ),
                    pltpu.make_async_copy(
                        inv_hbm.at[0, span(i), span(0, i + 1)],
                        inv_ref.at[span(i), span(0, i + 1)],
                        sems.at[1, i],
                    ),
                )
            )
            copies[i][0].start()
            copies[i][1].start()
        basis = pltpu.make_async_copy(rb_hbm.at[0, 0], rb_v, sems.at[2, 0])
        basis.start()
        for i in range(blocks):
            copies[i][0].wait()
            copies[i][1].wait()
            x_ref[span(i), :] = dot(
                inv_ref[span(i), span(0, i + 1)], rhs_v[span(0, i + 1), :].astype(BF)
            )
        basis.wait()
        p_ref[...] = (dot_t(rb_v[...], x_ref[...].astype(BF)) * s1).astype(BF)

    state0, inverse, proj1 = call(
        start_body,
        [((rows, cols), f32), ((rows, rows), BF), (wide, BF)],
        right_side,
        leaf_inverse,
        right_basis,
        hbm=(0, 1, 2),
        scratch=[
            pltpu.VMEM((rows, cols), f32),
            pltpu.VMEM((rows, rank), BF),
            pltpu.SemaphoreType.DMA((3, blocks)),
        ],
    )
    proj1_sib = swap(proj1, "leaf", 1)

    def early_body(lb, caps, tl, tr, out):
        for i, basis in enumerate((tr, tl)):
            gram = (dot_t(basis[0], lb[1, 0]) * st).astype(BF)
            out[:, span(2 * i, 2)] = dot(gram, caps[1, 0]).astype(BF)
        out[:, span(4)] = (dot_t(tl[0], tl[0]) * st).astype(BF)

    (early,) = call(
        early_body, [((rank, 5 * rank), BF)], left_basis, level_caps, top_left, top_right
    )
    early_sib = swap(early, "leaf", 1)

    def pair_body(own, sib, send, keep, gram, scratch):
        upper = side(1)
        for i in range(2):
            scratch[...] = own[:, span(2 * i, 2)].astype(f32) + sib[:, span(2 * i, 2)]
            send[:, span(i)] = scratch[:, block(1 - upper, rank)].astype(BF)
            keep[:, span(2 * i)] = scratch[:, block(upper, rank)].astype(BF)
            keep[:, span(2 * i + 1)] = send[:, span(i)]
        gram[...] = own[:, span(4)].astype(f32) + sib[:, span(4)]
        send[:, span(2)] = gram[...].astype(BF)

    next_send, next_keep, gram_pair = call(
        pair_body,
        [((rank, 3 * rank), BF), ((rank, 4 * rank), BF), (square, f32)],
        early,
        early_sib,
        scratch=[pltpu.VMEM((rank, 2 * rank), f32)],
    )
    next_far = swap(next_send, "leaf", 2)

    def one_body(x0, p, p_sib, lb, rb, caps, tl, tr, x1, send, keep, stack, scratch):
        odd = side(0)
        put_ordered(stack, odd, p[...], p_sib[...])
        coef = dot(caps[0, 0], stack[...]).astype(BF)
        x1[...] = x0[...] - dot(lb[0, 0], coef)
        state = x1[...].astype(BF)
        keep[:, :cols] = dot_t(rb[1, 0], state) * s2
        send[:, :cols] = keep[:, :cols].astype(BF)
        for i, basis in enumerate((tr, tl)):
            at = slice(cols + i * half, cols + (i + 1) * half)
            scratch[...] = dot_t(basis[0], state) * st
            send[:, at] = scratch[:, block(1 - odd, half)].astype(BF)
            keep[:, at] = scratch[:, block(odd, half)]

    state1, pair_send, pair_keep = call(
        one_body,
        [((rows, cols), f32), ((rank, 2 * cols), BF), ((rank, 2 * cols), f32)],
        state0,
        proj1,
        proj1_sib,
        left_basis,
        right_basis,
        level_caps,
        top_left,
        top_right,
        scratch=[pltpu.VMEM((2 * rank, cols), BF), pltpu.VMEM(wide, f32)],
    )
    pair_in = swap(pair_send, "leaf", 1)

    def half_body(keep, pair, nexts, send, keep2):
        odd = side(0)
        send[:, :cols] = (keep[:, :cols] + pair[:, :cols]).astype(BF)
        own = send[:, block(odd, half)]
        for i in range(2):
            at = slice(cols + i * half, cols + (i + 1) * half)
            keep2[:, i * half : (i + 1) * half] = (
                keep[:, at] + pair[:, at] - dot(nexts[:, span(2 * i)], own)
            )
        send[:, cols:] = keep2[...].astype(BF)

    cross_send, cross_keep = call(
        half_body, [((rank, 2 * cols), BF), (wide, f32)], pair_keep, pair_in, next_keep
    )
    cross_in = swap(cross_send, "leaf", 2)

    def column_body(send, keep2, far, nexts, nexts_far, gram, out):
        odd = side(0)
        own, other = send[:, block(odd, half)], far[:, block(odd, half)]
        for i in range(2):
            at = slice(i * half, (i + 1) * half)
            out[:, at] = (
                keep2[:, at]
                + far[:, cols + i * half : cols + (i + 1) * half]
                - dot(nexts[:, span(2 * i + 1)], other)
                - dot(nexts_far[:, span(i)], own)
            ).astype(BF)
        out[:, 2 * half :] = (gram[...] + nexts_far[:, span(2)]).astype(BF)

    (top_send,) = call(
        column_body,
        [((rank, 2 * half + rank), BF)],
        cross_send,
        cross_keep,
        cross_in,
        next_keep,
        next_far,
        gram_pair,
    )

    def around_top(value):
        far = swap(value, "top", 2)
        near = swap(value, "top", 1)
        return value, near, far, swap(far, "top", 1)

    def two_body(x1, send, far, lb, caps, x2, z5, z, stack):
        put_ordered(stack, side(1), send[:, :cols], far[:, :cols])
        coef = dot(caps[1, 0], stack[...]).astype(BF)
        x2[...] = x1[...] - dot(lb[1, 0], coef)
        state = x2[...].astype(BF)
        z5[...] = dot_t(lb[1, 0], state) * s2
        z[:, :cols] = z5[...].astype(BF)
        z[:, cols:] = (dot_t(lb[0, 0], state) * s1).astype(BF)

    top_parts = around_top(top_send)
    state2, down5, down_send = call(
        two_body,
        [((rows, cols), f32), (wide, f32), ((rank, 2 * cols), BF)],
        state1,
        cross_send,
        cross_in,
        left_basis,
        level_caps,
        scratch=[pltpu.VMEM((2 * rank, cols), BF)],
    )
    down_in = swap(down_send, "leaf", 1)

    def add_body(own, sib, out, out_b):
        out[...] = own[...] + sib[:, :cols]
        out_b[...] = out[...].astype(BF)

    down5, down5_send = call(add_body, [(wide, f32), (wide, BF)], down5, down_in)
    down5_far = swap(down5_send, "leaf", 2)

    def late_body(lb, rb, caps, tl, tr, out):
        for i, basis in enumerate((tl, tr)):
            out[:, span(i)] = (dot_t(lb[1, 0], basis[0]) * s2).astype(BF)
            out[:, span(2 + i)] = (dot_t(lb[0, 0], basis[0]) * s1).astype(BF)
        out[:, span(4)] = (dot_t(lb[0, 0], rb[1, 0]) * s1).astype(BF)
        out[:, span(5, cols // rank)] = caps[1, 0]

    (late,) = call(
        late_body,
        [((rank, 5 * rank + cols), BF)],
        left_basis,
        right_basis,
        level_caps,
        top_left,
        top_right,
    )
    late_sib = swap(late, "leaf", 1)

    def grams_body(own, sib, out):
        out[...] = (own[:, span(0, 2)].astype(f32) + sib[:, span(0, 2)]).astype(BF)

    (gram5,) = call(grams_body, [((rank, 2 * rank), BF)], late, late_sib)
    gram5_far = swap(gram5, "leaf", 2)

    def turn_body(inv, inv_t):
        for r in range(blocks):
            for c in range(r + 1):
                inv_t[span(c), span(r)] = inv[span(r), span(c)].T

    (inverse_t,) = call(turn_body, [((rows, rows), BF)], inverse)

    caps_parts = around_top(top_caps)

    def order_body(a, b, c, d, out):
        here = lax.axis_index("top")
        for i, part in enumerate((a, b, c, d)):
            for k in range(4):
                out[span(i), span(k)] = part[:, block(here ^ k, rank)]

    (caps_all,) = call(order_body, [((4 * rank, 4 * rank), BF)], *caps_parts)

    def top_body(a, b, c, d, caps, out, up, down):
        for i, part in enumerate((a, b, c, d)):
            up[span(i), :] = part[:, :half]
        coef = dot(caps[...], up[...]).astype(BF)
        for i, part in enumerate((a, b, c, d)):
            down[span(i), :] = (
                part[:, half : 2 * half] - dot(part[:, 2 * half :], coef[span(i), :])
            ).astype(BF)
        out[:, :half] = coef[:rank, :]
        out[:, half:] = dot(caps[:rank, :], down[...]).astype(BF)

    (back_send,) = call(
        top_body,
        [(wide, BF)],
        *top_parts,
        caps_all,
        scratch=[pltpu.VMEM((4 * rank, half), BF)] * 2,
    )
    back_in = swap(back_send, "leaf", 1)

    def last_body(
        x2, back, back_sib, down5, down5_far, gram5, gram5_far, late, late_sib,
        z, z_sib, lb, rb, caps, tl, tr, inv_t, out, both, stack, coefs, x6, out_v, sems,
    ):
        odd, high = side(0), side(1)
        for i in range(2):
            at = slice(i * half, (i + 1) * half)
            both[span(i), block(odd, half)] = back[:, at]
            both[span(i), block(1 - odd, half)] = back_sib[:, at]
        put_ordered(
            stack,
            high,
            (down5[...] - dot(gram5[...], both[...])).astype(BF),
            (down5_far[...] - dot(gram5_far[...], both[...])).astype(BF),
        )
        coef5 = dot(caps[1, 0], stack[...]).astype(BF)
        coef5_sib = dot(late_sib[:, span(5, cols // rank)], stack[...]).astype(BF)

        def proj(zs, grams, coef):
            return (
                zs[:, cols:]
                - dot(grams[:, span(2, 2)], both[...])
                - dot(grams[:, span(4)], coef)
            ).astype(BF)

        put_ordered(coefs, odd, proj(z, late, coef5), proj(z_sib, late_sib, coef5_sib))
        coef6 = dot(caps[0, 0], coefs[...]).astype(BF)
        x6[...] = (
            x2[...]
            - dot(tl[0], both[span(0), :])
            - dot(tr[0], both[span(1), :])
            - dot(rb[1, 0], coef5)
            - dot(rb[0, 0], coef6)
        ).astype(BF)
        copies = []
        for c in reversed(range(blocks)):
            out_v[span(c), :] = dot(inv_t[span(c), c * rank :], x6[c * rank :, :])
            copy = pltpu.make_async_copy(out_v.at[span(c), :], out.at[0, span(c), :], sems.at[c])
            copy.start()
            copies.append(copy)
        for copy in copies:
            copy.wait()

    args = (
        state2, back_send, back_in, down5, down5_far, gram5, gram5_far, late, late_sib,
        down_send, down_in, left_basis, right_basis, level_caps, top_left, top_right, inverse_t,
    )
    return pl.pallas_call(
        last_body,
        out_shape=jax.ShapeDtypeStruct((1, rows, cols), f32),
        in_specs=[pl.BlockSpec(memory_space=pltpu.VMEM)] * len(args),
        out_specs=pl.BlockSpec(memory_space=pl.ANY),
        scratch_shapes=[
            pltpu.VMEM((2 * rank, cols), BF),
            pltpu.VMEM((2 * rank, cols), BF),
            pltpu.VMEM((2 * rank, cols), BF),
            pltpu.VMEM((rows, cols), BF),
            pltpu.VMEM((rows, cols), f32),
            pltpu.SemaphoreType.DMA((blocks,)),
        ],
    )(*args)


def on_device(*args):
    levels = args[2].shape[0]
    sizes = lax.axis_size("leaf"), lax.axis_size("top")
    if levels == 2 and sizes == (4, 4):
        return two_levels(*args)
    return step_by_step(*args)


def solution(mesh):
    rows = P(("parts", "top"), "leaf", None)
    level_rows = P(None, ("parts", "top"), "leaf", None)
    return jax.shard_map(
        on_device,
        mesh=mesh,
        in_specs=(
            rows,
            rows,
            level_rows,
            level_rows,
            level_rows,
            rows,
            rows,
            P(("parts", "top"), None),
        ),
        out_specs=rows,
        check_vma=False,
    )
```

```python
import math

import jax
import jax.numpy as jnp
from jax import lax
from jax.experimental import pallas as pl
from jax.experimental.pallas import tpu as pltpu
from jax.sharding import PartitionSpec as P

BF = jnp.bfloat16
VMEM_LIMIT = 8 * 2**20


def swap(value, axis, mask):
    pairs = [(source, source ^ mask) for source in range(lax.axis_size(axis))]
    return lax.ppermute(value, axis, pairs)


def dot(a, b):
    return jnp.dot(a, b, preferred_element_type=jnp.float32)


def dot_t(a, b):
    return lax.dot_general(a, b, (((0,), (0,)), ((), ())), preferred_element_type=jnp.float32)


def ordered(upper_side, own, other):
    return jnp.where(
        upper_side, jnp.concatenate([other, own], 0), jnp.concatenate([own, other], 0)
    )


def level_step(current, project_basis, update_basis, caps_rows, level_num):
    leaf_rows = current.shape[0]
    shift_bits = level_num - 1
    partial_value = dot_t(project_basis, current.astype(BF)) * (
        1.0 / math.sqrt(leaf_rows * 2**shift_bits)
    )
    for bit_index in range(shift_bits):
        partial_value = partial_value + swap(partial_value, "leaf", 2**bit_index)
    own = partial_value.astype(BF)
    other = swap(own, "leaf", 2**shift_bits)
    upper_side = (lax.axis_index("leaf") >> shift_bits) & 1 == 1
    stacked = ordered(upper_side, own, other)
    weights = dot(caps_rows, stacked).astype(BF)
    return current - dot(update_basis, weights)


def top_step(current, project_basis, update_basis, caps_rows):
    leaf_count = lax.axis_size("leaf")
    partial_value = dot_t(project_basis, current.astype(BF)) * (
        1.0 / math.sqrt(leaf_count * current.shape[0])
    )
    column_total = lax.psum(partial_value, "leaf")
    stacked = lax.all_gather(column_total.astype(BF), "top", axis=0, tiled=True)
    weights = dot(caps_rows, stacked).astype(BF)
    return current - dot(update_basis, weights)


def step_by_step(
    right_side, leaf_inverse, left_basis, right_basis, level_caps, top_left, top_right, top_caps
):
    levels = left_basis.shape[0]
    lefts = [left_basis[k, 0] for k in range(levels)]
    rights = [right_basis[k, 0] for k in range(levels)]
    current = dot(leaf_inverse[0], right_side[0].astype(BF))
    for k in range(levels):
        current = level_step(current, rights[k], lefts[k], level_caps[k, 0], k + 1)
    current = top_step(current, top_right[0], top_left[0], top_caps)
    current = top_step(current, top_left[0], top_right[0], top_caps)
    for k in reversed(range(levels)):
        current = level_step(current, lefts[k], rights[k], level_caps[k, 0], k + 1)
    return dot_t(leaf_inverse[0], current.astype(BF))[None]


def call(body, outs, *args, scratch=(), hbm=()):
    vmem = pl.BlockSpec(memory_space=pltpu.VMEM)
    anywhere = pl.BlockSpec(memory_space=pl.ANY)
    return pl.pallas_call(
        body,
        out_shape=[pltpu.VMEM(shape, dtype) for shape, dtype in outs],
        in_specs=[anywhere if i in hbm else vmem for i in range(len(args))],
        out_specs=[vmem] * len(outs),
        scratch_shapes=list(scratch),
        compiler_params=pltpu.CompilerParams(vmem_limit_bytes=VMEM_LIMIT),
    )(*[in_hbm(a) if i in hbm else in_vmem(a) for i, a in enumerate(args)])


def in_hbm(value):
    return pltpu.with_memory_space_constraint(value, pltpu.HBM)


def in_vmem(value):
    return pltpu.with_memory_space_constraint(value, pltpu.VMEM)


def side(bit):
    return (lax.axis_index("leaf") >> bit) & 1


def block(index, width):
    return pl.ds(pl.multiple_of(index * width, width), width)


def put_ordered(scratch, upper, own, other):
    rows = own.shape[0]
    scratch[block(upper, rows), :] = own
    scratch[block(1 - upper, rows), :] = other


def two_levels(
    right_side, leaf_inverse, left_basis, right_basis, level_caps, top_left, top_right, top_caps
):
    rows, cols = right_side.shape[1:]
    rank = top_left.shape[2]
    half = cols // 2
    f32 = jnp.float32
    s1 = 1.0 / math.sqrt(rows)
    s2 = 1.0 / math.sqrt(rows * 2)
    st = 1.0 / math.sqrt(rows * 4)
    blocks = rows // rank
    square, wide = (rank, rank), (rank, cols)

    def span(i, n=1):
        return slice(i * rank, (i + n) * rank)

    def start_body(rhs_hbm, inv_hbm, rb_hbm, x_ref, inv_ref, p_ref, rhs_v, rb_v, sems):
        copies = []
        for i in range(blocks):
            copies.append(
                (
                    pltpu.make_async_copy(
                        rhs_hbm.at[0, span(i), :], rhs_v.at[span(i), :], sems.at[0, i]
                    ),
                    pltpu.make_async_copy(
                        inv_hbm.at[0, span(i), span(0, i + 1)],
                        inv_ref.at[span(i), span(0, i + 1)],
                        sems.at[1, i],
                    ),
                )
            )
            copies[i][0].start()
            copies[i][1].start()
        basis = pltpu.make_async_copy(rb_hbm.at[0, 0], rb_v, sems.at[2, 0])
        basis.start()
        for i in range(blocks):
            copies[i][0].wait()
            copies[i][1].wait()
            x_ref[span(i), :] = dot(
                inv_ref[span(i), span(0, i + 1)], rhs_v[span(0, i + 1), :].astype(BF)
            )
        basis.wait()
        p_ref[...] = (dot_t(rb_v[...], x_ref[...].astype(BF)) * s1).astype(BF)

    state0, inverse, proj1 = call(
        start_body,
        [((rows, cols), f32), ((rows, rows), BF), (wide, BF)],
        right_side,
        leaf_inverse,
        right_basis,
        hbm=(0, 1, 2),
        scratch=[
            pltpu.VMEM((rows, cols), f32),
            pltpu.VMEM((rows, rank), BF),
            pltpu.SemaphoreType.DMA((3, blocks)),
        ],
    )
    proj1_sib = swap(proj1, "leaf", 1)

    def early_body(lb, caps, tl, tr, out):
        for i, basis in enumerate((tr, tl)):
            gram = (dot_t(basis[0], lb[1, 0]) * st).astype(BF)
            out[:, span(2 * i, 2)] = dot(gram, caps[1, 0]).astype(BF)
        out[:, span(4)] = (dot_t(tl[0], tl[0]) * st).astype(BF)

    (early,) = call(
        early_body, [((rank, 5 * rank), BF)], left_basis, level_caps, top_left, top_right
    )
    early_sib = swap(early, "leaf", 1)

    def pair_body(own, sib, send, keep, gram, scratch):
        upper = side(1)
        for i in range(2):
            scratch[...] = own[:, span(2 * i, 2)].astype(f32) + sib[:, span(2 * i, 2)]
            send[:, span(i)] = scratch[:, block(1 - upper, rank)].astype(BF)
            keep[:, span(2 * i)] = scratch[:, block(upper, rank)].astype(BF)
            keep[:, span(2 * i + 1)] = send[:, span(i)]
        gram[...] = own[:, span(4)].astype(f32) + sib[:, span(4)]
        send[:, span(2)] = gram[...].astype(BF)

    next_send, next_keep, gram_pair = call(
        pair_body,
        [((rank, 3 * rank), BF), ((rank, 4 * rank), BF), (square, f32)],
        early,
        early_sib,
        scratch=[pltpu.VMEM((rank, 2 * rank), f32)],
    )
    next_far = swap(next_send, "leaf", 2)

    def one_body(x0, p, p_sib, lb, rb, caps, tl, tr, x1, send, keep, stack, scratch):
        odd = side(0)
        put_ordered(stack, odd, p[...], p_sib[...])
        coef = dot(caps[0, 0], stack[...]).astype(BF)
        x1[...] = x0[...] - dot(lb[0, 0], coef)
        state = x1[...].astype(BF)
        keep[:, :cols] = dot_t(rb[1, 0], state) * s2
        send[:, :cols] = keep[:, :cols].astype(BF)
        for i, basis in enumerate((tr, tl)):
            at = slice(cols + i * half, cols + (i + 1) * half)
            scratch[...] = dot_t(basis[0], state) * st
            send[:, at] = scratch[:, block(1 - odd, half)].astype(BF)
            keep[:, at] = scratch[:, block(odd, half)]

    state1, pair_send, pair_keep = call(
        one_body,
        [((rows, cols), f32), ((rank, 2 * cols), BF), ((rank, 2 * cols), f32)],
        state0,
        proj1,
        proj1_sib,
        left_basis,
        right_basis,
        level_caps,
        top_left,
        top_right,
        scratch=[pltpu.VMEM((2 * rank, cols), BF), pltpu.VMEM(wide, f32)],
    )
    pair_in = swap(pair_send, "leaf", 1)

    def half_body(keep, pair, nexts, send, keep2):
        odd = side(0)
        send[:, :cols] = (keep[:, :cols] + pair[:, :cols]).astype(BF)
        own = send[:, block(odd, half)]
        for i in range(2):
            at = slice(cols + i * half, cols + (i + 1) * half)
            keep2[:, i * half : (i + 1) * half] = (
                keep[:, at] + pair[:, at] - dot(nexts[:, span(2 * i)], own)
            )
        send[:, cols:] = keep2[...].astype(BF)

    cross_send, cross_keep = call(
        half_body, [((rank, 2 * cols), BF), (wide, f32)], pair_keep, pair_in, next_keep
    )
    cross_in = swap(cross_send, "leaf", 2)

    def column_body(send, keep2, far, nexts, nexts_far, gram, out):
        odd = side(0)
        own, other = send[:, block(odd, half)], far[:, block(odd, half)]
        for i in range(2):
            at = slice(i * half, (i + 1) * half)
            out[:, at] = (
                keep2[:, at]
                + far[:, cols + i * half : cols + (i + 1) * half]
                - dot(nexts[:, span(2 * i + 1)], other)
                - dot(nexts_far[:, span(i)], own)
            ).astype(BF)
        out[:, 2 * half :] = (gram[...] + nexts_far[:, span(2)]).astype(BF)

    (top_send,) = call(
        column_body,
        [((rank, 2 * half + rank), BF)],
        cross_send,
        cross_keep,
        cross_in,
        next_keep,
        next_far,
        gram_pair,
    )

    def around_top(value):
        far = swap(value, "top", 2)
        near = swap(value, "top", 1)
        return value, near, far, swap(far, "top", 1)

    def two_body(x1, send, far, lb, caps, x2, z5, z, stack):
        put_ordered(stack, side(1), send[:, :cols], far[:, :cols])
        coef = dot(caps[1, 0], stack[...]).astype(BF)
        x2[...] = x1[...] - dot(lb[1, 0], coef)
        state = x2[...].astype(BF)
        z5[...] = dot_t(lb[1, 0], state) * s2
        z[:, :cols] = z5[...].astype(BF)
        z[:, cols:] = (dot_t(lb[0, 0], state) * s1).astype(BF)

    top_parts = around_top(top_send)
    state2, down5, down_send = call(
        two_body,
        [((rows, cols), f32), (wide, f32), ((rank, 2 * cols), BF)],
        state1,
        cross_send,
        cross_in,
        left_basis,
        level_caps,
        scratch=[pltpu.VMEM((2 * rank, cols), BF)],
    )
    down_in = swap(down_send, "leaf", 1)

    def add_body(own, sib, out, out_b):
        out[...] = own[...] + sib[:, :cols]
        out_b[...] = out[...].astype(BF)

    down5, down5_send = call(add_body, [(wide, f32), (wide, BF)], down5, down_in)
    down5_far = swap(down5_send, "leaf", 2)

    def late_body(lb, rb, caps, tl, tr, out):
        for i, basis in enumerate((tl, tr)):
            out[:, span(i)] = (dot_t(lb[1, 0], basis[0]) * s2).astype(BF)
            out[:, span(2 + i)] = (dot_t(lb[0, 0], basis[0]) * s1).astype(BF)
        out[:, span(4)] = (dot_t(lb[0, 0], rb[1, 0]) * s1).astype(BF)
        out[:, span(5, cols // rank)] = caps[1, 0]

    (late,) = call(
        late_body,
        [((rank, 5 * rank + cols), BF)],
        left_basis,
        right_basis,
        level_caps,
        top_left,
        top_right,
    )
    late_sib = swap(late, "leaf", 1)

    def grams_body(own, sib, out):
        out[...] = (own[:, span(0, 2)].astype(f32) + sib[:, span(0, 2)]).astype(BF)

    (gram5,) = call(grams_body, [((rank, 2 * rank), BF)], late, late_sib)
    gram5_far = swap(gram5, "leaf", 2)

    def turn_body(inv, inv_t):
        for r in range(blocks):
            for c in range(r + 1):
                inv_t[span(c), span(r)] = inv[span(r), span(c)].T

    (inverse_t,) = call(turn_body, [((rows, rows), BF)], inverse)

    caps_parts = around_top(top_caps)

    def order_body(a, b, c, d, out):
        here = lax.axis_index("top")
        for i, part in enumerate((a, b, c, d)):
            for k in range(4):
                out[span(i), span(k)] = part[:, block(here ^ k, rank)]

    (caps_all,) = call(order_body, [((4 * rank, 4 * rank), BF)], *caps_parts)

    def top_body(a, b, c, d, caps, out, up, down):
        for i, part in enumerate((a, b, c, d)):
            up[span(i), :] = part[:, :half]
        coef = dot(caps[...], up[...]).astype(BF)
        for i, part in enumerate((a, b, c, d)):
            down[span(i), :] = (
                part[:, half : 2 * half] - dot(part[:, 2 * half :], coef[span(i), :])
            ).astype(BF)
        out[:, :half] = coef[:rank, :]
        out[:, half:] = dot(caps[:rank, :], down[...]).astype(BF)

    (back_send,) = call(
        top_body,
        [(wide, BF)],
        *top_parts,
        caps_all,
        scratch=[pltpu.VMEM((4 * rank, half), BF)] * 2,
    )
    back_in = swap(back_send, "leaf", 1)

    def last_body(
        x2, back, back_sib, down5, down5_far, gram5, gram5_far, late, late_sib,
        z, z_sib, lb, rb, caps, tl, tr, inv_t, out, both, stack, coefs, x6, out_v, sems,
    ):
        odd, high = side(0), side(1)
        for i in range(2):
            at = slice(i * half, (i + 1) * half)
            both[span(i), block(odd, half)] = back[:, at]
            both[span(i), block(1 - odd, half)] = back_sib[:, at]
        put_ordered(
            stack,
            high,
            (down5[...] - dot(gram5[...], both[...])).astype(BF),
            (down5_far[...] - dot(gram5_far[...], both[...])).astype(BF),
        )
        coef5 = dot(caps[1, 0], stack[...]).astype(BF)
        coef5_sib = dot(late_sib[:, span(5, cols // rank)], stack[...]).astype(BF)

        def proj(zs, grams, coef):
            return (
                zs[:, cols:]
                - dot(grams[:, span(2, 2)], both[...])
                - dot(grams[:, span(4)], coef)
            ).astype(BF)

        put_ordered(coefs, odd, proj(z, late, coef5), proj(z_sib, late_sib, coef5_sib))
        coef6 = dot(caps[0, 0], coefs[...]).astype(BF)
        x6[...] = (
            x2[...]
            - dot(tl[0], both[span(0), :])
            - dot(tr[0], both[span(1), :])
            - dot(rb[1, 0], coef5)
            - dot(rb[0, 0], coef6)
        ).astype(BF)
        copies = []
        for c in reversed(range(blocks)):
            out_v[span(c), :] = dot(inv_t[span(c), c * rank :], x6[c * rank :, :])
            copy = pltpu.make_async_copy(out_v.at[span(c), :], out.at[0, span(c), :], sems.at[c])
            copy.start()
            copies.append(copy)
        for copy in copies:
            copy.wait()

    args = (
        state2, back_send, back_in, down5, down5_far, gram5, gram5_far, late, late_sib,
        down_send, down_in, left_basis, right_basis, level_caps, top_left, top_right, inverse_t,
    )
    return pl.pallas_call(
        last_body,
        out_shape=jax.ShapeDtypeStruct((1, rows, cols), f32),
        in_specs=[pl.BlockSpec(memory_space=pltpu.VMEM)] * len(args),
        out_specs=pl.BlockSpec(memory_space=pl.ANY),
        scratch_shapes=[
            pltpu.VMEM((2 * rank, cols), BF),
            pltpu.VMEM((2 * rank, cols), BF),
            pltpu.VMEM((2 * rank, cols), BF),
            pltpu.VMEM((rows, cols), BF),
            pltpu.VMEM((rows, cols), f32),
            pltpu.SemaphoreType.DMA((blocks,)),
        ],
        compiler_params=pltpu.CompilerParams(vmem_limit_bytes=VMEM_LIMIT),
    )(*[in_vmem(a) for a in args])


def on_device(*args):
    levels = args[2].shape[0]
    sizes = lax.axis_size("leaf"), lax.axis_size("top")
    if levels == 2 and sizes == (4, 4):
        return two_levels(*args)
    return step_by_step(*args)


def solution(mesh):
    rows = P(("parts", "top"), "leaf", None)
    level_rows = P(None, ("parts", "top"), "leaf", None)
    return jax.shard_map(
        on_device,
        mesh=mesh,
        in_specs=(
            rows,
            rows,
            level_rows,
            level_rows,
            level_rows,
            rows,
            rows,
            P(("parts", "top"), None),
        ),
        out_specs=rows,
        check_vma=False,
    )
```

```python
import math

import jax
import jax.numpy as jnp
from jax import lax
from jax.experimental import pallas as pl
from jax.experimental.pallas import tpu as pltpu
from jax.sharding import PartitionSpec as P

BF = jnp.bfloat16
VMEM_LIMIT = 8 * 2**20
FLOPS_PER_MICRO = 1e9


def swap(value, axis, mask):
    pairs = [(source, source ^ mask) for source in range(lax.axis_size(axis))]
    return lax.ppermute(value, axis, pairs)


def dot(a, b):
    return jnp.dot(a, b, preferred_element_type=jnp.float32)


def dot_t(a, b):
    return lax.dot_general(a, b, (((0,), (0,)), ((), ())), preferred_element_type=jnp.float32)


def ordered(upper_side, own, other):
    return jnp.where(
        upper_side, jnp.concatenate([other, own], 0), jnp.concatenate([own, other], 0)
    )


def level_step(current, project_basis, update_basis, caps_rows, level_num):
    leaf_rows = current.shape[0]
    shift_bits = level_num - 1
    partial_value = dot_t(project_basis, current.astype(BF)) * (
        1.0 / math.sqrt(leaf_rows * 2**shift_bits)
    )
    for bit_index in range(shift_bits):
        partial_value = partial_value + swap(partial_value, "leaf", 2**bit_index)
    own = partial_value.astype(BF)
    other = swap(own, "leaf", 2**shift_bits)
    upper_side = (lax.axis_index("leaf") >> shift_bits) & 1 == 1
    stacked = ordered(upper_side, own, other)
    weights = dot(caps_rows, stacked).astype(BF)
    return current - dot(update_basis, weights)


def top_step(current, project_basis, update_basis, caps_rows):
    leaf_count = lax.axis_size("leaf")
    partial_value = dot_t(project_basis, current.astype(BF)) * (
        1.0 / math.sqrt(leaf_count * current.shape[0])
    )
    column_total = lax.psum(partial_value, "leaf")
    stacked = lax.all_gather(column_total.astype(BF), "top", axis=0, tiled=True)
    weights = dot(caps_rows, stacked).astype(BF)
    return current - dot(update_basis, weights)


def step_by_step(
    right_side, leaf_inverse, left_basis, right_basis, level_caps, top_left, top_right, top_caps
):
    levels = left_basis.shape[0]
    lefts = [left_basis[k, 0] for k in range(levels)]
    rights = [right_basis[k, 0] for k in range(levels)]
    current = dot(leaf_inverse[0], right_side[0].astype(BF))
    for k in range(levels):
        current = level_step(current, rights[k], lefts[k], level_caps[k, 0], k + 1)
    current = top_step(current, top_right[0], top_left[0], top_caps)
    current = top_step(current, top_left[0], top_right[0], top_caps)
    for k in reversed(range(levels)):
        current = level_step(current, lefts[k], rights[k], level_caps[k, 0], k + 1)
    return dot_t(leaf_inverse[0], current.astype(BF))[None]


def in_hbm(value):
    return pltpu.with_memory_space_constraint(value, pltpu.HBM)


def in_vmem(value):
    return pltpu.with_memory_space_constraint(value, pltpu.VMEM)


def call(body, outs, *args, scratch=(), hbm=(), hbm_out=False, micros=1):
    vmem = pl.BlockSpec(memory_space=pltpu.VMEM)
    anywhere = pl.BlockSpec(memory_space=pl.ANY)
    return pl.pallas_call(
        body,
        out_shape=[
            jax.ShapeDtypeStruct(shape, dtype) if hbm_out else pltpu.VMEM(shape, dtype)
            for shape, dtype in outs
        ],
        in_specs=[anywhere if i in hbm else vmem for i in range(len(args))],
        out_specs=[anywhere if hbm_out else vmem] * len(outs),
        scratch_shapes=list(scratch),
        compiler_params=pltpu.CompilerParams(vmem_limit_bytes=VMEM_LIMIT),
        cost_estimate=pl.CostEstimate(
            flops=int(micros * FLOPS_PER_MICRO), bytes_accessed=0, transcendentals=0
        ),
    )(*[in_hbm(a) if i in hbm else in_vmem(a) for i, a in enumerate(args)])


def after(value, *others):
    return lax.optimization_barrier((value, *others))[0]


def side(bit):
    return (lax.axis_index("leaf") >> bit) & 1


def block(index, width):
    return pl.ds(pl.multiple_of(index * width, width), width)


def put_rows(scratch, upper, own, other):
    rows = own.shape[0]
    scratch[block(upper, rows), :] = own
    scratch[block(1 - upper, rows), :] = other


def put_columns(out, upper, own, other):
    width = own.shape[1]
    out[:, block(upper, width)] = own
    out[:, block(1 - upper, width)] = other


def two_levels(
    right_side, leaf_inverse, left_basis, right_basis, level_caps, top_left, top_right, top_caps
):
    rows, cols = right_side.shape[1:]
    rank = top_left.shape[2]
    half = cols // 2
    f32 = jnp.float32
    s1 = 1.0 / math.sqrt(rows)
    s2 = 1.0 / math.sqrt(rows * 2)
    st = 1.0 / math.sqrt(rows * 4)
    blocks = rows // rank
    square, wide, tall = (rank, rank), (rank, cols), (rows, cols)

    def span(i, n=1):
        return slice(i * rank, (i + n) * rank)

    def part(i, n=1):
        return slice(i * half, (i + n) * half)

    def around_top(value):
        far = swap(value, "top", 2)
        return value, swap(value, "top", 1), far, swap(far, "top", 1)

    caps_far = swap(top_caps, "top", 2)

    def start_body(
        rhs_hbm, inv_hbm, lb_hbm, rb_hbm, caps_hbm, tl_hbm, tr_hbm,
        x_ref, p_ref, inv_ref, lb, rb, caps, tl, tr, rhs_v, sems,
    ):
        def load(source, target, *at):
            copy = pltpu.make_async_copy(source, target, sems.at[at])
            copy.start()
            return copy

        copies = []
        for i in range(blocks):
            copies.append(load(rhs_hbm.at[0, span(i), :], rhs_v.at[span(i), :], 0, i))
            copies.append(
                load(
                    inv_hbm.at[0, span(i), span(0, i + 1)],
                    inv_ref.at[span(i), span(0, i + 1)],
                    1,
                    i,
                )
            )
        bases = [
            load(source, target, 2, i)
            for i, (source, target) in enumerate(
                ((rb_hbm, rb), (lb_hbm, lb), (tl_hbm, tl), (tr_hbm, tr), (caps_hbm, caps))
            )
        ]
        for i in range(blocks):
            copies[2 * i].wait()
            copies[2 * i + 1].wait()
            x_ref[span(i), :] = dot(
                inv_ref[span(i), span(0, i + 1)], rhs_v[span(0, i + 1), :].astype(BF)
            )
        bases[0].wait()
        p_ref[...] = (dot_t(rb[0, 0], x_ref[...].astype(BF)) * s1).astype(BF)
        for copy in bases[1:]:
            copy.wait()

    state0, proj1, inverse, lb, rb, caps, tl, tr = call(
        start_body,
        [(tall, f32), (wide, BF), ((rows, rows), BF)]
        + [(a.shape, a.dtype) for a in (left_basis, right_basis, level_caps, top_left, top_right)],
        right_side,
        leaf_inverse,
        left_basis,
        right_basis,
        level_caps,
        top_left,
        top_right,
        hbm=range(7),
        scratch=[pltpu.VMEM(tall, f32), pltpu.SemaphoreType.DMA((3, max(blocks, 5)))],
    )
    proj1_sib = swap(proj1, "leaf", 1)
    caps_near = swap(after(top_caps, proj1), "top", 1)
    caps_parts = top_caps, caps_near, caps_far, swap(after(caps_far, proj1), "top", 1)

    def grams_body(lb, caps, tl, tr, seen, out, send, scratch):
        upper = side(1)
        left2, caps2 = lb[1, 0], caps[1, 0]
        for i, (basis, scale) in enumerate(((tr[0], st), (tl[0], st), (left2, s2))):
            gram = (dot_t(basis, left2) * scale).astype(BF)
            scratch[...] = dot(gram, caps2).astype(BF)
            out[:, span(2 * i, 2)] = scratch[...]
            if i < 2:
                send[:, span(i)] = scratch[:, block(1 - upper, rank)]
        out[:, span(6)] = (dot_t(left2, tl[0]) * s2).astype(BF)
        out[:, span(7)] = (dot_t(left2, tr[0]) * s2).astype(BF)
        out[:, span(8)] = (dot_t(tl[0], tl[0]) * st).astype(BF)
        send[:, span(2)] = out[:, span(8)]

    grams, next_send = call(
        grams_body,
        [((rank, 9 * rank), BF), ((rank, 3 * rank), BF)],
        lb,
        caps,
        tl,
        tr,
        caps_near,
        scratch=[pltpu.VMEM((rank, 2 * rank), BF)],
        micros=10,
    )
    grams_sib = swap(grams, "leaf", 1)
    next_far = swap(next_send, "leaf", 2)

    def one_body(x0, p, p_sib, lb, rb, caps, tl, tr, x1, send, keep, y6, stack, scratch):
        odd = side(0)
        put_rows(stack, odd, p[...], p_sib[...])
        coef = dot(caps[0, 0], stack[...]).astype(BF)
        x1[...] = x0[...] - dot(lb[0, 0], coef)
        state = x1[...].astype(BF)
        bases = ((rb[1, 0], s2), (tr[0], st), (tl[0], st), (lb[1, 0], s2))
        for i, (basis, scale) in enumerate(bases):
            scratch[...] = dot_t(basis, state) * scale
            send[:, part(i)] = scratch[:, block(1 - odd, half)].astype(BF)
            keep[:, part(i)] = scratch[:, block(odd, half)]
        y6[...] = (dot_t(lb[0, 0], state) * s1).astype(BF)

    state1, pair_send, pair_keep, down6 = call(
        one_body,
        [(tall, f32), ((rank, 4 * half), BF), ((rank, 4 * half), f32), (wide, BF)],
        state0,
        proj1,
        proj1_sib,
        lb,
        rb,
        caps,
        tl,
        tr,
        scratch=[pltpu.VMEM((2 * rank, cols), BF), pltpu.VMEM(wide, f32)],
        micros=3,
    )
    pair_in = swap(pair_send, "leaf", 1)
    next_far_sib = swap(after(next_far, state1), "leaf", 1)

    def pair_body(own, sib, keep, gram, late, scratch):
        upper = side(1)
        for i in range(2):
            scratch[...] = (own[:, span(2 * i, 2)].astype(f32) + sib[:, span(2 * i, 2)]).astype(BF)
            keep[:, span(2 * i)] = scratch[:, block(upper, rank)]
            keep[:, span(2 * i + 1)] = scratch[:, block(1 - upper, rank)]
        late[...] = (own[:, span(4, 4)].astype(f32) + sib[:, span(4, 4)]).astype(BF)
        gram[...] = own[:, span(8)].astype(f32) + sib[:, span(8)]

    next_keep, gram_pair, gram5 = call(
        pair_body,
        [((rank, 4 * rank), BF), (square, f32), ((rank, 4 * rank), BF)],
        grams,
        grams_sib,
        scratch=[pltpu.VMEM((rank, 2 * rank), BF)],
    )

    def order_body(a, b, c, d, out):
        here = lax.axis_index("top")
        for i, piece in enumerate((a, b, c, d)):
            for k in range(4):
                out[span(i), span(k)] = piece[:, block(here ^ k, rank)]

    (caps_all,) = call(order_body, [((4 * rank, 4 * rank), BF)], *caps_parts)

    def half_body(keep, pair, nexts, seen, send, keep2):
        keep2[...] = keep[...] + pair[...]
        own = keep2[:, part(0)].astype(BF)
        for i in range(2):
            keep2[:, part(1 + i)] = keep2[:, part(1 + i)] - dot(nexts[:, span(2 * i)], own)
        send[...] = keep2[...].astype(BF)

    cross_send, cross_keep = call(
        half_body,
        [((rank, 4 * half), BF), ((rank, 4 * half), f32)],
        pair_keep,
        pair_in,
        next_keep,
        caps_all,
    )
    cross_in = swap(cross_send, "leaf", 2)
    gram5_far = swap(after(gram5, cross_send), "leaf", 2)

    def late_body(lb, rb, caps, tl, tr, y6, seen, out):
        left1 = lb[0, 0]
        for i, basis in enumerate((lb[1, 0], rb[1, 0])):
            gram = (dot_t(left1, basis) * s1).astype(BF)
            out[:, span(2 * i, 2)] = dot(gram, caps[1, 0]).astype(BF)
        for i, basis in enumerate((tl, tr)):
            out[:, span(4 + i)] = (dot_t(left1, basis[0]) * s1).astype(BF)
        out[:, 6 * rank :] = y6[...]

    (late,) = call(
        late_body, [((rank, 6 * rank + cols), BF)], lb, rb, caps, tl, tr, down6, cross_send
    )

    def column_body(send, keep2, far, nexts, nexts_far, nexts_far_sib, gram, top, halves, total):
        own, other = send[:, part(0)], far[:, part(0)]
        total[...] = nexts_far[...].astype(f32) + nexts_far_sib[...]
        for i in range(2):
            top[:, part(i)] = (
                keep2[:, part(1 + i)]
                + far[:, part(1 + i)]
                - dot(nexts[:, span(2 * i + 1)], other)
                - dot(total[:, span(i)].astype(BF), own)
            ).astype(BF)
        top[:, 2 * half :] = (gram[...] + total[:, span(2)]).astype(BF)
        halves[:, part(0)] = own
        halves[:, part(1)] = other

    top_send, halves_send = call(
        column_body,
        [((rank, 2 * half + rank), BF), (wide, BF)],
        cross_send,
        cross_keep,
        cross_in,
        next_keep,
        next_far,
        next_far_sib,
        gram_pair,
        scratch=[pltpu.VMEM((rank, 3 * rank), f32)],
    )
    top_parts = around_top(top_send)
    halves_in = swap(halves_send, "leaf", 1)
    late_sib = swap(after(late, top_send, halves_in), "leaf", 1)

    def two_body(x1, own, sib, lb, rb, caps, tl, tr, inv, out2, under, both, mine, x2):
        odd, high = side(0), side(1)
        for i in range(2):
            put_columns(mine.at[span(i), :], odd, own[:, part(i)], sib[:, part(i)])
        put_rows(both, high, mine[span(0), :], mine[span(1), :])
        coef = dot(caps[1, 0], both[...]).astype(BF)
        x2[...] = (x1[...] - dot(lb[1, 0], coef)).astype(BF)
        for c in range(blocks):
            column = inv[c * rank :, span(c)]
            out2[span(c), :] = dot_t(column, x2[c * rank :, :])
            for i, basis in enumerate((tl[0], tr[0], rb[1, 0], rb[0, 0])):
                under[span(c), span(i)] = dot_t(column, basis[c * rank :, :]).astype(BF)

    out2, under, stack2 = call(
        two_body,
        [(tall, f32), ((rows, 4 * rank), BF), ((2 * rank, cols), BF)],
        state1,
        halves_send,
        halves_in,
        lb,
        rb,
        caps,
        tl,
        tr,
        inverse,
        scratch=[pltpu.VMEM((2 * rank, cols), BF), pltpu.VMEM(tall, BF)],
    )

    def top_body(
        a, b, c, d, caps, send, keep2, far, gram5, gram5_far, seen, out, up, down, both
    ):
        pieces = (a, b, c, d)
        for i, piece in enumerate(pieces):
            up[span(i), :] = piece[:, part(0)]
        coef = dot(caps[...], up[...]).astype(BF)
        for i, piece in enumerate(pieces):
            down[span(i), :] = (
                piece[:, part(1)] - dot(piece[:, 2 * half :], coef[span(i), :])
            ).astype(BF)
        out[:, part(0)] = coef[:rank, :]
        out[:, part(1)] = dot(caps[:rank, :], down[...]).astype(BF)
        put_rows(both.at[: 2 * rank, :], side(1), send[:, part(0)], far[:, part(0)])
        both[span(2), :] = out[:, part(0)]
        both[span(3), :] = out[:, part(1)]
        out[:, part(2)] = (keep2[:, part(3)] - dot(gram5[...], both[...])).astype(BF)
        out[:, part(3)] = (far[:, part(3)] - dot(gram5_far[...], both[...])).astype(BF)

    (back_send,) = call(
        top_body,
        [((rank, 4 * half), BF)],
        *top_parts,
        caps_all,
        cross_send,
        cross_keep,
        cross_in,
        gram5,
        gram5_far,
        out2,
        scratch=[pltpu.VMEM((4 * rank, half), BF)] * 3,
    )
    back_in = swap(back_send, "leaf", 1)

    def last_body(
        out2, under, stack2, back, back_sib, late, late_sib, caps, out,
        mine, coefs, proj, out_v, sems,
    ):
        odd, high = side(0), side(1)
        for i in range(2):
            put_columns(coefs.at[span(i), :], odd, back[:, part(i)], back_sib[:, part(i)])
            put_columns(mine.at[span(i), :], odd, back[:, part(2 + i)], back_sib[:, part(2 + i)])
        put_rows(proj, high, mine[span(0), :], mine[span(1), :])
        stack5 = proj[...]
        coefs[span(2), :] = dot(caps[1, 0], stack5).astype(BF)

        def down(grams):
            return (
                grams[:, 6 * rank :]
                - dot(grams[:, span(0, 2)], stack2[...])
                - dot(grams[:, span(2, 2)], stack5)
                - dot(grams[:, span(4, 2)], coefs[span(0, 2), :])
            ).astype(BF)

        put_rows(proj, odd, down(late), down(late_sib))
        coefs[span(3), :] = dot(caps[0, 0], proj[...]).astype(BF)
        copies = []
        for c in range(blocks):
            out_v[span(c), :] = out2[span(c), :] - dot(under[span(c), :], coefs[...])
            copy = pltpu.make_async_copy(out_v.at[span(c), :], out.at[0, span(c), :], sems.at[c])
            copy.start()
            copies.append(copy)
        for copy in copies:
            copy.wait()

    (out,) = call(
        last_body,
        [((1, rows, cols), f32)],
        out2,
        under,
        stack2,
        back_send,
        back_in,
        late,
        late_sib,
        caps,
        hbm_out=True,
        scratch=[
            pltpu.VMEM((2 * rank, cols), BF),
            pltpu.VMEM((4 * rank, cols), BF),
            pltpu.VMEM((2 * rank, cols), BF),
            pltpu.VMEM(tall, f32),
            pltpu.SemaphoreType.DMA((blocks,)),
        ],
    )
    return out


def on_device(*args):
    levels = args[2].shape[0]
    sizes = lax.axis_size("leaf"), lax.axis_size("top")
    if levels == 2 and sizes == (4, 4):
        return two_levels(*args)
    return step_by_step(*args)


def solution(mesh):
    rows = P(("parts", "top"), "leaf", None)
    level_rows = P(None, ("parts", "top"), "leaf", None)
    return jax.shard_map(
        on_device,
        mesh=mesh,
        in_specs=(
            rows,
            rows,
            level_rows,
            level_rows,
            level_rows,
            rows,
            rows,
            P(("parts", "top"), None),
        ),
        out_specs=rows,
        check_vma=False,
    )
```

```python
import math

import jax
import jax.numpy as jnp
from jax import lax
from jax.experimental import pallas as pl
from jax.experimental.pallas import tpu as pltpu
from jax.sharding import PartitionSpec as P

BF = jnp.bfloat16
VMEM_LIMIT = 8 * 2**20
FLOPS_PER_MICRO = 1e9


def swap(value, axis, mask):
    pairs = [(source, source ^ mask) for source in range(lax.axis_size(axis))]
    return lax.ppermute(value, axis, pairs)


def dot(a, b):
    return jnp.dot(a, b, preferred_element_type=jnp.float32)


def dot_t(a, b):
    return lax.dot_general(a, b, (((0,), (0,)), ((), ())), preferred_element_type=jnp.float32)


def ordered(upper_side, own, other):
    return jnp.where(
        upper_side, jnp.concatenate([other, own], 0), jnp.concatenate([own, other], 0)
    )


def level_step(current, project_basis, update_basis, caps_rows, level_num):
    leaf_rows = current.shape[0]
    shift_bits = level_num - 1
    partial_value = dot_t(project_basis, current.astype(BF)) * (
        1.0 / math.sqrt(leaf_rows * 2**shift_bits)
    )
    for bit_index in range(shift_bits):
        partial_value = partial_value + swap(partial_value, "leaf", 2**bit_index)
    own = partial_value.astype(BF)
    other = swap(own, "leaf", 2**shift_bits)
    upper_side = (lax.axis_index("leaf") >> shift_bits) & 1 == 1
    stacked = ordered(upper_side, own, other)
    weights = dot(caps_rows, stacked).astype(BF)
    return current - dot(update_basis, weights)


def top_step(current, project_basis, update_basis, caps_rows):
    leaf_count = lax.axis_size("leaf")
    partial_value = dot_t(project_basis, current.astype(BF)) * (
        1.0 / math.sqrt(leaf_count * current.shape[0])
    )
    column_total = lax.psum(partial_value, "leaf")
    stacked = lax.all_gather(column_total.astype(BF), "top", axis=0, tiled=True)
    weights = dot(caps_rows, stacked).astype(BF)
    return current - dot(update_basis, weights)


def step_by_step(
    right_side, leaf_inverse, left_basis, right_basis, level_caps, top_left, top_right, top_caps
):
    levels = left_basis.shape[0]
    lefts = [left_basis[k, 0] for k in range(levels)]
    rights = [right_basis[k, 0] for k in range(levels)]
    current = dot(leaf_inverse[0], right_side[0].astype(BF))
    for k in range(levels):
        current = level_step(current, rights[k], lefts[k], level_caps[k, 0], k + 1)
    current = top_step(current, top_right[0], top_left[0], top_caps)
    current = top_step(current, top_left[0], top_right[0], top_caps)
    for k in reversed(range(levels)):
        current = level_step(current, lefts[k], rights[k], level_caps[k, 0], k + 1)
    return dot_t(leaf_inverse[0], current.astype(BF))[None]


def in_hbm(value):
    return pltpu.with_memory_space_constraint(value, pltpu.HBM)


def in_vmem(value):
    return pltpu.with_memory_space_constraint(value, pltpu.VMEM)


def call(body, outs, *args, scratch=(), hbm=(), hbm_out=False, micros=1):
    vmem = pl.BlockSpec(memory_space=pltpu.VMEM)
    anywhere = pl.BlockSpec(memory_space=pl.ANY)
    return pl.pallas_call(
        body,
        out_shape=[
            jax.ShapeDtypeStruct(shape, dtype) if hbm_out else pltpu.VMEM(shape, dtype)
            for shape, dtype in outs
        ],
        in_specs=[anywhere if i in hbm else vmem for i in range(len(args))],
        out_specs=[anywhere if hbm_out else vmem] * len(outs),
        scratch_shapes=list(scratch),
        compiler_params=pltpu.CompilerParams(vmem_limit_bytes=VMEM_LIMIT),
        cost_estimate=pl.CostEstimate(
            flops=int(micros * FLOPS_PER_MICRO), bytes_accessed=0, transcendentals=0
        ),
    )(*[in_hbm(a) if i in hbm else in_vmem(a) for i, a in enumerate(args)])


def after(value, *others):
    return lax.optimization_barrier((value, *others))[0]


def tree_side(bit):
    return (lax.axis_index("leaf") >> bit) & 1


def column_side():
    leaf = lax.axis_index("leaf")
    return (leaf ^ (leaf >> 1)) & 1


def block(index, width):
    return pl.ds(pl.multiple_of(index * width, width), width)


def put_rows(scratch, upper, own, other):
    rows = own.shape[0]
    scratch[block(upper, rows), :] = own
    scratch[block(1 - upper, rows), :] = other


def put_columns(out, upper, own, other):
    width = own.shape[1]
    out[:, block(upper, width)] = own
    out[:, block(1 - upper, width)] = other


def two_levels(
    right_side, leaf_inverse, left_basis, right_basis, level_caps, top_left, top_right, top_caps
):
    rows, cols = right_side.shape[1:]
    rank = top_left.shape[2]
    half = cols // 2
    f32 = jnp.float32
    s1 = 1.0 / math.sqrt(rows)
    s2 = 1.0 / math.sqrt(rows * 2)
    st = 1.0 / math.sqrt(rows * 4)
    blocks = rows // rank
    square, wide, tall = (rank, rank), (rank, cols), (rows, cols)

    def span(i, n=1):
        return slice(i * rank, (i + n) * rank)

    def part(i, n=1):
        return slice(i * half, (i + n) * half)

    caps_far = swap(top_caps, "top", 2)

    def start_body(
        rhs_hbm, inv_hbm, lb_hbm, rb_hbm, caps_hbm, tl_hbm, tr_hbm,
        x_ref, send, keep, inv_ref, lb, rb, caps, tl, tr, rhs_v, nexts, sems,
    ):
        def load(source, target, *at):
            copy = pltpu.make_async_copy(source, target, sems.at[at])
            copy.start()
            return copy

        first = [
            load(lb_hbm.at[0], lb.at[0], 2, 0),
            load(rb_hbm.at[1], rb.at[1], 2, 1),
            load(caps_hbm, caps, 2, 2),
        ]
        copies = []
        for i in range(blocks):
            copies.append(load(rhs_hbm.at[0, span(i), :], rhs_v.at[span(i), :], 0, i))
            copies.append(
                load(
                    inv_hbm.at[0, span(i), span(0, i + 1)],
                    inv_ref.at[span(i), span(0, i + 1)],
                    1,
                    i,
                )
            )
        basis1 = load(rb_hbm.at[0], rb.at[0], 2, 3)
        rest = [
            load(lb_hbm.at[1], lb.at[1], 2, 4),
            load(tl_hbm, tl, 2, 5),
            load(tr_hbm, tr, 2, 6),
        ]
        odd = tree_side(0)
        for copy in first:
            copy.wait()
        gram = (dot_t(rb[1, 0], lb[0, 0]) * s2).astype(BF)
        nexts[...] = dot(gram, caps[0, 0]).astype(BF)
        send[:, 2 * cols :] = nexts[:, block(1 - odd, rank)]
        for i in range(blocks):
            copies[2 * i].wait()
            copies[2 * i + 1].wait()
            x_ref[span(i), :] = dot(
                inv_ref[span(i), span(0, i + 1)], rhs_v[span(0, i + 1), :].astype(BF)
            )
        basis1.wait()
        state = x_ref[...].astype(BF)
        send[:, :cols] = (dot_t(rb[0, 0], state) * s1).astype(BF)
        keep[...] = dot_t(rb[1, 0], state) * s2 - dot(nexts[:, block(odd, rank)], send[:, :cols])
        send[:, cols : 2 * cols] = keep[...].astype(BF)
        for copy in rest:
            copy.wait()

    state0, pair_send, pair_keep, inverse, lb, rb, caps, tl, tr = call(
        start_body,
        [(tall, f32), ((rank, 2 * cols + rank), BF), (wide, f32), ((rows, rows), BF)]
        + [(a.shape, a.dtype) for a in (left_basis, right_basis, level_caps, top_left, top_right)],
        right_side,
        leaf_inverse,
        left_basis,
        right_basis,
        level_caps,
        top_left,
        top_right,
        hbm=range(7),
        scratch=[
            pltpu.VMEM(tall, f32),
            pltpu.VMEM((rank, 2 * rank), BF),
            pltpu.SemaphoreType.DMA((3, max(blocks, 7))),
        ],
    )
    pair_in = swap(pair_send, "leaf", 1)
    caps_near = swap(after(top_caps, pair_send), "top", 1)
    caps_far_near = swap(after(caps_far, pair_send), "top", 1)

    def grams_body(lb, rb, caps, tl, tr, seen, out, late):
        out[:, span(0)] = (dot_t(tl[0], tl[0]) * st).astype(BF)
        for i, basis in enumerate((tl[0], tr[0])):
            out[:, span(1 + i)] = (dot_t(lb[1, 0], basis) * s2).astype(BF)
        for i, basis in enumerate((tl[0], tr[0], rb[1, 0])):
            late[:, span(i)] = (dot_t(lb[0, 0], basis) * s1).astype(BF)
        late[:, span(3, 2)] = caps[1, 0]

    grams, late = call(
        grams_body,
        [((rank, 3 * rank), BF), ((rank, 5 * rank), BF)],
        lb,
        rb,
        caps,
        tl,
        tr,
        caps_near,
        micros=10,
    )
    grams_sib = swap(grams, "leaf", 1)

    def half_body(keep, own, sib, out):
        out[...] = (
            keep[...]
            + sib[:, cols : 2 * cols]
            - dot(own[:, 2 * cols :], sib[:, :cols])
            - dot(sib[:, 2 * cols :], own[:, :cols])
        ).astype(BF)

    (half2,) = call(half_body, [(wide, BF)], pair_keep, pair_send, pair_in, micros=3)
    half2_far = swap(half2, "leaf", 3)

    def order_body(a, b, c, d, seen, out):
        here = lax.axis_index("top")
        for i, piece in enumerate((a, b, c, d)):
            for k in range(4):
                out[span(i), span(k)] = piece[:, block(here ^ k, rank)]

    (caps_all,) = call(
        order_body,
        [((4 * rank, 4 * rank), BF)],
        top_caps,
        caps_near,
        caps_far,
        caps_far_near,
        half2,
    )

    def sum_body(own, sib, seen, out):
        out[...] = (own[...].astype(f32) + sib[...]).astype(BF)

    (gram_pair,) = call(sum_body, [((rank, 3 * rank), BF)], grams, grams_sib, half2)
    gram_far = swap(gram_pair, "leaf", 3)

    def one_body(x0, own, sib, lb, caps, seen, x1, stack):
        put_rows(stack, tree_side(0), own[:, :cols], sib[:, :cols])
        coef = dot(caps[0, 0], stack[...]).astype(BF)
        x1[...] = x0[...] - dot(lb[0, 0], coef)

    (state1,) = call(
        one_body,
        [(tall, f32)],
        state0,
        pair_send,
        pair_in,
        lb,
        caps,
        half2,
        scratch=[pltpu.VMEM((2 * rank, cols), BF)],
    )

    def two_body(x1, own, far, lb, caps, tl, tr, seen, x2, send, keep, stack, scratch):
        side = column_side()
        put_rows(stack, tree_side(1), own[...], far[...])
        coef = dot(caps[1, 0], stack[...]).astype(BF)
        x2[...] = (x1[...] - dot(lb[1, 0], coef)).astype(BF)
        for i, basis in enumerate((tr[0], tl[0])):
            scratch[...] = dot_t(basis, x2[...]) * st
            send[:, part(i)] = scratch[:, block(1 - side, half)].astype(BF)
            keep[:, part(i)] = scratch[:, block(side, half)]

    state2, top_pair_send, top_keep = call(
        two_body,
        [(tall, BF), (wide, BF), (wide, f32)],
        state1,
        half2,
        half2_far,
        lb,
        caps,
        tl,
        tr,
        caps_all,
        scratch=[pltpu.VMEM((2 * rank, cols), BF), pltpu.VMEM(wide, f32)],
    )
    top_pair_in = swap(top_pair_send, "leaf", 1)

    def down_body(lb, x2, z5, z):
        z5[...] = dot_t(lb[1, 0], x2[...]) * s2
        z[:, :cols] = z5[...].astype(BF)
        z[:, cols:] = (dot_t(lb[0, 0], x2[...]) * s1).astype(BF)

    down5, down_send = call(down_body, [(wide, f32), ((rank, 2 * cols), BF)], lb, state2)
    down_in = swap(down_send, "leaf", 1)

    def add_body(own, other, out, out_b):
        out[...] = own[...] + other[:, :cols]
        out_b[...] = out[...].astype(BF)

    top_half, top_half_send = call(add_body, [(wide, f32), (wide, BF)], top_keep, top_pair_in)
    top_half_far = swap(top_half_send, "leaf", 3)
    down5, down5_send = call(add_body, [(wide, f32), (wide, BF)], down5, down_in)
    down5_far = swap(down5_send, "leaf", 3)

    def column_body(own, far, gram, gram_far, out):
        out[:, : 2 * half] = (own[...] + far[...]).astype(BF)
        out[:, 2 * half :] = (gram[:, span(0)].astype(f32) + gram_far[:, span(0)]).astype(BF)

    (top_send,) = call(
        column_body,
        [((rank, 2 * half + rank), BF)],
        top_half,
        top_half_far,
        gram_pair,
        gram_far,
    )
    top_far = swap(top_send, "top", 2)
    top_parts = top_send, swap(top_send, "top", 1), top_far, swap(top_far, "top", 1)
    late_sib = swap(after(late, top_send), "leaf", 1)

    def under_body(x2, rb, tl, tr, inv, seen, out2, under):
        for c in range(blocks):
            column = inv[c * rank :, span(c)]
            out2[span(c), :] = dot_t(column, x2[c * rank :, :])
            for i, basis in enumerate((tl[0], tr[0], rb[1, 0], rb[0, 0])):
                under[span(c), span(i)] = dot_t(column, basis[c * rank :, :]).astype(BF)

    out2, under = call(
        under_body,
        [(tall, f32), ((rows, 4 * rank), BF)],
        state2,
        rb,
        tl,
        tr,
        inverse,
        top_send,
    )

    def top_body(a, b, c, d, caps, seen, out, up, down):
        pieces = (a, b, c, d)
        for i, piece in enumerate(pieces):
            up[span(i), :] = piece[:, part(0)]
        coef = dot(caps[...], up[...]).astype(BF)
        for i, piece in enumerate(pieces):
            down[span(i), :] = (
                piece[:, part(1)] - dot(piece[:, 2 * half :], coef[span(i), :])
            ).astype(BF)
        out[:, part(0)] = coef[:rank, :]
        out[:, part(1)] = dot(caps[:rank, :], down[...]).astype(BF)

    (back_send,) = call(
        top_body,
        [(wide, BF)],
        *top_parts,
        caps_all,
        out2,
        scratch=[pltpu.VMEM((4 * rank, half), BF)] * 2,
    )
    back_in = swap(back_send, "leaf", 1)

    def last_body(
        out2, under, back, back_sib, down5, down5_far, gram, gram_far, late, late_sib,
        z, z_sib, caps, out, coefs, stack, out_v, sems,
    ):
        side = column_side()
        for i in range(2):
            put_columns(coefs.at[span(i), :], side, back[:, part(i)], back_sib[:, part(i)])
        both = coefs[span(0, 2), :]
        put_rows(
            stack,
            tree_side(1),
            (down5[...] - dot(gram[:, span(1, 2)], both)).astype(BF),
            (down5_far[...] - dot(gram_far[:, span(1, 2)], both)).astype(BF),
        )
        coef5 = dot(caps[1, 0], stack[...]).astype(BF)
        coef5_sib = dot(late_sib[:, span(3, 2)], stack[...]).astype(BF)
        coefs[span(2), :] = coef5

        def proj(zs, grams, coef):
            return (
                zs[:, cols:] - dot(grams[:, span(0, 2)], both) - dot(grams[:, span(2)], coef)
            ).astype(BF)

        put_rows(stack, tree_side(0), proj(z, late, coef5), proj(z_sib, late_sib, coef5_sib))
        coefs[span(3), :] = dot(caps[0, 0], stack[...]).astype(BF)
        copies = []
        for c in range(blocks):
            out_v[span(c), :] = out2[span(c), :] - dot(under[span(c), :], coefs[...])
            copy = pltpu.make_async_copy(out_v.at[span(c), :], out.at[0, span(c), :], sems.at[c])
            copy.start()
            copies.append(copy)
        for copy in copies:
            copy.wait()

    (out,) = call(
        last_body,
        [((1, rows, cols), f32)],
        out2,
        under,
        back_send,
        back_in,
        down5,
        down5_far,
        gram_pair,
        gram_far,
        late,
        late_sib,
        down_send,
        down_in,
        caps,
        hbm_out=True,
        scratch=[
            pltpu.VMEM((4 * rank, cols), BF),
            pltpu.VMEM((2 * rank, cols), BF),
            pltpu.VMEM(tall, f32),
            pltpu.SemaphoreType.DMA((blocks,)),
        ],
    )
    return out


def on_device(*args):
    levels = args[2].shape[0]
    sizes = lax.axis_size("leaf"), lax.axis_size("top")
    if levels == 2 and sizes == (4, 4):
        return two_levels(*args)
    return step_by_step(*args)


def solution(mesh):
    rows = P(("parts", "top"), "leaf", None)
    level_rows = P(None, ("parts", "top"), "leaf", None)
    return jax.shard_map(
        on_device,
        mesh=mesh,
        in_specs=(
            rows,
            rows,
            level_rows,
            level_rows,
            level_rows,
            rows,
            rows,
            P(("parts", "top"), None),
        ),
        out_specs=rows,
        check_vma=False,
    )
```

```python
import math

import jax
import jax.numpy as jnp
from jax import lax
from jax.experimental import pallas as pl
from jax.experimental.pallas import tpu as pltpu
from jax.sharding import PartitionSpec as P

BF = jnp.bfloat16
VMEM_LIMIT = 8 * 2**20
FLOPS_PER_MICRO = 1e9


def swap(value, axis, mask):
    pairs = [(source, source ^ mask) for source in range(lax.axis_size(axis))]
    return lax.ppermute(value, axis, pairs)


def dot(a, b):
    return jnp.dot(a, b, preferred_element_type=jnp.float32)


def dot_t(a, b):
    return lax.dot_general(a, b, (((0,), (0,)), ((), ())), preferred_element_type=jnp.float32)


def ordered(upper_side, own, other):
    return jnp.where(
        upper_side, jnp.concatenate([other, own], 0), jnp.concatenate([own, other], 0)
    )


def level_step(current, project_basis, update_basis, caps_rows, level_num):
    leaf_rows = current.shape[0]
    shift_bits = level_num - 1
    partial_value = dot_t(project_basis, current.astype(BF)) * (
        1.0 / math.sqrt(leaf_rows * 2**shift_bits)
    )
    for bit_index in range(shift_bits):
        partial_value = partial_value + swap(partial_value, "leaf", 2**bit_index)
    own = partial_value.astype(BF)
    other = swap(own, "leaf", 2**shift_bits)
    upper_side = (lax.axis_index("leaf") >> shift_bits) & 1 == 1
    stacked = ordered(upper_side, own, other)
    weights = dot(caps_rows, stacked).astype(BF)
    return current - dot(update_basis, weights)


def top_step(current, project_basis, update_basis, caps_rows):
    leaf_count = lax.axis_size("leaf")
    partial_value = dot_t(project_basis, current.astype(BF)) * (
        1.0 / math.sqrt(leaf_count * current.shape[0])
    )
    column_total = lax.psum(partial_value, "leaf")
    stacked = lax.all_gather(column_total.astype(BF), "top", axis=0, tiled=True)
    weights = dot(caps_rows, stacked).astype(BF)
    return current - dot(update_basis, weights)


def step_by_step(
    right_side, leaf_inverse, left_basis, right_basis, level_caps, top_left, top_right, top_caps
):
    levels = left_basis.shape[0]
    lefts = [left_basis[k, 0] for k in range(levels)]
    rights = [right_basis[k, 0] for k in range(levels)]
    current = dot(leaf_inverse[0], right_side[0].astype(BF))
    for k in range(levels):
        current = level_step(current, rights[k], lefts[k], level_caps[k, 0], k + 1)
    current = top_step(current, top_right[0], top_left[0], top_caps)
    current = top_step(current, top_left[0], top_right[0], top_caps)
    for k in reversed(range(levels)):
        current = level_step(current, lefts[k], rights[k], level_caps[k, 0], k + 1)
    return dot_t(leaf_inverse[0], current.astype(BF))[None]


def in_hbm(value):
    return pltpu.with_memory_space_constraint(value, pltpu.HBM)


def in_vmem(value):
    return pltpu.with_memory_space_constraint(value, pltpu.VMEM)


def call(body, outs, *args, scratch=(), hbm=(), hbm_out=False, micros=1):
    vmem = pl.BlockSpec(memory_space=pltpu.VMEM)
    anywhere = pl.BlockSpec(memory_space=pl.ANY)
    return pl.pallas_call(
        body,
        out_shape=[
            jax.ShapeDtypeStruct(shape, dtype) if hbm_out else pltpu.VMEM(shape, dtype)
            for shape, dtype in outs
        ],
        in_specs=[anywhere if i in hbm else vmem for i in range(len(args))],
        out_specs=[anywhere if hbm_out else vmem] * len(outs),
        scratch_shapes=list(scratch),
        compiler_params=pltpu.CompilerParams(vmem_limit_bytes=VMEM_LIMIT),
        cost_estimate=pl.CostEstimate(
            flops=int(micros * FLOPS_PER_MICRO), bytes_accessed=0, transcendentals=0
        ),
    )(*[in_hbm(a) if i in hbm else in_vmem(a) for i, a in enumerate(args)])


def after(value, *others):
    return lax.optimization_barrier((value, *others))[0]


def tree_side(bit):
    return (lax.axis_index("leaf") >> bit) & 1


def column_side():
    leaf = lax.axis_index("leaf")
    return (leaf ^ (leaf >> 1)) & 1


def block(index, width):
    return pl.ds(pl.multiple_of(index * width, width), width)


def put_rows(scratch, upper, own, other):
    rows = own.shape[0]
    scratch[block(upper, rows), :] = own
    scratch[block(1 - upper, rows), :] = other


def put_columns(out, upper, own, other):
    width = own.shape[1]
    out[:, block(upper, width)] = own
    out[:, block(1 - upper, width)] = other


def two_levels(
    right_side, leaf_inverse, left_basis, right_basis, level_caps, top_left, top_right, top_caps
):
    rows, cols = right_side.shape[1:]
    rank = top_left.shape[2]
    half = cols // 2
    f32 = jnp.float32
    s1 = 1.0 / math.sqrt(rows)
    s2 = 1.0 / math.sqrt(rows * 2)
    st = 1.0 / math.sqrt(rows * 4)
    blocks = rows // rank
    square, wide, tall = (rank, rank), (rank, cols), (rows, cols)

    def span(i, n=1):
        return slice(i * rank, (i + n) * rank)

    def part(i, n=1):
        return slice(i * half, (i + n) * half)

    def start_body(
        rhs_hbm, inv_hbm, lb_hbm, rb_hbm, caps_hbm, tl_hbm, tr_hbm,
        x_ref, send, keep, inv_ref, lb, rb, caps, tl, tr, rhs_v, nexts, sems,
    ):
        def load(source, target, *at):
            copy = pltpu.make_async_copy(source, target, sems.at[at])
            copy.start()
            return copy

        first = [
            load(lb_hbm.at[0], lb.at[0], 2, 0),
            load(rb_hbm.at[1], rb.at[1], 2, 1),
            load(caps_hbm, caps, 2, 2),
        ]
        copies = []
        for i in range(blocks):
            copies.append(load(rhs_hbm.at[0, span(i), :], rhs_v.at[span(i), :], 0, i))
            copies.append(
                load(
                    inv_hbm.at[0, span(i), span(0, i + 1)],
                    inv_ref.at[span(i), span(0, i + 1)],
                    1,
                    i,
                )
            )
        basis1 = load(rb_hbm.at[0], rb.at[0], 2, 3)
        rest = [
            load(lb_hbm.at[1], lb.at[1], 2, 4),
            load(tl_hbm, tl, 2, 5),
            load(tr_hbm, tr, 2, 6),
        ]
        odd = tree_side(0)
        for copy in first:
            copy.wait()
        gram = (dot_t(rb[1, 0], lb[0, 0]) * s2).astype(BF)
        nexts[...] = dot(gram, caps[0, 0]).astype(BF)
        send[:, 2 * cols :] = nexts[:, block(1 - odd, rank)]
        for i in range(blocks):
            copies[2 * i].wait()
            copies[2 * i + 1].wait()
            x_ref[span(i), :] = dot(
                inv_ref[span(i), span(0, i + 1)], rhs_v[span(0, i + 1), :].astype(BF)
            )
        basis1.wait()
        state = x_ref[...].astype(BF)
        send[:, :cols] = (dot_t(rb[0, 0], state) * s1).astype(BF)
        keep[...] = dot_t(rb[1, 0], state) * s2 - dot(nexts[:, block(odd, rank)], send[:, :cols])
        send[:, cols : 2 * cols] = keep[...].astype(BF)
        for copy in rest:
            copy.wait()

    state0, pair_send, pair_keep, inverse, lb, rb, caps, tl, tr = call(
        start_body,
        [(tall, f32), ((rank, 2 * cols + rank), BF), (wide, f32), ((rows, rows), BF)]
        + [(a.shape, a.dtype) for a in (left_basis, right_basis, level_caps, top_left, top_right)],
        right_side,
        leaf_inverse,
        left_basis,
        right_basis,
        level_caps,
        top_left,
        top_right,
        hbm=range(7),
        scratch=[
            pltpu.VMEM(tall, f32),
            pltpu.VMEM((rank, 2 * rank), BF),
            pltpu.SemaphoreType.DMA((3, max(blocks, 7))),
        ],
    )
    pair_in = swap(pair_send, "leaf", 1)
    caps_here = after(top_caps, pair_send)
    caps_near = swap(caps_here, "top", 1)
    caps_far = swap(caps_here, "top", 2)
    caps_far_near = swap(caps_far, "top", 1)

    def grams_body(lb, rb, caps, tl, tr, seen, out, late):
        out[:, span(0)] = (dot_t(tl[0], tl[0]) * st).astype(BF)
        for i, basis in enumerate((tl[0], tr[0])):
            out[:, span(1 + i)] = (dot_t(lb[1, 0], basis) * s2).astype(BF)
        for i, basis in enumerate((tl[0], tr[0], rb[1, 0])):
            late[:, span(i)] = (dot_t(lb[0, 0], basis) * s1).astype(BF)
        late[:, span(3, 2)] = caps[1, 0]

    grams, late = call(
        grams_body,
        [((rank, 3 * rank), BF), ((rank, 5 * rank), BF)],
        lb,
        rb,
        caps,
        tl,
        tr,
        caps_near,
        micros=10,
    )
    grams_sib = swap(grams, "leaf", 1)

    def half_body(keep, own, sib, out):
        out[...] = (
            keep[...]
            + sib[:, cols : 2 * cols]
            - dot(own[:, 2 * cols :], sib[:, :cols])
            - dot(sib[:, 2 * cols :], own[:, :cols])
        ).astype(BF)

    (half2,) = call(half_body, [(wide, BF)], pair_keep, pair_send, pair_in, micros=3)
    half2_far = swap(half2, "leaf", 3)
    late_sib = swap(after(late, half2), "leaf", 1)

    def order_body(a, b, c, d, seen, out):
        here = lax.axis_index("top")
        for i, piece in enumerate((a, b, c, d)):
            for k in range(4):
                out[span(i), span(k)] = piece[:, block(here ^ k, rank)]

    (caps_all,) = call(
        order_body,
        [((4 * rank, 4 * rank), BF)],
        top_caps,
        caps_near,
        caps_far,
        caps_far_near,
        half2,
    )

    def sum_body(own, sib, seen, out):
        out[...] = (own[...].astype(f32) + sib[...]).astype(BF)

    (gram_pair,) = call(sum_body, [((rank, 3 * rank), BF)], grams, grams_sib, half2)
    gram_far = swap(gram_pair, "leaf", 3)

    def one_body(x0, own, sib, lb, caps, seen, x1, stack):
        put_rows(stack, tree_side(0), own[:, :cols], sib[:, :cols])
        coef = dot(caps[0, 0], stack[...]).astype(BF)
        x1[...] = x0[...] - dot(lb[0, 0], coef)

    (state1,) = call(
        one_body,
        [(tall, f32)],
        state0,
        pair_send,
        pair_in,
        lb,
        caps,
        half2,
        scratch=[pltpu.VMEM((2 * rank, cols), BF)],
    )

    def two_body(x1, own, far, lb, caps, tl, tr, seen, x2, send, keep, stack, scratch):
        side = column_side()
        put_rows(stack, tree_side(1), own[...], far[...])
        coef = dot(caps[1, 0], stack[...]).astype(BF)
        x2[...] = (x1[...] - dot(lb[1, 0], coef)).astype(BF)
        for i, basis in enumerate((tr[0], tl[0])):
            scratch[...] = dot_t(basis, x2[...]) * st
            send[:, part(i)] = scratch[:, block(1 - side, half)].astype(BF)
            keep[:, part(i)] = scratch[:, block(side, half)]

    state2, top_pair_send, top_keep = call(
        two_body,
        [(tall, BF), (wide, BF), (wide, f32)],
        state1,
        half2,
        half2_far,
        lb,
        caps,
        tl,
        tr,
        caps_all,
        scratch=[pltpu.VMEM((2 * rank, cols), BF), pltpu.VMEM(wide, f32)],
    )
    top_pair_in = swap(top_pair_send, "leaf", 1)

    def down_body(lb, x2, z5, z):
        z5[...] = dot_t(lb[1, 0], x2[...]) * s2
        z[:, :cols] = z5[...].astype(BF)
        z[:, cols:] = (dot_t(lb[0, 0], x2[...]) * s1).astype(BF)

    down5, down_send = call(down_body, [(wide, f32), ((rank, 2 * cols), BF)], lb, state2)
    down_in = swap(down_send, "leaf", 1)

    def add_body(own, other, seen, out, out_b):
        out[...] = own[...] + other[:, :cols]
        out_b[...] = out[...].astype(BF)

    top_half, top_half_send = call(add_body, [(wide, f32), (wide, BF)], top_keep, top_pair_in, late_sib)
    top_half_far = swap(top_half_send, "leaf", 3)
    down5, down5_send = call(
        add_body, [(wide, f32), (wide, BF)], down5, down_in, gram_pair
    )
    down5_far = swap(down5_send, "leaf", 3)

    def column_body(own, far, gram, gram_far, out):
        out[:, : 2 * half] = (own[...] + far[...]).astype(BF)
        out[:, 2 * half :] = (gram[:, span(0)].astype(f32) + gram_far[:, span(0)]).astype(BF)

    (top_send,) = call(
        column_body,
        [((rank, 2 * half + rank), BF)],
        top_half,
        top_half_far,
        gram_pair,
        gram_far,
    )
    top_far = swap(top_send, "top", 2)
    top_near = swap(after(top_send, down5_send), "top", 1)
    top_parts = top_send, top_near, top_far, swap(top_far, "top", 1)

    def under_body(x2, rb, tl, tr, inv, seen, out2, under):
        for c in range(blocks):
            column = inv[c * rank :, span(c)]
            out2[span(c), :] = dot_t(column, x2[c * rank :, :])
            for i, basis in enumerate((tl[0], tr[0], rb[1, 0], rb[0, 0])):
                under[span(c), span(i)] = dot_t(column, basis[c * rank :, :]).astype(BF)

    out2, under = call(
        under_body,
        [(tall, f32), ((rows, 4 * rank), BF)],
        state2,
        rb,
        tl,
        tr,
        inverse,
        down5_far,
    )

    def top_body(a, b, c, d, caps, out, up, down):
        pieces = (a, b, c, d)
        for i, piece in enumerate(pieces):
            up[span(i), :] = piece[:, part(0)]
        coef = dot(caps[...], up[...]).astype(BF)
        for i, piece in enumerate(pieces):
            down[span(i), :] = (
                piece[:, part(1)] - dot(piece[:, 2 * half :], coef[span(i), :])
            ).astype(BF)
        out[:, part(0)] = coef[:rank, :]
        out[:, part(1)] = dot(caps[:rank, :], down[...]).astype(BF)

    (back_send,) = call(
        top_body,
        [(wide, BF)],
        *top_parts,
        caps_all,
        scratch=[pltpu.VMEM((4 * rank, half), BF)] * 2,
    )
    back_in = swap(back_send, "leaf", 1)

    def last_body(
        out2, under, back, back_sib, down5, down5_far, gram, gram_far, late, late_sib,
        z, z_sib, caps, out, coefs, stack, out_v, sems,
    ):
        side = column_side()
        for i in range(2):
            put_columns(coefs.at[span(i), :], side, back[:, part(i)], back_sib[:, part(i)])
        both = coefs[span(0, 2), :]
        put_rows(
            stack,
            tree_side(1),
            (down5[...] - dot(gram[:, span(1, 2)], both)).astype(BF),
            (down5_far[...] - dot(gram_far[:, span(1, 2)], both)).astype(BF),
        )
        coef5 = dot(caps[1, 0], stack[...]).astype(BF)
        coef5_sib = dot(late_sib[:, span(3, 2)], stack[...]).astype(BF)
        coefs[span(2), :] = coef5

        def proj(zs, grams, coef):
            return (
                zs[:, cols:] - dot(grams[:, span(0, 2)], both) - dot(grams[:, span(2)], coef)
            ).astype(BF)

        put_rows(stack, tree_side(0), proj(z, late, coef5), proj(z_sib, late_sib, coef5_sib))
        coefs[span(3), :] = dot(caps[0, 0], stack[...]).astype(BF)
        copies = []
        for c in range(blocks):
            out_v[span(c), :] = out2[span(c), :] - dot(under[span(c), :], coefs[...])
            copy = pltpu.make_async_copy(out_v.at[span(c), :], out.at[0, span(c), :], sems.at[c])
            copy.start()
            copies.append(copy)
        for copy in copies:
            copy.wait()

    (out,) = call(
        last_body,
        [((1, rows, cols), f32)],
        out2,
        under,
        back_send,
        back_in,
        down5,
        down5_far,
        gram_pair,
        gram_far,
        late,
        late_sib,
        down_send,
        down_in,
        caps,
        hbm_out=True,
        scratch=[
            pltpu.VMEM((4 * rank, cols), BF),
            pltpu.VMEM((2 * rank, cols), BF),
            pltpu.VMEM(tall, f32),
            pltpu.SemaphoreType.DMA((blocks,)),
        ],
    )
    return out


def on_device(*args):
    levels = args[2].shape[0]
    sizes = lax.axis_size("leaf"), lax.axis_size("top")
    if levels == 2 and sizes == (4, 4):
        return two_levels(*args)
    return step_by_step(*args)


def solution(mesh):
    rows = P(("parts", "top"), "leaf", None)
    level_rows = P(None, ("parts", "top"), "leaf", None)
    return jax.shard_map(
        on_device,
        mesh=mesh,
        in_specs=(
            rows,
            rows,
            level_rows,
            level_rows,
            level_rows,
            rows,
            rows,
            P(("parts", "top"), None),
        ),
        out_specs=rows,
        check_vma=False,
    )
```

```python
import math

import jax
import jax.numpy as jnp
from jax import lax
from jax.experimental import pallas as pl
from jax.experimental.pallas import tpu as pltpu
from jax.sharding import PartitionSpec as P

BF = jnp.bfloat16
VMEM_LIMIT = 8 * 2**20
FLOPS_PER_MICRO = 1e9


def swap(value, axis, mask):
    pairs = [(source, source ^ mask) for source in range(lax.axis_size(axis))]
    return lax.ppermute(value, axis, pairs)


def dot(a, b):
    return jnp.dot(a, b, preferred_element_type=jnp.float32)


def dot_t(a, b):
    return lax.dot_general(a, b, (((0,), (0,)), ((), ())), preferred_element_type=jnp.float32)


def ordered(upper_side, own, other):
    return jnp.where(
        upper_side, jnp.concatenate([other, own], 0), jnp.concatenate([own, other], 0)
    )


def level_step(current, project_basis, update_basis, caps_rows, level_num):
    leaf_rows = current.shape[0]
    shift_bits = level_num - 1
    partial_value = dot_t(project_basis, current.astype(BF)) * (
        1.0 / math.sqrt(leaf_rows * 2**shift_bits)
    )
    for bit_index in range(shift_bits):
        partial_value = partial_value + swap(partial_value, "leaf", 2**bit_index)
    own = partial_value.astype(BF)
    other = swap(own, "leaf", 2**shift_bits)
    upper_side = (lax.axis_index("leaf") >> shift_bits) & 1 == 1
    stacked = ordered(upper_side, own, other)
    weights = dot(caps_rows, stacked).astype(BF)
    return current - dot(update_basis, weights)


def top_step(current, project_basis, update_basis, caps_rows):
    leaf_count = lax.axis_size("leaf")
    partial_value = dot_t(project_basis, current.astype(BF)) * (
        1.0 / math.sqrt(leaf_count * current.shape[0])
    )
    column_total = lax.psum(partial_value, "leaf")
    stacked = lax.all_gather(column_total.astype(BF), "top", axis=0, tiled=True)
    weights = dot(caps_rows, stacked).astype(BF)
    return current - dot(update_basis, weights)


def step_by_step(
    right_side, leaf_inverse, left_basis, right_basis, level_caps, top_left, top_right, top_caps
):
    levels = left_basis.shape[0]
    lefts = [left_basis[k, 0] for k in range(levels)]
    rights = [right_basis[k, 0] for k in range(levels)]
    current = dot(leaf_inverse[0], right_side[0].astype(BF))
    for k in range(levels):
        current = level_step(current, rights[k], lefts[k], level_caps[k, 0], k + 1)
    current = top_step(current, top_right[0], top_left[0], top_caps)
    current = top_step(current, top_left[0], top_right[0], top_caps)
    for k in reversed(range(levels)):
        current = level_step(current, lefts[k], rights[k], level_caps[k, 0], k + 1)
    return dot_t(leaf_inverse[0], current.astype(BF))[None]


def in_hbm(value):
    return pltpu.with_memory_space_constraint(value, pltpu.HBM)


def in_vmem(value):
    return pltpu.with_memory_space_constraint(value, pltpu.VMEM)


def call(body, outs, *args, scratch=(), hbm=(), hbm_out=False, micros=1):
    vmem = pl.BlockSpec(memory_space=pltpu.VMEM)
    anywhere = pl.BlockSpec(memory_space=pl.ANY)
    return pl.pallas_call(
        body,
        out_shape=[
            jax.ShapeDtypeStruct(shape, dtype) if hbm_out else pltpu.VMEM(shape, dtype)
            for shape, dtype in outs
        ],
        in_specs=[anywhere if i in hbm else vmem for i in range(len(args))],
        out_specs=[anywhere if hbm_out else vmem] * len(outs),
        scratch_shapes=list(scratch),
        compiler_params=pltpu.CompilerParams(vmem_limit_bytes=VMEM_LIMIT),
        cost_estimate=pl.CostEstimate(
            flops=int(micros * FLOPS_PER_MICRO), bytes_accessed=0, transcendentals=0
        ),
    )(*[in_hbm(a) if i in hbm else in_vmem(a) for i, a in enumerate(args)])


def after(value, *others):
    return lax.optimization_barrier((value, *others))[0]


def tree_side(bit):
    return (lax.axis_index("leaf") >> bit) & 1


def column_side():
    leaf = lax.axis_index("leaf")
    return (leaf ^ (leaf >> 1)) & 1


def block(index, width):
    return pl.ds(pl.multiple_of(index * width, width), width)


def put_rows(scratch, upper, own, other):
    rows = own.shape[0]
    scratch[block(upper, rows), :] = own
    scratch[block(1 - upper, rows), :] = other


def put_columns(out, upper, own, other):
    width = own.shape[1]
    out[:, block(upper, width)] = own
    out[:, block(1 - upper, width)] = other


def two_levels(
    right_side, leaf_inverse, left_basis, right_basis, level_caps, top_left, top_right, top_caps
):
    rows, cols = right_side.shape[1:]
    rank = top_left.shape[2]
    half = cols // 2
    f32 = jnp.float32
    s1 = 1.0 / math.sqrt(rows)
    s2 = 1.0 / math.sqrt(rows * 2)
    st = 1.0 / math.sqrt(rows * 4)
    blocks = rows // rank
    square, wide, tall = (rank, rank), (rank, cols), (rows, cols)

    def span(i, n=1):
        return slice(i * rank, (i + n) * rank)

    def part(i, n=1):
        return slice(i * half, (i + n) * half)

    def start_body(
        rhs_hbm, inv_hbm, lb_hbm, rb_hbm, caps_hbm, tl_hbm, tr_hbm,
        x_ref, send, keep, inv_ref, lb, rb, caps, tl, tr, rhs_v, nexts, sems,
    ):
        def load(source, target, *at):
            copy = pltpu.make_async_copy(source, target, sems.at[at])
            copy.start()
            return copy

        first = [
            load(lb_hbm.at[0], lb.at[0], 2, 0),
            load(rb_hbm.at[1], rb.at[1], 2, 1),
            load(caps_hbm, caps, 2, 2),
        ]
        copies = []
        for i in range(blocks):
            copies.append(load(rhs_hbm.at[0, span(i), :], rhs_v.at[span(i), :], 0, i))
            copies.append(
                load(
                    inv_hbm.at[0, span(i), span(0, i + 1)],
                    inv_ref.at[span(i), span(0, i + 1)],
                    1,
                    i,
                )
            )
        basis1 = load(rb_hbm.at[0], rb.at[0], 2, 3)
        rest = [
            load(lb_hbm.at[1], lb.at[1], 2, 4),
            load(tl_hbm, tl, 2, 5),
            load(tr_hbm, tr, 2, 6),
        ]
        odd = tree_side(0)
        for copy in first:
            copy.wait()
        gram = (dot_t(rb[1, 0], lb[0, 0]) * s2).astype(BF)
        nexts[...] = dot(gram, caps[0, 0]).astype(BF)
        send[:, 2 * cols :] = nexts[:, block(1 - odd, rank)]
        for i in range(blocks):
            copies[2 * i].wait()
            copies[2 * i + 1].wait()
            x_ref[span(i), :] = dot(
                inv_ref[span(i), span(0, i + 1)], rhs_v[span(0, i + 1), :].astype(BF)
            )
        basis1.wait()
        state = x_ref[...].astype(BF)
        send[:, :cols] = (dot_t(rb[0, 0], state) * s1).astype(BF)
        keep[...] = dot_t(rb[1, 0], state) * s2 - dot(nexts[:, block(odd, rank)], send[:, :cols])
        send[:, cols : 2 * cols] = keep[...].astype(BF)
        for copy in rest:
            copy.wait()

    state0, pair_send, pair_keep, inverse, lb, rb, caps, tl, tr = call(
        start_body,
        [(tall, f32), ((rank, 2 * cols + rank), BF), (wide, f32), ((rows, rows), BF)]
        + [(a.shape, a.dtype) for a in (left_basis, right_basis, level_caps, top_left, top_right)],
        right_side,
        leaf_inverse,
        left_basis,
        right_basis,
        level_caps,
        top_left,
        top_right,
        hbm=range(7),
        scratch=[
            pltpu.VMEM(tall, f32),
            pltpu.VMEM((rank, 2 * rank), BF),
            pltpu.SemaphoreType.DMA((3, max(blocks, 7))),
        ],
    )
    pair_in = swap(pair_send, "leaf", 1)
    caps_here = after(top_caps, pair_send)
    caps_near = swap(caps_here, "top", 1)
    caps_far = swap(caps_here, "top", 2)

    def grams_body(lb, rb, caps, tl, tr, out):
        out[:, span(0)] = (dot_t(tl[0], tl[0]) * st).astype(BF)
        for i, basis in enumerate((tl[0], tr[0])):
            out[:, span(1 + i)] = (dot_t(lb[1, 0], basis) * s2).astype(BF)
        for i, basis in enumerate((tl[0], tr[0], rb[1, 0])):
            out[:, span(3 + i)] = (dot_t(lb[0, 0], basis) * s1).astype(BF)
        out[:, span(6, 2)] = caps[1, 0]

    (grams,) = call(
        grams_body,
        [((rank, 8 * rank), BF)],
        lb,
        rb,
        caps,
        tl,
        tr,
        micros=0.5,
    )
    def half_body(keep, own, sib, seen, out):
        out[...] = (
            keep[...]
            + sib[:, cols : 2 * cols]
            - dot(own[:, 2 * cols :], sib[:, :cols])
            - dot(sib[:, 2 * cols :], own[:, :cols])
        ).astype(BF)

    (half2,) = call(half_body, [(wide, BF)], pair_keep, pair_send, pair_in, grams, micros=0.2)
    half2_far = swap(half2, "leaf", 3)
    grams_sib = swap(after(grams, half2), "leaf", 1)

    def one_body(x0, own, sib, lb, caps, seen, x1, stack):
        put_rows(stack, tree_side(0), own[:, :cols], sib[:, :cols])
        coef = dot(caps[0, 0], stack[...]).astype(BF)
        x1[...] = x0[...] - dot(lb[0, 0], coef)

    (state1,) = call(
        one_body,
        [(tall, f32)],
        state0,
        pair_send,
        pair_in,
        lb,
        caps,
        half2,
        scratch=[pltpu.VMEM((2 * rank, cols), BF)],
        micros=0.4,
    )

    def sum_body(own, sib, out):
        out[...] = (own[:, span(0, 3)].astype(f32) + sib[:, span(0, 3)]).astype(BF)

    (gram_pair,) = call(sum_body, [((rank, 3 * rank), BF)], grams, grams_sib, micros=0.1)
    gram_far = swap(gram_pair, "leaf", 3)

    def two_body(x1, own, far, lb, caps, tl, tr, x2, send, keep, stack, scratch):
        side = column_side()
        put_rows(stack, tree_side(1), own[...], far[...])
        coef = dot(caps[1, 0], stack[...]).astype(BF)
        x2[...] = (x1[...] - dot(lb[1, 0], coef)).astype(BF)
        for i, basis in enumerate((tr[0], tl[0])):
            scratch[...] = dot_t(basis, x2[...]) * st
            send[:, part(i)] = scratch[:, block(1 - side, half)].astype(BF)
            keep[:, part(i)] = scratch[:, block(side, half)]

    state2, top_pair_send, top_keep = call(
        two_body,
        [(tall, BF), (wide, BF), (wide, f32)],
        state1,
        half2,
        half2_far,
        lb,
        caps,
        tl,
        tr,
        scratch=[pltpu.VMEM((2 * rank, cols), BF), pltpu.VMEM(wide, f32)],
        micros=5,
    )
    top_pair_in = swap(top_pair_send, "leaf", 1)

    caps_far_near = swap(after(caps_far, state2), "top", 1)

    def order_body(a, b, c, d, out):
        here = lax.axis_index("top")
        for i, piece in enumerate((a, b, c, d)):
            for k in range(4):
                out[span(i), span(k)] = piece[:, block(here ^ k, rank)]

    (caps_all,) = call(
        order_body,
        [((4 * rank, 4 * rank), BF)],
        top_caps,
        caps_near,
        caps_far,
        caps_far_near,
        micros=0.1,
    )


    def down_body(lb, x2, z5, z):
        z5[...] = dot_t(lb[1, 0], x2[...]) * s2
        z[:, :cols] = z5[...].astype(BF)
        z[:, cols:] = (dot_t(lb[0, 0], x2[...]) * s1).astype(BF)

    down5, down_send = call(
        down_body, [(wide, f32), ((rank, 2 * cols), BF)], lb, state2, micros=0.3
    )
    down_in = swap(down_send, "leaf", 1)

    def add_body(own, other, seen, seen2, out, out_b):
        out[...] = own[...] + other[:, :cols]
        out_b[...] = out[...].astype(BF)

    top_half, top_half_send = call(add_body, [(wide, f32), (wide, BF)], top_keep, top_pair_in, gram_pair, caps_all, micros=0.1)
    top_half_far = swap(top_half_send, "leaf", 3)
    down5, down5_send = call(
        add_body, [(wide, f32), (wide, BF)], down5, down_in, gram_pair, caps_all, micros=0.1
    )

    def column_body(own, far, gram, gram_far, out):
        out[:, : 2 * half] = (own[...] + far[...]).astype(BF)
        out[:, 2 * half :] = (gram[:, span(0)].astype(f32) + gram_far[:, span(0)]).astype(BF)

    (top_send,) = call(
        column_body,
        [((rank, 2 * half + rank), BF)],
        top_half,
        top_half_far,
        gram_pair,
        gram_far,
    )
    top_far = swap(top_send, "top", 2)
    top_near = swap(top_send, "top", 1)
    top_parts = top_send, top_near, top_far, swap(top_far, "top", 1)

    def under_body(x2, rb, tl, tr, inv, seen, out2, under):
        for c in range(blocks):
            column = inv[c * rank :, span(c)]
            out2[span(c), :] = dot_t(column, x2[c * rank :, :])
            for i, basis in enumerate((tl[0], tr[0], rb[1, 0], rb[0, 0])):
                under[span(c), span(i)] = dot_t(column, basis[c * rank :, :]).astype(BF)

    out2, under = call(
        under_body,
        [(tall, f32), ((rows, 4 * rank), BF)],
        state2,
        rb,
        tl,
        tr,
        inverse,
        top_send,
    )

    def top_body(a, b, c, d, caps, seen, out, up, down):
        pieces = (a, b, c, d)
        for i, piece in enumerate(pieces):
            up[span(i), :] = piece[:, part(0)]
        coef = dot(caps[...], up[...]).astype(BF)
        for i, piece in enumerate(pieces):
            down[span(i), :] = (
                piece[:, part(1)] - dot(piece[:, 2 * half :], coef[span(i), :])
            ).astype(BF)
        out[:, part(0)] = coef[:rank, :]
        out[:, part(1)] = dot(caps[:rank, :], down[...]).astype(BF)

    (back_send,) = call(
        top_body,
        [(wide, BF)],
        *top_parts,
        caps_all,
        out2,
        scratch=[pltpu.VMEM((4 * rank, half), BF)] * 2,
    )
    down5_far = swap(after(down5_send, back_send), "leaf", 3)
    back_in = swap(back_send, "leaf", 1)

    def last_body(
        out2, under, back, back_sib, down5, down5_far, gram, gram_far, grams, grams_sib,
        z, z_sib, caps, out, coefs, stack, out_v, sems,
    ):
        side = column_side()
        for i in range(2):
            put_columns(coefs.at[span(i), :], side, back[:, part(i)], back_sib[:, part(i)])
        both = coefs[span(0, 2), :]
        put_rows(
            stack,
            tree_side(1),
            (down5[...] - dot(gram[:, span(1, 2)], both)).astype(BF),
            (down5_far[...] - dot(gram_far[:, span(1, 2)], both)).astype(BF),
        )
        coef5 = dot(caps[1, 0], stack[...]).astype(BF)
        coef5_sib = dot(grams_sib[:, span(6, 2)], stack[...]).astype(BF)
        coefs[span(2), :] = coef5

        def proj(zs, gram1, coef):
            return (
                zs[:, cols:] - dot(gram1[:, span(3, 2)], both) - dot(gram1[:, span(5)], coef)
            ).astype(BF)

        put_rows(stack, tree_side(0), proj(z, grams, coef5), proj(z_sib, grams_sib, coef5_sib))
        coefs[span(3), :] = dot(caps[0, 0], stack[...]).astype(BF)
        copies = []
        for c in range(blocks):
            out_v[span(c), :] = out2[span(c), :] - dot(under[span(c), :], coefs[...])
            copy = pltpu.make_async_copy(out_v.at[span(c), :], out.at[0, span(c), :], sems.at[c])
            copy.start()
            copies.append(copy)
        for copy in copies:
            copy.wait()

    (out,) = call(
        last_body,
        [((1, rows, cols), f32)],
        out2,
        under,
        back_send,
        back_in,
        down5,
        down5_far,
        gram_pair,
        gram_far,
        grams,
        grams_sib,
        down_send,
        down_in,
        caps,
        hbm_out=True,
        scratch=[
            pltpu.VMEM((4 * rank, cols), BF),
            pltpu.VMEM((2 * rank, cols), BF),
            pltpu.VMEM(tall, f32),
            pltpu.SemaphoreType.DMA((blocks,)),
        ],
    )
    return out


def on_device(*args):
    levels = args[2].shape[0]
    sizes = lax.axis_size("leaf"), lax.axis_size("top")
    if levels == 2 and sizes == (4, 4):
        return two_levels(*args)
    return step_by_step(*args)


def solution(mesh):
    rows = P(("parts", "top"), "leaf", None)
    level_rows = P(None, ("parts", "top"), "leaf", None)
    return jax.shard_map(
        on_device,
        mesh=mesh,
        in_specs=(
            rows,
            rows,
            level_rows,
            level_rows,
            level_rows,
            rows,
            rows,
            P(("parts", "top"), None),
        ),
        out_specs=rows,
        check_vma=False,
    )
```

```python
import math

import jax
import jax.numpy as jnp
from jax import lax
from jax.experimental import pallas as pl
from jax.experimental.pallas import tpu as pltpu
from jax.sharding import PartitionSpec as P

BF = jnp.bfloat16
VMEM_LIMIT = 8 * 2**20
FLOPS_PER_MICRO = 1e9


def swap(value, axis, mask):
    pairs = [(source, source ^ mask) for source in range(lax.axis_size(axis))]
    return lax.ppermute(value, axis, pairs)


def dot(a, b):
    return jnp.dot(a, b, preferred_element_type=jnp.float32)


def dot_t(a, b):
    return lax.dot_general(a, b, (((0,), (0,)), ((), ())), preferred_element_type=jnp.float32)


def ordered(upper_side, own, other):
    return jnp.where(
        upper_side, jnp.concatenate([other, own], 0), jnp.concatenate([own, other], 0)
    )


def level_step(current, project_basis, update_basis, caps_rows, level_num):
    leaf_rows = current.shape[0]
    shift_bits = level_num - 1
    partial_value = dot_t(project_basis, current.astype(BF)) * (
        1.0 / math.sqrt(leaf_rows * 2**shift_bits)
    )
    for bit_index in range(shift_bits):
        partial_value = partial_value + swap(partial_value, "leaf", 2**bit_index)
    own = partial_value.astype(BF)
    other = swap(own, "leaf", 2**shift_bits)
    upper_side = (lax.axis_index("leaf") >> shift_bits) & 1 == 1
    stacked = ordered(upper_side, own, other)
    weights = dot(caps_rows, stacked).astype(BF)
    return current - dot(update_basis, weights)


def top_step(current, project_basis, update_basis, caps_rows):
    leaf_count = lax.axis_size("leaf")
    partial_value = dot_t(project_basis, current.astype(BF)) * (
        1.0 / math.sqrt(leaf_count * current.shape[0])
    )
    column_total = lax.psum(partial_value, "leaf")
    stacked = lax.all_gather(column_total.astype(BF), "top", axis=0, tiled=True)
    weights = dot(caps_rows, stacked).astype(BF)
    return current - dot(update_basis, weights)


def step_by_step(
    right_side, leaf_inverse, left_basis, right_basis, level_caps, top_left, top_right, top_caps
):
    levels = left_basis.shape[0]
    lefts = [left_basis[k, 0] for k in range(levels)]
    rights = [right_basis[k, 0] for k in range(levels)]
    current = dot(leaf_inverse[0], right_side[0].astype(BF))
    for k in range(levels):
        current = level_step(current, rights[k], lefts[k], level_caps[k, 0], k + 1)
    current = top_step(current, top_right[0], top_left[0], top_caps)
    current = top_step(current, top_left[0], top_right[0], top_caps)
    for k in reversed(range(levels)):
        current = level_step(current, lefts[k], rights[k], level_caps[k, 0], k + 1)
    return dot_t(leaf_inverse[0], current.astype(BF))[None]


def in_hbm(value):
    return pltpu.with_memory_space_constraint(value, pltpu.HBM)


def in_vmem(value):
    return pltpu.with_memory_space_constraint(value, pltpu.VMEM)


def call(body, outs, *args, scratch=(), hbm=(), hbm_out=False, micros=1):
    vmem = pl.BlockSpec(memory_space=pltpu.VMEM)
    anywhere = pl.BlockSpec(memory_space=pl.ANY)
    return pl.pallas_call(
        body,
        out_shape=[
            jax.ShapeDtypeStruct(shape, dtype) if hbm_out else pltpu.VMEM(shape, dtype)
            for shape, dtype in outs
        ],
        in_specs=[anywhere if i in hbm else vmem for i in range(len(args))],
        out_specs=[anywhere if hbm_out else vmem] * len(outs),
        scratch_shapes=list(scratch),
        compiler_params=pltpu.CompilerParams(vmem_limit_bytes=VMEM_LIMIT),
        cost_estimate=pl.CostEstimate(
            flops=int(micros * FLOPS_PER_MICRO), bytes_accessed=0, transcendentals=0
        ),
    )(*[in_hbm(a) if i in hbm else in_vmem(a) for i, a in enumerate(args)])


def after(value, *others):
    return lax.optimization_barrier((value, *others))[0]


def tree_side(bit):
    return (lax.axis_index("leaf") >> bit) & 1


def column_side():
    leaf = lax.axis_index("leaf")
    return (leaf ^ (leaf >> 1)) & 1


def block(index, width):
    return pl.ds(pl.multiple_of(index * width, width), width)


def put_rows(scratch, upper, own, other):
    rows = own.shape[0]
    scratch[block(upper, rows), :] = own
    scratch[block(1 - upper, rows), :] = other


def put_columns(out, upper, own, other):
    width = own.shape[1]
    out[:, block(upper, width)] = own
    out[:, block(1 - upper, width)] = other


def two_levels(
    right_side, leaf_inverse, left_basis, right_basis, level_caps, top_left, top_right, top_caps
):
    rows, cols = right_side.shape[1:]
    rank = top_left.shape[2]
    half = cols // 2
    f32 = jnp.float32
    s1 = 1.0 / math.sqrt(rows)
    s2 = 1.0 / math.sqrt(rows * 2)
    st = 1.0 / math.sqrt(rows * 4)
    blocks = rows // rank
    square, wide, tall = (rank, rank), (rank, cols), (rows, cols)

    def span(i, n=1):
        return slice(i * rank, (i + n) * rank)

    def part(i, n=1):
        return slice(i * half, (i + n) * half)

    def start_body(
        rhs_hbm, inv_hbm, lb_hbm, rb_hbm, caps_hbm, tl_hbm, tr_hbm,
        x_ref, send, keep, inv_ref, lb, rb, caps, tl, tr, rhs_v, nexts, sems,
    ):
        def load(source, target, *at):
            copy = pltpu.make_async_copy(source, target, sems.at[at])
            copy.start()
            return copy

        first = [
            load(lb_hbm.at[0], lb.at[0], 2, 0),
            load(rb_hbm.at[1], rb.at[1], 2, 1),
            load(caps_hbm, caps, 2, 2),
        ]
        copies = []
        for i in range(blocks):
            copies.append(load(rhs_hbm.at[0, span(i), :], rhs_v.at[span(i), :], 0, i))
            copies.append(
                load(
                    inv_hbm.at[0, span(i), span(0, i + 1)],
                    inv_ref.at[span(i), span(0, i + 1)],
                    1,
                    i,
                )
            )
        basis1 = load(rb_hbm.at[0], rb.at[0], 2, 3)
        rest = [
            load(lb_hbm.at[1], lb.at[1], 2, 4),
            load(tl_hbm, tl, 2, 5),
            load(tr_hbm, tr, 2, 6),
        ]
        odd = tree_side(0)
        for copy in first:
            copy.wait()
        gram = (dot_t(rb[1, 0], lb[0, 0]) * s2).astype(BF)
        nexts[...] = dot(gram, caps[0, 0]).astype(BF)
        send[:, 2 * cols :] = nexts[:, block(1 - odd, rank)]
        for i in range(blocks):
            copies[2 * i].wait()
            copies[2 * i + 1].wait()
            x_ref[span(i), :] = dot(
                inv_ref[span(i), span(0, i + 1)], rhs_v[span(0, i + 1), :].astype(BF)
            )
        basis1.wait()
        state = x_ref[...].astype(BF)
        send[:, :cols] = (dot_t(rb[0, 0], state) * s1).astype(BF)
        keep[...] = dot_t(rb[1, 0], state) * s2 - dot(nexts[:, block(odd, rank)], send[:, :cols])
        send[:, cols : 2 * cols] = keep[...].astype(BF)
        for copy in rest:
            copy.wait()

    state0, pair_send, pair_keep, inverse, lb, rb, caps, tl, tr = call(
        start_body,
        [(tall, f32), ((rank, 2 * cols + rank), BF), (wide, f32), ((rows, rows), BF)]
        + [(a.shape, a.dtype) for a in (left_basis, right_basis, level_caps, top_left, top_right)],
        right_side,
        leaf_inverse,
        left_basis,
        right_basis,
        level_caps,
        top_left,
        top_right,
        hbm=range(7),
        scratch=[
            pltpu.VMEM(tall, f32),
            pltpu.VMEM((rank, 2 * rank), BF),
            pltpu.SemaphoreType.DMA((3, max(blocks, 7))),
        ],
    )
    pair_in = swap(pair_send, "leaf", 1)
    caps_here = after(top_caps, pair_send)
    caps_near = swap(caps_here, "top", 1)
    caps_far = swap(caps_here, "top", 2)

    def grams_body(lb, rb, caps, tl, tr, seen, out, late):
        out[:, span(0)] = (dot_t(tl[0], tl[0]) * st).astype(BF)
        for i, basis in enumerate((tl[0], tr[0])):
            out[:, span(1 + i)] = (dot_t(lb[1, 0], basis) * s2).astype(BF)
        for i, basis in enumerate((tl[0], tr[0], rb[1, 0])):
            late[:, span(i)] = (dot_t(lb[0, 0], basis) * s1).astype(BF)
        late[:, span(3, 2)] = caps[1, 0]

    grams, late = call(
        grams_body,
        [((rank, 3 * rank), BF), ((rank, 5 * rank), BF)],
        lb,
        rb,
        caps,
        tl,
        tr,
        caps_near,
        micros=10,
    )
    grams_sib = swap(grams, "leaf", 1)

    def half_body(keep, own, sib, out):
        out[...] = (
            keep[...]
            + sib[:, cols : 2 * cols]
            - dot(own[:, 2 * cols :], sib[:, :cols])
            - dot(sib[:, 2 * cols :], own[:, :cols])
        ).astype(BF)

    (half2,) = call(half_body, [(wide, BF)], pair_keep, pair_send, pair_in, micros=3)
    half2_far = swap(half2, "leaf", 3)
    late_sib = swap(after(late, half2), "leaf", 1)

    def sum_body(own, sib, seen, out):
        out[...] = (own[...].astype(f32) + sib[...]).astype(BF)

    (gram_pair,) = call(sum_body, [((rank, 3 * rank), BF)], grams, grams_sib, half2)
    gram_far = swap(gram_pair, "leaf", 3)

    def one_body(x0, own, sib, lb, caps, seen, seen2, x1, stack):
        put_rows(stack, tree_side(0), own[:, :cols], sib[:, :cols])
        coef = dot(caps[0, 0], stack[...]).astype(BF)
        x1[...] = x0[...] - dot(lb[0, 0], coef)

    (state1,) = call(
        one_body,
        [(tall, f32)],
        state0,
        pair_send,
        pair_in,
        lb,
        caps,
        half2,
        grams_sib,
        scratch=[pltpu.VMEM((2 * rank, cols), BF)],
    )

    def two_body(x1, own, far, lb, caps, tl, tr, x2, send, keep, stack, scratch):
        side = column_side()
        put_rows(stack, tree_side(1), own[...], far[...])
        coef = dot(caps[1, 0], stack[...]).astype(BF)
        x2[...] = (x1[...] - dot(lb[1, 0], coef)).astype(BF)
        for i, basis in enumerate((tr[0], tl[0])):
            scratch[...] = dot_t(basis, x2[...]) * st
            send[:, part(i)] = scratch[:, block(1 - side, half)].astype(BF)
            keep[:, part(i)] = scratch[:, block(side, half)]

    state2, top_pair_send, top_keep = call(
        two_body,
        [(tall, BF), (wide, BF), (wide, f32)],
        state1,
        half2,
        half2_far,
        lb,
        caps,
        tl,
        tr,
        scratch=[pltpu.VMEM((2 * rank, cols), BF), pltpu.VMEM(wide, f32)],
    )
    top_pair_in = swap(top_pair_send, "leaf", 1)

    def down_body(lb, x2, z5, z):
        z5[...] = dot_t(lb[1, 0], x2[...]) * s2
        z[:, :cols] = z5[...].astype(BF)
        z[:, cols:] = (dot_t(lb[0, 0], x2[...]) * s1).astype(BF)

    down5, down_send = call(down_body, [(wide, f32), ((rank, 2 * cols), BF)], lb, state2)
    down_in = swap(down_send, "leaf", 1)

    def add_body(own, other, seen, out, out_b):
        out[...] = own[...] + other[:, :cols]
        out_b[...] = out[...].astype(BF)

    top_half, top_half_send = call(add_body, [(wide, f32), (wide, BF)], top_keep, top_pair_in, late_sib)
    top_half_far = swap(top_half_send, "leaf", 3)
    down5, down5_send = call(
        add_body, [(wide, f32), (wide, BF)], down5, down_in, gram_pair
    )

    caps_far_near = swap(after(caps_far, down_send), "top", 1)

    def order_body(a, b, c, d, out):
        here = lax.axis_index("top")
        for i, piece in enumerate((a, b, c, d)):
            for k in range(4):
                out[span(i), span(k)] = piece[:, block(here ^ k, rank)]

    (caps_all,) = call(
        order_body,
        [((4 * rank, 4 * rank), BF)],
        top_caps,
        caps_near,
        caps_far,
        caps_far_near,
        micros=0.1,
    )

    def column_body(own, far, gram, gram_far, seen, out):
        out[:, : 2 * half] = (own[...] + far[...]).astype(BF)
        out[:, 2 * half :] = (gram[:, span(0)].astype(f32) + gram_far[:, span(0)]).astype(BF)

    (top_send,) = call(
        column_body,
        [((rank, 2 * half + rank), BF)],
        top_half,
        top_half_far,
        gram_pair,
        gram_far,
        caps_all,
    )
    top_far = swap(top_send, "top", 2)
    top_near = swap(top_send, "top", 1)
    top_parts = top_send, top_near, top_far, swap(top_far, "top", 1)

    def under_body(x2, rb, tl, tr, inv, seen, out2, under):
        for c in range(blocks):
            column = inv[c * rank :, span(c)]
            out2[span(c), :] = dot_t(column, x2[c * rank :, :])
            for i, basis in enumerate((tl[0], tr[0], rb[1, 0], rb[0, 0])):
                under[span(c), span(i)] = dot_t(column, basis[c * rank :, :]).astype(BF)

    out2, under = call(
        under_body,
        [(tall, f32), ((rows, 4 * rank), BF)],
        state2,
        rb,
        tl,
        tr,
        inverse,
        top_send,
    )

    def top_body(a, b, c, d, caps, seen, out, up, down):
        pieces = (a, b, c, d)
        for i, piece in enumerate(pieces):
            up[span(i), :] = piece[:, part(0)]
        coef = dot(caps[...], up[...]).astype(BF)
        for i, piece in enumerate(pieces):
            down[span(i), :] = (
                piece[:, part(1)] - dot(piece[:, 2 * half :], coef[span(i), :])
            ).astype(BF)
        out[:, part(0)] = coef[:rank, :]
        out[:, part(1)] = dot(caps[:rank, :], down[...]).astype(BF)

    (back_send,) = call(
        top_body,
        [(wide, BF)],
        *top_parts,
        caps_all,
        out2,
        scratch=[pltpu.VMEM((4 * rank, half), BF)] * 2,
    )
    down5_far = swap(after(down5_send, back_send), "leaf", 3)
    back_in = swap(back_send, "leaf", 1)

    def last_body(
        out2, under, back, back_sib, down5, down5_far, gram, gram_far, late, late_sib,
        z, z_sib, caps, out, coefs, stack, out_v, sems,
    ):
        side = column_side()
        for i in range(2):
            put_columns(coefs.at[span(i), :], side, back[:, part(i)], back_sib[:, part(i)])
        both = coefs[span(0, 2), :]
        put_rows(
            stack,
            tree_side(1),
            (down5[...] - dot(gram[:, span(1, 2)], both)).astype(BF),
            (down5_far[...] - dot(gram_far[:, span(1, 2)], both)).astype(BF),
        )
        coef5 = dot(caps[1, 0], stack[...]).astype(BF)
        coef5_sib = dot(late_sib[:, span(3, 2)], stack[...]).astype(BF)
        coefs[span(2), :] = coef5

        def proj(zs, grams, coef):
            return (
                zs[:, cols:] - dot(grams[:, span(0, 2)], both) - dot(grams[:, span(2)], coef)
            ).astype(BF)

        put_rows(stack, tree_side(0), proj(z, late, coef5), proj(z_sib, late_sib, coef5_sib))
        coefs[span(3), :] = dot(caps[0, 0], stack[...]).astype(BF)
        copies = []
        for c in range(blocks):
            out_v[span(c), :] = out2[span(c), :] - dot(under[span(c), :], coefs[...])
            copy = pltpu.make_async_copy(out_v.at[span(c), :], out.at[0, span(c), :], sems.at[c])
            copy.start()
            copies.append(copy)
        for copy in copies:
            copy.wait()

    (out,) = call(
        last_body,
        [((1, rows, cols), f32)],
        out2,
        under,
        back_send,
        back_in,
        down5,
        down5_far,
        gram_pair,
        gram_far,
        late,
        late_sib,
        down_send,
        down_in,
        caps,
        hbm_out=True,
        scratch=[
            pltpu.VMEM((4 * rank, cols), BF),
            pltpu.VMEM((2 * rank, cols), BF),
            pltpu.VMEM(tall, f32),
            pltpu.SemaphoreType.DMA((blocks,)),
        ],
    )
    return out


def on_device(*args):
    levels = args[2].shape[0]
    sizes = lax.axis_size("leaf"), lax.axis_size("top")
    if levels == 2 and sizes == (4, 4):
        return two_levels(*args)
    return step_by_step(*args)


def solution(mesh):
    rows = P(("parts", "top"), "leaf", None)
    level_rows = P(None, ("parts", "top"), "leaf", None)
    return jax.shard_map(
        on_device,
        mesh=mesh,
        in_specs=(
            rows,
            rows,
            level_rows,
            level_rows,
            level_rows,
            rows,
            rows,
            P(("parts", "top"), None),
        ),
        out_specs=rows,
        check_vma=False,
    )
```

```python
import math

import jax
import jax.numpy as jnp
from jax import lax
from jax.experimental import pallas as pl
from jax.experimental.pallas import tpu as pltpu
from jax.sharding import PartitionSpec as P

BF = jnp.bfloat16
VMEM_LIMIT = 8 * 2**20
FLOPS_PER_MICRO = 1e9


def swap(value, axis, mask):
    pairs = [(source, source ^ mask) for source in range(lax.axis_size(axis))]
    return lax.ppermute(value, axis, pairs)


def dot(a, b):
    return jnp.dot(a, b, preferred_element_type=jnp.float32)


def dot_t(a, b):
    return lax.dot_general(a, b, (((0,), (0,)), ((), ())), preferred_element_type=jnp.float32)


def ordered(upper_side, own, other):
    return jnp.where(
        upper_side, jnp.concatenate([other, own], 0), jnp.concatenate([own, other], 0)
    )


def level_step(current, project_basis, update_basis, caps_rows, level_num):
    leaf_rows = current.shape[0]
    shift_bits = level_num - 1
    partial_value = dot_t(project_basis, current.astype(BF)) * (
        1.0 / math.sqrt(leaf_rows * 2**shift_bits)
    )
    for bit_index in range(shift_bits):
        partial_value = partial_value + swap(partial_value, "leaf", 2**bit_index)
    own = partial_value.astype(BF)
    other = swap(own, "leaf", 2**shift_bits)
    upper_side = (lax.axis_index("leaf") >> shift_bits) & 1 == 1
    stacked = ordered(upper_side, own, other)
    weights = dot(caps_rows, stacked).astype(BF)
    return current - dot(update_basis, weights)


def top_step(current, project_basis, update_basis, caps_rows):
    leaf_count = lax.axis_size("leaf")
    partial_value = dot_t(project_basis, current.astype(BF)) * (
        1.0 / math.sqrt(leaf_count * current.shape[0])
    )
    column_total = lax.psum(partial_value, "leaf")
    stacked = lax.all_gather(column_total.astype(BF), "top", axis=0, tiled=True)
    weights = dot(caps_rows, stacked).astype(BF)
    return current - dot(update_basis, weights)


def step_by_step(
    right_side, leaf_inverse, left_basis, right_basis, level_caps, top_left, top_right, top_caps
):
    levels = left_basis.shape[0]
    lefts = [left_basis[k, 0] for k in range(levels)]
    rights = [right_basis[k, 0] for k in range(levels)]
    current = dot(leaf_inverse[0], right_side[0].astype(BF))
    for k in range(levels):
        current = level_step(current, rights[k], lefts[k], level_caps[k, 0], k + 1)
    current = top_step(current, top_right[0], top_left[0], top_caps)
    current = top_step(current, top_left[0], top_right[0], top_caps)
    for k in reversed(range(levels)):
        current = level_step(current, lefts[k], rights[k], level_caps[k, 0], k + 1)
    return dot_t(leaf_inverse[0], current.astype(BF))[None]


def in_hbm(value):
    return pltpu.with_memory_space_constraint(value, pltpu.HBM)


def in_vmem(value):
    return pltpu.with_memory_space_constraint(value, pltpu.VMEM)


def call(body, outs, *args, scratch=(), hbm=(), hbm_out=False, micros=1):
    vmem = pl.BlockSpec(memory_space=pltpu.VMEM)
    anywhere = pl.BlockSpec(memory_space=pl.ANY)
    return pl.pallas_call(
        body,
        out_shape=[
            jax.ShapeDtypeStruct(shape, dtype) if hbm_out else pltpu.VMEM(shape, dtype)
            for shape, dtype in outs
        ],
        in_specs=[anywhere if i in hbm else vmem for i in range(len(args))],
        out_specs=[anywhere if hbm_out else vmem] * len(outs),
        scratch_shapes=list(scratch),
        compiler_params=pltpu.CompilerParams(vmem_limit_bytes=VMEM_LIMIT),
        cost_estimate=pl.CostEstimate(
            flops=int(micros * FLOPS_PER_MICRO), bytes_accessed=0, transcendentals=0
        ),
    )(*[in_hbm(a) if i in hbm else in_vmem(a) for i, a in enumerate(args)])


def after(value, *others):
    return lax.optimization_barrier((value, *others))[0]


def tree_side(bit):
    return (lax.axis_index("leaf") >> bit) & 1


def column_side():
    leaf = lax.axis_index("leaf")
    return (leaf ^ (leaf >> 1)) & 1


def block(index, width):
    return pl.ds(pl.multiple_of(index * width, width), width)


def put_rows(scratch, upper, own, other):
    rows = own.shape[0]
    scratch[block(upper, rows), :] = own
    scratch[block(1 - upper, rows), :] = other


def put_columns(out, upper, own, other):
    width = own.shape[1]
    out[:, block(upper, width)] = own
    out[:, block(1 - upper, width)] = other


def two_levels(
    right_side, leaf_inverse, left_basis, right_basis, level_caps, top_left, top_right, top_caps
):
    rows, cols = right_side.shape[1:]
    rank = top_left.shape[2]
    half = cols // 2
    f32 = jnp.float32
    s1 = 1.0 / math.sqrt(rows)
    s2 = 1.0 / math.sqrt(rows * 2)
    st = 1.0 / math.sqrt(rows * 4)
    blocks = rows // rank
    square, wide, tall = (rank, rank), (rank, cols), (rows, cols)

    def span(i, n=1):
        return slice(i * rank, (i + n) * rank)

    def part(i, n=1):
        return slice(i * half, (i + n) * half)

    def start_body(
        rhs_hbm, inv_hbm, lb_hbm, rb_hbm, caps_hbm, tl_hbm, tr_hbm,
        x_ref, send, inv_ref, lb, rb, caps, tl, tr, rhs_v, sems,
    ):
        def load(source, target, *at):
            copy = pltpu.make_async_copy(source, target, sems.at[at])
            copy.start()
            return copy

        copies = []
        for i in range(blocks):
            copies.append(load(rhs_hbm.at[0, span(i), :], rhs_v.at[span(i), :], 0, i))
            copies.append(
                load(
                    inv_hbm.at[0, span(i), span(0, i + 1)],
                    inv_ref.at[span(i), span(0, i + 1)],
                    1,
                    i,
                )
            )
        pairs = ((rb_hbm, rb), (lb_hbm, lb), (tl_hbm, tl), (tr_hbm, tr), (caps_hbm, caps))
        bases = [load(source, target, 2, i) for i, (source, target) in enumerate(pairs)]
        for i in range(blocks):
            copies[2 * i].wait()
            copies[2 * i + 1].wait()
            x_ref[span(i), :] = dot(
                inv_ref[span(i), span(0, i + 1)], rhs_v[span(0, i + 1), :].astype(BF)
            )
        bases[0].wait()
        send[...] = (dot_t(rb[0, 0], x_ref[...].astype(BF)) * s1).astype(BF)
        for copy in bases[1:]:
            copy.wait()

    state0, proj1, inverse, lb, rb, caps, tl, tr = call(
        start_body,
        [(tall, f32), (wide, BF), ((rows, rows), BF)]
        + [(a.shape, a.dtype) for a in (left_basis, right_basis, level_caps, top_left, top_right)],
        right_side,
        leaf_inverse,
        left_basis,
        right_basis,
        level_caps,
        top_left,
        top_right,
        hbm=range(7),
        scratch=[pltpu.VMEM(tall, f32), pltpu.SemaphoreType.DMA((3, max(blocks, 5)))],
    )
    proj1_sib = swap(proj1, "leaf", 1)
    caps_here = after(top_caps, proj1)
    caps_near = swap(caps_here, "top", 1)
    caps_far = swap(caps_here, "top", 2)

    def early_body(lb, caps, tl, tr, seen, out):
        for i, basis in enumerate((tr, tl)):
            gram = (dot_t(basis[0], lb[1, 0]) * st).astype(BF)
            out[:, span(2 * i, 2)] = dot(gram, caps[1, 0]).astype(BF)
        out[:, span(4)] = (dot_t(tl[0], tl[0]) * st).astype(BF)

    (early,) = call(
        early_body, [((rank, 5 * rank), BF)], lb, caps, tl, tr, caps_near, micros=10
    )
    early_sib = swap(early, "leaf", 1)

    def one_body(x0, p, p_sib, lb, rb, caps, tl, tr, x1, send, keep, stack, scratch):
        side = column_side()
        put_rows(stack, tree_side(0), p[...], p_sib[...])
        coef = dot(caps[0, 0], stack[...]).astype(BF)
        x1[...] = x0[...] - dot(lb[0, 0], coef)
        state = x1[...].astype(BF)
        keep[:, :cols] = dot_t(rb[1, 0], state) * s2
        send[:, :cols] = keep[:, :cols].astype(BF)
        for i, basis in enumerate((tr, tl)):
            scratch[...] = dot_t(basis[0], state) * st
            send[:, part(2 + i)] = scratch[:, block(1 - side, half)].astype(BF)
            keep[:, part(2 + i)] = scratch[:, block(side, half)]

    state1, pair_send, pair_keep = call(
        one_body,
        [(tall, f32), ((rank, 2 * cols), BF), ((rank, 2 * cols), f32)],
        state0,
        proj1,
        proj1_sib,
        lb,
        rb,
        caps,
        tl,
        tr,
        scratch=[pltpu.VMEM((2 * rank, cols), BF), pltpu.VMEM(wide, f32)],
        micros=3,
    )
    pair_in = swap(pair_send, "leaf", 1)

    def pair_body(own, sib, seen, send, keep, gram, scratch):
        upper = tree_side(1)
        for i in range(2):
            scratch[...] = (own[:, span(2 * i, 2)].astype(f32) + sib[:, span(2 * i, 2)]).astype(BF)
            send[:, span(i)] = scratch[:, block(1 - upper, rank)]
            keep[:, span(2 * i)] = scratch[:, block(upper, rank)]
            keep[:, span(2 * i + 1)] = send[:, span(i)]
        gram[...] = own[:, span(4)].astype(f32) + sib[:, span(4)]
        send[:, span(2)] = gram[...].astype(BF)

    next_send, next_keep, gram_pair = call(
        pair_body,
        [((rank, 3 * rank), BF), ((rank, 4 * rank), BF), (square, f32)],
        early,
        early_sib,
        state1,
        scratch=[pltpu.VMEM((rank, 2 * rank), BF)],
        micros=0.1,
    )
    next_far = swap(next_send, "leaf", 3)
    def half_body(keep, pair, nexts, send, keep2):
        side = column_side()
        send[:, :cols] = (keep[:, :cols] + pair[:, :cols]).astype(BF)
        own = send[:, block(side, half)]
        for i in range(2):
            keep2[:, part(i)] = (
                keep[:, part(2 + i)] + pair[:, part(2 + i)] - dot(nexts[:, span(2 * i)], own)
            )
        send[:, cols:] = keep2[...].astype(BF)

    cross_send, cross_keep = call(
        half_body,
        [((rank, 2 * cols), BF), (wide, f32)],
        pair_keep,
        pair_in,
        next_keep,
        micros=5,
    )
    cross_in = swap(cross_send, "leaf", 3)

    caps_far_near = swap(after(caps_far, cross_send), "top", 1)

    def order_body(a, b, c, d, out):
        here = lax.axis_index("top")
        for i, piece in enumerate((a, b, c, d)):
            for k in range(4):
                out[span(i), span(k)] = piece[:, block(here ^ k, rank)]

    (caps_all,) = call(
        order_body,
        [((4 * rank, 4 * rank), BF)],
        top_caps,
        caps_near,
        caps_far,
        caps_far_near,
        micros=0.1,
    )

    def late_body(lb, rb, caps, tl, tr, seen, seen2, out, gram5):
        for i, basis in enumerate((tl[0], tr[0])):
            out[:, span(i)] = (dot_t(lb[0, 0], basis) * s1).astype(BF)
            gram5[:, span(i)] = (dot_t(lb[1, 0], basis) * s2).astype(BF)
        out[:, span(2)] = (dot_t(lb[0, 0], rb[1, 0]) * s1).astype(BF)
        out[:, span(3, 2)] = caps[1, 0]

    late, gram5 = call(
        late_body,
        [((rank, 5 * rank), BF), ((rank, 2 * rank), BF)],
        lb,
        rb,
        caps,
        tl,
        tr,
        cross_send,
        next_far,
        micros=5,
    )
    late_sib = swap(late, "leaf", 1)

    def column_body(send, keep2, far, nexts, nexts_far, gram, seen, seen2, out):
        side = column_side()
        own, other = send[:, block(side, half)], far[:, block(side, half)]
        for i in range(2):
            out[:, part(i)] = (
                keep2[:, part(i)]
                + far[:, part(2 + i)]
                - dot(nexts[:, span(2 * i + 1)], other)
                - dot(nexts_far[:, span(i)], own)
            ).astype(BF)
        out[:, 2 * half :] = (gram[...] + nexts_far[:, span(2)]).astype(BF)

    (top_send,) = call(
        column_body,
        [((rank, 2 * half + rank), BF)],
        cross_send,
        cross_keep,
        cross_in,
        next_keep,
        next_far,
        gram_pair,
        late,
        caps_all,
        micros=0.2,
    )
    top_near = swap(top_send, "top", 1)
    top_far = swap(top_send, "top", 2)

    def two_body(x1, send, far, lb, caps, gram5, seen, x2, z5, z, stack):
        put_rows(stack, tree_side(1), send[:, :cols], far[:, :cols])
        coef = dot(caps[1, 0], stack[...]).astype(BF)
        x2[...] = (x1[...] - dot(lb[1, 0], coef)).astype(BF)
        z5[...] = dot_t(lb[1, 0], x2[...]) * s2
        z[:, :cols] = z5[...].astype(BF)
        z[:, cols : 2 * cols] = (dot_t(lb[0, 0], x2[...]) * s1).astype(BF)
        z[:, 2 * cols :] = gram5[...]

    state2, down5, down_send = call(
        two_body,
        [(tall, BF), (wide, f32), ((rank, 2 * cols + 2 * rank), BF)],
        state1,
        cross_send,
        cross_in,
        lb,
        caps,
        gram5,
        top_send,
        scratch=[pltpu.VMEM((2 * rank, cols), BF)],
        micros=0.1,
    )
    down_in = swap(down_send, "leaf", 1)
    top_parts = top_send, top_near, top_far, swap(after(top_far, state2), "top", 1)

    def under_body(x2, rb, tl, tr, inv, seen, out2, under):
        for c in range(blocks):
            column = inv[c * rank :, span(c)]
            out2[span(c), :] = dot_t(column, x2[c * rank :, :])
            for i, basis in enumerate((tl[0], tr[0], rb[1, 0], rb[0, 0])):
                under[span(c), span(i)] = dot_t(column, basis[c * rank :, :]).astype(BF)

    out2, under = call(
        under_body,
        [(tall, f32), ((rows, 4 * rank), BF)],
        state2,
        rb,
        tl,
        tr,
        inverse,
        late_sib,
    )

    def top_body(a, b, c, d, caps, seen, out, up, down):
        pieces = (a, b, c, d)
        for i, piece in enumerate(pieces):
            up[span(i), :] = piece[:, part(0)]
        coef = dot(caps[...], up[...]).astype(BF)
        for i, piece in enumerate(pieces):
            down[span(i), :] = (
                piece[:, part(1)] - dot(piece[:, 2 * half :], coef[span(i), :])
            ).astype(BF)
        out[:, part(0)] = coef[:rank, :]
        out[:, part(1)] = dot(caps[:rank, :], down[...]).astype(BF)

    (back_send,) = call(
        top_body,
        [(wide, BF)],
        *top_parts,
        caps_all,
        out2,
        scratch=[pltpu.VMEM((4 * rank, half), BF)] * 2,
    )
    back_in = swap(back_send, "leaf", 1)

    def down_body(back, back_sib, down5, z, z_sib, both, send):
        side = column_side()
        for i in range(2):
            put_columns(both.at[span(i), :], side, back[:, part(i)], back_sib[:, part(i)])
        gram = (z[:, 2 * cols :].astype(f32) + z_sib[:, 2 * cols :]).astype(BF)
        send[...] = (down5[...] + z_sib[:, :cols] - dot(gram, both[...])).astype(BF)

    both, half5 = call(
        down_body,
        [((2 * rank, cols), BF), (wide, BF)],
        back_send,
        back_in,
        down5,
        down_send,
        down_in,
        micros=0.3,
    )
    half5_far = swap(half5, "leaf", 3)

    def last_body(
        out2, under, both, half5, half5_far, late, late_sib, z, z_sib, caps, out,
        coefs, stack, out_v, sems,
    ):
        coefs[span(0, 2), :] = both[...]
        put_rows(stack, tree_side(1), half5[...], half5_far[...])
        coef5 = dot(caps[1, 0], stack[...]).astype(BF)
        coef5_sib = dot(late_sib[:, span(3, 2)], stack[...]).astype(BF)
        coefs[span(2), :] = coef5

        def proj(zs, gram, coef):
            return (
                zs[:, cols : 2 * cols]
                - dot(gram[:, span(0, 2)], both[...])
                - dot(gram[:, span(2)], coef)
            ).astype(BF)

        put_rows(stack, tree_side(0), proj(z, late, coef5), proj(z_sib, late_sib, coef5_sib))
        coefs[span(3), :] = dot(caps[0, 0], stack[...]).astype(BF)
        copies = []
        for c in range(blocks):
            out_v[span(c), :] = out2[span(c), :] - dot(under[span(c), :], coefs[...])
            copy = pltpu.make_async_copy(out_v.at[span(c), :], out.at[0, span(c), :], sems.at[c])
            copy.start()
            copies.append(copy)
        for copy in copies:
            copy.wait()

    (out,) = call(
        last_body,
        [((1, rows, cols), f32)],
        out2,
        under,
        both,
        half5,
        half5_far,
        late,
        late_sib,
        down_send,
        down_in,
        caps,
        hbm_out=True,
        scratch=[
            pltpu.VMEM((4 * rank, cols), BF),
            pltpu.VMEM((2 * rank, cols), BF),
            pltpu.VMEM(tall, f32),
            pltpu.SemaphoreType.DMA((blocks,)),
        ],
    )
    return out


def on_device(*args):
    levels = args[2].shape[0]
    sizes = lax.axis_size("leaf"), lax.axis_size("top")
    if levels == 2 and sizes == (4, 4):
        return two_levels(*args)
    return step_by_step(*args)


def solution(mesh):
    rows = P(("parts", "top"), "leaf", None)
    level_rows = P(None, ("parts", "top"), "leaf", None)
    return jax.shard_map(
        on_device,
        mesh=mesh,
        in_specs=(
            rows,
            rows,
            level_rows,
            level_rows,
            level_rows,
            rows,
            rows,
            P(("parts", "top"), None),
        ),
        out_specs=rows,
        check_vma=False,
    )
```

```python
import math

import jax
import jax.numpy as jnp
from jax import lax
from jax.experimental import pallas as pl
from jax.experimental.pallas import tpu as pltpu
from jax.sharding import PartitionSpec as P

BF = jnp.bfloat16
VMEM_LIMIT = 8 * 2**20
FLOPS_PER_MICRO = 1e9


def swap(value, axis, mask):
    pairs = [(source, source ^ mask) for source in range(lax.axis_size(axis))]
    return lax.ppermute(value, axis, pairs)


def dot(a, b):
    return jnp.dot(a, b, preferred_element_type=jnp.float32)


def dot_t(a, b):
    return lax.dot_general(a, b, (((0,), (0,)), ((), ())), preferred_element_type=jnp.float32)


def ordered(upper_side, own, other):
    return jnp.where(
        upper_side, jnp.concatenate([other, own], 0), jnp.concatenate([own, other], 0)
    )


def level_step(current, project_basis, update_basis, caps_rows, level_num):
    leaf_rows = current.shape[0]
    shift_bits = level_num - 1
    partial_value = dot_t(project_basis, current.astype(BF)) * (
        1.0 / math.sqrt(leaf_rows * 2**shift_bits)
    )
    for bit_index in range(shift_bits):
        partial_value = partial_value + swap(partial_value, "leaf", 2**bit_index)
    own = partial_value.astype(BF)
    other = swap(own, "leaf", 2**shift_bits)
    upper_side = (lax.axis_index("leaf") >> shift_bits) & 1 == 1
    stacked = ordered(upper_side, own, other)
    weights = dot(caps_rows, stacked).astype(BF)
    return current - dot(update_basis, weights)


def top_step(current, project_basis, update_basis, caps_rows):
    leaf_count = lax.axis_size("leaf")
    partial_value = dot_t(project_basis, current.astype(BF)) * (
        1.0 / math.sqrt(leaf_count * current.shape[0])
    )
    column_total = lax.psum(partial_value, "leaf")
    stacked = lax.all_gather(column_total.astype(BF), "top", axis=0, tiled=True)
    weights = dot(caps_rows, stacked).astype(BF)
    return current - dot(update_basis, weights)


def step_by_step(
    right_side, leaf_inverse, left_basis, right_basis, level_caps, top_left, top_right, top_caps
):
    levels = left_basis.shape[0]
    lefts = [left_basis[k, 0] for k in range(levels)]
    rights = [right_basis[k, 0] for k in range(levels)]
    current = dot(leaf_inverse[0], right_side[0].astype(BF))
    for k in range(levels):
        current = level_step(current, rights[k], lefts[k], level_caps[k, 0], k + 1)
    current = top_step(current, top_right[0], top_left[0], top_caps)
    current = top_step(current, top_left[0], top_right[0], top_caps)
    for k in reversed(range(levels)):
        current = level_step(current, lefts[k], rights[k], level_caps[k, 0], k + 1)
    return dot_t(leaf_inverse[0], current.astype(BF))[None]


def in_hbm(value):
    return pltpu.with_memory_space_constraint(value, pltpu.HBM)


def in_vmem(value):
    return pltpu.with_memory_space_constraint(value, pltpu.VMEM)


def call(body, outs, *args, scratch=(), hbm=(), hbm_out=False, micros=1):
    vmem = pl.BlockSpec(memory_space=pltpu.VMEM)
    anywhere = pl.BlockSpec(memory_space=pl.ANY)
    return pl.pallas_call(
        body,
        out_shape=[
            jax.ShapeDtypeStruct(shape, dtype) if hbm_out else pltpu.VMEM(shape, dtype)
            for shape, dtype in outs
        ],
        in_specs=[anywhere if i in hbm else vmem for i in range(len(args))],
        out_specs=[anywhere if hbm_out else vmem] * len(outs),
        scratch_shapes=list(scratch),
        compiler_params=pltpu.CompilerParams(vmem_limit_bytes=VMEM_LIMIT),
        cost_estimate=pl.CostEstimate(
            flops=int(micros * FLOPS_PER_MICRO), bytes_accessed=0, transcendentals=0
        ),
    )(*[in_hbm(a) if i in hbm else in_vmem(a) for i, a in enumerate(args)])


def after(value, *others):
    return lax.optimization_barrier((value, *others))[0]


def tree_side(bit):
    return (lax.axis_index("leaf") >> bit) & 1


def column_side():
    leaf = lax.axis_index("leaf")
    return (leaf ^ (leaf >> 1)) & 1


def block(index, width):
    return pl.ds(pl.multiple_of(index * width, width), width)


def put_rows(scratch, upper, own, other):
    rows = own.shape[0]
    scratch[block(upper, rows), :] = own
    scratch[block(1 - upper, rows), :] = other


def put_columns(out, upper, own, other):
    width = own.shape[1]
    out[:, block(upper, width)] = own
    out[:, block(1 - upper, width)] = other


def two_levels(
    right_side, leaf_inverse, left_basis, right_basis, level_caps, top_left, top_right, top_caps
):
    rows, cols = right_side.shape[1:]
    rank = top_left.shape[2]
    half = cols // 2
    f32 = jnp.float32
    s1 = 1.0 / math.sqrt(rows)
    s2 = 1.0 / math.sqrt(rows * 2)
    st = 1.0 / math.sqrt(rows * 4)
    blocks = rows // rank
    square, wide, tall = (rank, rank), (rank, cols), (rows, cols)

    def span(i, n=1):
        return slice(i * rank, (i + n) * rank)

    def part(i, n=1):
        return slice(i * half, (i + n) * half)

    def start_body(
        rhs_hbm, inv_hbm, lb_hbm, rb_hbm, caps_hbm, tl_hbm, tr_hbm,
        x_ref, send, inv_ref, lb, rb, caps, tl, tr, rhs_v, sems,
    ):
        def load(source, target, *at):
            copy = pltpu.make_async_copy(source, target, sems.at[at])
            copy.start()
            return copy

        copies = []
        for i in range(blocks):
            copies.append(load(rhs_hbm.at[0, span(i), :], rhs_v.at[span(i), :], 0, i))
            copies.append(
                load(
                    inv_hbm.at[0, span(i), span(0, i + 1)],
                    inv_ref.at[span(i), span(0, i + 1)],
                    1,
                    i,
                )
            )
        pairs = ((rb_hbm, rb), (lb_hbm, lb), (tl_hbm, tl), (tr_hbm, tr), (caps_hbm, caps))
        bases = [load(source, target, 2, i) for i, (source, target) in enumerate(pairs)]
        for i in range(blocks):
            copies[2 * i].wait()
            copies[2 * i + 1].wait()
            x_ref[span(i), :] = dot(
                inv_ref[span(i), span(0, i + 1)], rhs_v[span(0, i + 1), :].astype(BF)
            )
        bases[0].wait()
        send[...] = (dot_t(rb[0, 0], x_ref[...].astype(BF)) * s1).astype(BF)
        for copy in bases[1:]:
            copy.wait()

    state0, proj1, inverse, lb, rb, caps, tl, tr = call(
        start_body,
        [(tall, f32), (wide, BF), ((rows, rows), BF)]
        + [(a.shape, a.dtype) for a in (left_basis, right_basis, level_caps, top_left, top_right)],
        right_side,
        leaf_inverse,
        left_basis,
        right_basis,
        level_caps,
        top_left,
        top_right,
        hbm=range(7),
        scratch=[pltpu.VMEM(tall, f32), pltpu.SemaphoreType.DMA((3, max(blocks, 5)))],
    )
    proj1_sib = swap(proj1, "leaf", 1)
    caps_here = after(top_caps, proj1)
    caps_near = swap(caps_here, "top", 1)

    def early_body(lb, caps, tl, tr, seen, out):
        for i, basis in enumerate((tr, tl)):
            gram = (dot_t(basis[0], lb[1, 0]) * st).astype(BF)
            out[:, span(2 * i, 2)] = dot(gram, caps[1, 0]).astype(BF)
        out[:, span(4)] = (dot_t(tl[0], tl[0]) * st).astype(BF)

    (early,) = call(
        early_body, [((rank, 5 * rank), BF)], lb, caps, tl, tr, caps_near, micros=10
    )
    early_sib = swap(early, "leaf", 1)

    def one_body(x0, p, p_sib, lb, rb, caps, tl, tr, x1, send, keep, stack, scratch):
        side = column_side()
        put_rows(stack, tree_side(0), p[...], p_sib[...])
        coef = dot(caps[0, 0], stack[...]).astype(BF)
        x1[...] = x0[...] - dot(lb[0, 0], coef)
        state = x1[...].astype(BF)
        keep[:, :cols] = dot_t(rb[1, 0], state) * s2
        send[:, :cols] = keep[:, :cols].astype(BF)
        for i, basis in enumerate((tr, tl)):
            scratch[...] = dot_t(basis[0], state) * st
            send[:, part(2 + i)] = scratch[:, block(1 - side, half)].astype(BF)
            keep[:, part(2 + i)] = scratch[:, block(side, half)]

    state1, pair_send, pair_keep = call(
        one_body,
        [(tall, f32), ((rank, 2 * cols), BF), ((rank, 2 * cols), f32)],
        state0,
        proj1,
        proj1_sib,
        lb,
        rb,
        caps,
        tl,
        tr,
        scratch=[pltpu.VMEM((2 * rank, cols), BF), pltpu.VMEM(wide, f32)],
        micros=3,
    )
    pair_in = swap(pair_send, "leaf", 1)

    def pair_body(own, sib, seen, send, keep, gram, scratch):
        upper = tree_side(1)
        for i in range(2):
            scratch[...] = (own[:, span(2 * i, 2)].astype(f32) + sib[:, span(2 * i, 2)]).astype(BF)
            send[:, span(i)] = scratch[:, block(1 - upper, rank)]
            keep[:, span(2 * i)] = scratch[:, block(upper, rank)]
            keep[:, span(2 * i + 1)] = send[:, span(i)]
        gram[...] = own[:, span(4)].astype(f32) + sib[:, span(4)]
        send[:, span(2)] = gram[...].astype(BF)

    next_send, next_keep, gram_pair = call(
        pair_body,
        [((rank, 3 * rank), BF), ((rank, 4 * rank), BF), (square, f32)],
        early,
        early_sib,
        state1,
        scratch=[pltpu.VMEM((rank, 2 * rank), BF)],
        micros=0.1,
    )
    next_far = swap(next_send, "leaf", 3)
    def half_body(keep, pair, nexts, send, keep2):
        side = column_side()
        send[:, :cols] = (keep[:, :cols] + pair[:, :cols]).astype(BF)
        own = send[:, block(side, half)]
        for i in range(2):
            keep2[:, part(i)] = (
                keep[:, part(2 + i)] + pair[:, part(2 + i)] - dot(nexts[:, span(2 * i)], own)
            )
        send[:, cols:] = keep2[...].astype(BF)

    cross_send, cross_keep = call(
        half_body,
        [((rank, 2 * cols), BF), (wide, f32)],
        pair_keep,
        pair_in,
        next_keep,
        micros=5,
    )
    cross_in = swap(cross_send, "leaf", 3)

    caps_far = swap(after(top_caps, cross_send), "top", 2)
    caps_far_near = swap(caps_far, "top", 1)

    def order_body(a, b, c, d, out):
        here = lax.axis_index("top")
        for i, piece in enumerate((a, b, c, d)):
            for k in range(4):
                out[span(i), span(k)] = piece[:, block(here ^ k, rank)]

    (caps_all,) = call(
        order_body,
        [((4 * rank, 4 * rank), BF)],
        top_caps,
        caps_near,
        caps_far,
        caps_far_near,
        micros=0.1,
    )

    def late_body(lb, rb, caps, tl, tr, seen, seen2, out):
        for i, basis in enumerate((tl[0], tr[0])):
            out[:, span(i)] = (dot_t(lb[0, 0], basis) * s1).astype(BF)
            out[:, span(5 + i)] = (dot_t(lb[1, 0], basis) * s2).astype(BF)
        out[:, span(2)] = (dot_t(lb[0, 0], rb[1, 0]) * s1).astype(BF)
        out[:, span(3, 2)] = caps[1, 0]

    (late,) = call(
        late_body,
        [((rank, 7 * rank), BF)],
        lb,
        rb,
        caps,
        tl,
        tr,
        cross_send,
        next_far,
        micros=5,
    )
    late_sib = swap(late, "leaf", 1)

    def column_body(send, keep2, far, nexts, nexts_far, gram, seen, out):
        side = column_side()
        own, other = send[:, block(side, half)], far[:, block(side, half)]
        for i in range(2):
            out[:, part(i)] = (
                keep2[:, part(i)]
                + far[:, part(2 + i)]
                - dot(nexts[:, span(2 * i + 1)], other)
                - dot(nexts_far[:, span(i)], own)
            ).astype(BF)
        out[:, 2 * half :] = (gram[...] + nexts_far[:, span(2)]).astype(BF)

    (top_send,) = call(
        column_body,
        [((rank, 2 * half + rank), BF)],
        cross_send,
        cross_keep,
        cross_in,
        next_keep,
        next_far,
        gram_pair,
        late,
        micros=0.2,
    )
    top_far = swap(top_send, "top", 2)

    def two_body(x1, send, far, lb, caps, seen, x2, z5, z, stack):
        put_rows(stack, tree_side(1), send[:, :cols], far[:, :cols])
        coef = dot(caps[1, 0], stack[...]).astype(BF)
        x2[...] = (x1[...] - dot(lb[1, 0], coef)).astype(BF)
        z5[...] = dot_t(lb[1, 0], x2[...]) * s2
        z[:, :cols] = z5[...].astype(BF)
        z[:, cols:] = (dot_t(lb[0, 0], x2[...]) * s1).astype(BF)

    state2, down5, down_send = call(
        two_body,
        [(tall, BF), (wide, f32), ((rank, 2 * cols), BF)],
        state1,
        cross_send,
        cross_in,
        lb,
        caps,
        top_send,
        scratch=[pltpu.VMEM((2 * rank, cols), BF)],
        micros=0.1,
    )
    down_in = swap(down_send, "leaf", 1)
    top_near = swap(after(top_send, state2), "top", 1)
    top_parts = top_send, top_near, top_far, swap(top_far, "top", 1)

    def under_body(x2, rb, tl, tr, inv, seen, out2, under):
        for c in range(blocks):
            column = inv[c * rank :, span(c)]
            out2[span(c), :] = dot_t(column, x2[c * rank :, :])
            for i, basis in enumerate((tl[0], tr[0], rb[1, 0], rb[0, 0])):
                under[span(c), span(i)] = dot_t(column, basis[c * rank :, :]).astype(BF)

    out2, under = call(
        under_body,
        [(tall, f32), ((rows, 4 * rank), BF)],
        state2,
        rb,
        tl,
        tr,
        inverse,
        late_sib,
    )

    def top_body(a, b, c, d, caps, seen, out, up, down):
        pieces = (a, b, c, d)
        for i, piece in enumerate(pieces):
            up[span(i), :] = piece[:, part(0)]
        coef = dot(caps[...], up[...]).astype(BF)
        for i, piece in enumerate(pieces):
            down[span(i), :] = (
                piece[:, part(1)] - dot(piece[:, 2 * half :], coef[span(i), :])
            ).astype(BF)
        out[:, part(0)] = coef[:rank, :]
        out[:, part(1)] = dot(caps[:rank, :], down[...]).astype(BF)

    (back_send,) = call(
        top_body,
        [(wide, BF)],
        *top_parts,
        caps_all,
        out2,
        scratch=[pltpu.VMEM((4 * rank, half), BF)] * 2,
    )
    back_in = swap(back_send, "leaf", 1)

    def down_body(back, back_sib, down5, z_sib, late, late_sib, both, send):
        side = column_side()
        for i in range(2):
            put_columns(both.at[span(i), :], side, back[:, part(i)], back_sib[:, part(i)])
        gram = (late[:, span(5, 2)].astype(f32) + late_sib[:, span(5, 2)]).astype(BF)
        send[...] = (down5[...] + z_sib[:, :cols] - dot(gram, both[...])).astype(BF)

    both, half5 = call(
        down_body,
        [((2 * rank, cols), BF), (wide, BF)],
        back_send,
        back_in,
        down5,
        down_in,
        late,
        late_sib,
        micros=0.3,
    )
    half5_far = swap(half5, "leaf", 3)

    def last_body(
        out2, under, both, half5, half5_far, late, late_sib, z, z_sib, caps, out,
        coefs, stack, out_v, sems,
    ):
        coefs[span(0, 2), :] = both[...]
        put_rows(stack, tree_side(1), half5[...], half5_far[...])
        coef5 = dot(caps[1, 0], stack[...]).astype(BF)
        coef5_sib = dot(late_sib[:, span(3, 2)], stack[...]).astype(BF)
        coefs[span(2), :] = coef5

        def proj(zs, gram, coef):
            return (
                zs[:, cols:]
                - dot(gram[:, span(0, 2)], both[...])
                - dot(gram[:, span(2)], coef)
            ).astype(BF)

        put_rows(stack, tree_side(0), proj(z, late, coef5), proj(z_sib, late_sib, coef5_sib))
        coefs[span(3), :] = dot(caps[0, 0], stack[...]).astype(BF)
        copies = []
        for c in range(blocks):
            out_v[span(c), :] = out2[span(c), :] - dot(under[span(c), :], coefs[...])
            copy = pltpu.make_async_copy(out_v.at[span(c), :], out.at[0, span(c), :], sems.at[c])
            copy.start()
            copies.append(copy)
        for copy in copies:
            copy.wait()

    (out,) = call(
        last_body,
        [((1, rows, cols), f32)],
        out2,
        under,
        both,
        half5,
        half5_far,
        late,
        late_sib,
        down_send,
        down_in,
        caps,
        hbm_out=True,
        scratch=[
            pltpu.VMEM((4 * rank, cols), BF),
            pltpu.VMEM((2 * rank, cols), BF),
            pltpu.VMEM(tall, f32),
            pltpu.SemaphoreType.DMA((blocks,)),
        ],
    )
    return out


def on_device(*args):
    levels = args[2].shape[0]
    sizes = lax.axis_size("leaf"), lax.axis_size("top")
    if levels == 2 and sizes == (4, 4):
        return two_levels(*args)
    return step_by_step(*args)


def solution(mesh):
    rows = P(("parts", "top"), "leaf", None)
    level_rows = P(None, ("parts", "top"), "leaf", None)
    return jax.shard_map(
        on_device,
        mesh=mesh,
        in_specs=(
            rows,
            rows,
            level_rows,
            level_rows,
            level_rows,
            rows,
            rows,
            P(("parts", "top"), None),
        ),
        out_specs=rows,
        check_vma=False,
    )
```

```python
import math

import jax
import jax.numpy as jnp
from jax import lax
from jax.experimental import pallas as pl
from jax.experimental.pallas import tpu as pltpu
from jax.sharding import PartitionSpec as P

BF = jnp.bfloat16
VMEM_LIMIT = 8 * 2**20
FLOPS_PER_MICRO = 1e9


def swap(value, axis, mask):
    pairs = [(source, source ^ mask) for source in range(lax.axis_size(axis))]
    return lax.ppermute(value, axis, pairs)


def dot(a, b):
    return jnp.dot(a, b, preferred_element_type=jnp.float32)


def dot_t(a, b):
    return lax.dot_general(a, b, (((0,), (0,)), ((), ())), preferred_element_type=jnp.float32)


def ordered(upper_side, own, other):
    return jnp.where(
        upper_side, jnp.concatenate([other, own], 0), jnp.concatenate([own, other], 0)
    )


def level_step(current, project_basis, update_basis, caps_rows, level_num):
    leaf_rows = current.shape[0]
    shift_bits = level_num - 1
    partial_value = dot_t(project_basis, current.astype(BF)) * (
        1.0 / math.sqrt(leaf_rows * 2**shift_bits)
    )
    for bit_index in range(shift_bits):
        partial_value = partial_value + swap(partial_value, "leaf", 2**bit_index)
    own = partial_value.astype(BF)
    other = swap(own, "leaf", 2**shift_bits)
    upper_side = (lax.axis_index("leaf") >> shift_bits) & 1 == 1
    stacked = ordered(upper_side, own, other)
    weights = dot(caps_rows, stacked).astype(BF)
    return current - dot(update_basis, weights)


def top_step(current, project_basis, update_basis, caps_rows):
    leaf_count = lax.axis_size("leaf")
    partial_value = dot_t(project_basis, current.astype(BF)) * (
        1.0 / math.sqrt(leaf_count * current.shape[0])
    )
    column_total = lax.psum(partial_value, "leaf")
    stacked = lax.all_gather(column_total.astype(BF), "top", axis=0, tiled=True)
    weights = dot(caps_rows, stacked).astype(BF)
    return current - dot(update_basis, weights)


def step_by_step(
    right_side, leaf_inverse, left_basis, right_basis, level_caps, top_left, top_right, top_caps
):
    levels = left_basis.shape[0]
    lefts = [left_basis[k, 0] for k in range(levels)]
    rights = [right_basis[k, 0] for k in range(levels)]
    current = dot(leaf_inverse[0], right_side[0].astype(BF))
    for k in range(levels):
        current = level_step(current, rights[k], lefts[k], level_caps[k, 0], k + 1)
    current = top_step(current, top_right[0], top_left[0], top_caps)
    current = top_step(current, top_left[0], top_right[0], top_caps)
    for k in reversed(range(levels)):
        current = level_step(current, lefts[k], rights[k], level_caps[k, 0], k + 1)
    return dot_t(leaf_inverse[0], current.astype(BF))[None]


def in_hbm(value):
    return pltpu.with_memory_space_constraint(value, pltpu.HBM)


def in_vmem(value):
    return pltpu.with_memory_space_constraint(value, pltpu.VMEM)


def call(body, outs, *args, scratch=(), hbm=(), hbm_out=False, micros=1):
    vmem = pl.BlockSpec(memory_space=pltpu.VMEM)
    anywhere = pl.BlockSpec(memory_space=pl.ANY)
    return pl.pallas_call(
        body,
        out_shape=[
            jax.ShapeDtypeStruct(shape, dtype) if hbm_out else pltpu.VMEM(shape, dtype)
            for shape, dtype in outs
        ],
        in_specs=[anywhere if i in hbm else vmem for i in range(len(args))],
        out_specs=[anywhere if hbm_out else vmem] * len(outs),
        scratch_shapes=list(scratch),
        compiler_params=pltpu.CompilerParams(vmem_limit_bytes=VMEM_LIMIT),
        cost_estimate=pl.CostEstimate(
            flops=int(micros * FLOPS_PER_MICRO), bytes_accessed=0, transcendentals=0
        ),
    )(*[in_hbm(a) if i in hbm else in_vmem(a) for i, a in enumerate(args)])


def after(value, *others):
    return lax.optimization_barrier((value, *others))[0]


def tree_side(bit):
    return (lax.axis_index("leaf") >> bit) & 1


def column_side():
    leaf = lax.axis_index("leaf")
    return (leaf ^ (leaf >> 1)) & 1


def block(index, width):
    return pl.ds(pl.multiple_of(index * width, width), width)


def put_rows(scratch, upper, own, other):
    rows = own.shape[0]
    scratch[block(upper, rows), :] = own
    scratch[block(1 - upper, rows), :] = other


def put_columns(out, upper, own, other):
    width = own.shape[1]
    out[:, block(upper, width)] = own
    out[:, block(1 - upper, width)] = other


def two_levels(
    right_side, leaf_inverse, left_basis, right_basis, level_caps, top_left, top_right, top_caps
):
    rows, cols = right_side.shape[1:]
    rank = top_left.shape[2]
    half = cols // 2
    f32 = jnp.float32
    s1 = 1.0 / math.sqrt(rows)
    s2 = 1.0 / math.sqrt(rows * 2)
    st = 1.0 / math.sqrt(rows * 4)
    blocks = rows // rank
    square, wide, tall = (rank, rank), (rank, cols), (rows, cols)

    def span(i, n=1):
        return slice(i * rank, (i + n) * rank)

    def part(i, n=1):
        return slice(i * half, (i + n) * half)

    def start_body(
        rhs_hbm, inv_hbm, lb_hbm, rb_hbm, caps_hbm, tl_hbm, tr_hbm,
        x_ref, send, inv_ref, lb, rb, caps, tl, tr, rhs_v, sems,
    ):
        def load(source, target, *at):
            copy = pltpu.make_async_copy(source, target, sems.at[at])
            copy.start()
            return copy

        copies = []
        for i in range(blocks):
            copies.append(load(rhs_hbm.at[0, span(i), :], rhs_v.at[span(i), :], 0, i))
            copies.append(
                load(
                    inv_hbm.at[0, span(i), span(0, i + 1)],
                    inv_ref.at[span(i), span(0, i + 1)],
                    1,
                    i,
                )
            )
        pairs = ((rb_hbm, rb), (lb_hbm, lb), (tl_hbm, tl), (tr_hbm, tr), (caps_hbm, caps))
        bases = [load(source, target, 2, i) for i, (source, target) in enumerate(pairs)]
        for i in range(blocks):
            copies[2 * i].wait()
            copies[2 * i + 1].wait()
            x_ref[span(i), :] = dot(
                inv_ref[span(i), span(0, i + 1)], rhs_v[span(0, i + 1), :].astype(BF)
            )
        bases[0].wait()
        send[...] = (dot_t(rb[0, 0], x_ref[...].astype(BF)) * s1).astype(BF)
        for copy in bases[1:]:
            copy.wait()

    state0, proj1, inverse, lb, rb, caps, tl, tr = call(
        start_body,
        [(tall, f32), (wide, BF), ((rows, rows), BF)]
        + [(a.shape, a.dtype) for a in (left_basis, right_basis, level_caps, top_left, top_right)],
        right_side,
        leaf_inverse,
        left_basis,
        right_basis,
        level_caps,
        top_left,
        top_right,
        hbm=range(7),
        scratch=[pltpu.VMEM(tall, f32), pltpu.SemaphoreType.DMA((3, max(blocks, 5)))],
    )
    proj1_sib = swap(proj1, "leaf", 1)
    caps_here = after(top_caps, proj1)
    caps_near = swap(caps_here, "top", 1)

    def early_body(lb, caps, tl, tr, seen, out):
        for i, basis in enumerate((tr, tl)):
            gram = (dot_t(basis[0], lb[1, 0]) * st).astype(BF)
            out[:, span(2 * i, 2)] = dot(gram, caps[1, 0]).astype(BF)
        out[:, span(4)] = (dot_t(tl[0], tl[0]) * st).astype(BF)

    (early,) = call(
        early_body, [((rank, 5 * rank), BF)], lb, caps, tl, tr, caps_near, micros=10
    )
    early_sib = swap(early, "leaf", 1)

    def one_body(x0, p, p_sib, lb, rb, caps, tl, tr, x1, send, keep, stack, scratch):
        side = column_side()
        put_rows(stack, tree_side(0), p[...], p_sib[...])
        coef = dot(caps[0, 0], stack[...]).astype(BF)
        x1[...] = x0[...] - dot(lb[0, 0], coef)
        state = x1[...].astype(BF)
        keep[:, :cols] = dot_t(rb[1, 0], state) * s2
        send[:, :cols] = keep[:, :cols].astype(BF)
        for i, basis in enumerate((tr, tl)):
            scratch[...] = dot_t(basis[0], state) * st
            send[:, part(2 + i)] = scratch[:, block(1 - side, half)].astype(BF)
            keep[:, part(2 + i)] = scratch[:, block(side, half)]

    state1, pair_send, pair_keep = call(
        one_body,
        [(tall, f32), ((rank, 2 * cols), BF), ((rank, 2 * cols), f32)],
        state0,
        proj1,
        proj1_sib,
        lb,
        rb,
        caps,
        tl,
        tr,
        scratch=[pltpu.VMEM((2 * rank, cols), BF), pltpu.VMEM(wide, f32)],
        micros=3,
    )
    pair_in = swap(pair_send, "leaf", 1)

    def pair_body(own, sib, seen, send, keep, gram, scratch):
        upper = tree_side(1)
        for i in range(2):
            scratch[...] = (own[:, span(2 * i, 2)].astype(f32) + sib[:, span(2 * i, 2)]).astype(BF)
            send[:, span(i)] = scratch[:, block(1 - upper, rank)]
            keep[:, span(2 * i)] = scratch[:, block(upper, rank)]
            keep[:, span(2 * i + 1)] = send[:, span(i)]
        gram[...] = own[:, span(4)].astype(f32) + sib[:, span(4)]
        send[:, span(2)] = gram[...].astype(BF)

    next_send, next_keep, gram_pair = call(
        pair_body,
        [((rank, 3 * rank), BF), ((rank, 4 * rank), BF), (square, f32)],
        early,
        early_sib,
        state1,
        scratch=[pltpu.VMEM((rank, 2 * rank), BF)],
        micros=0.1,
    )
    next_far = swap(next_send, "leaf", 3)
    def half_body(keep, pair, nexts, send, keep2):
        side = column_side()
        send[:, :cols] = (keep[:, :cols] + pair[:, :cols]).astype(BF)
        own = send[:, block(side, half)]
        for i in range(2):
            keep2[:, part(i)] = (
                keep[:, part(2 + i)] + pair[:, part(2 + i)] - dot(nexts[:, span(2 * i)], own)
            )
        send[:, cols:] = keep2[...].astype(BF)

    cross_send, cross_keep = call(
        half_body,
        [((rank, 2 * cols), BF), (wide, f32)],
        pair_keep,
        pair_in,
        next_keep,
        micros=5,
    )
    cross_in = swap(cross_send, "leaf", 3)

    caps_far = swap(after(top_caps, cross_send), "top", 2)
    caps_far_near = swap(caps_far, "top", 1)

    def order_body(a, b, c, d, out):
        here = lax.axis_index("top")
        for i, piece in enumerate((a, b, c, d)):
            for k in range(4):
                out[span(i), span(k)] = piece[:, block(here ^ k, rank)]

    (caps_all,) = call(
        order_body,
        [((4 * rank, 4 * rank), BF)],
        top_caps,
        caps_near,
        caps_far,
        caps_far_near,
        micros=0.1,
    )

    def late_body(lb, rb, caps, tl, tr, seen, seen2, out):
        for i, basis in enumerate((tl[0], tr[0])):
            out[:, span(i)] = (dot_t(lb[0, 0], basis) * s1).astype(BF)
            out[:, span(4 + i)] = (dot_t(lb[1, 0], basis) * s2).astype(BF)
        gram = (dot_t(lb[0, 0], rb[1, 0]) * s1).astype(BF)
        out[:, span(2, 2)] = dot(gram, caps[1, 0]).astype(BF)

    (late,) = call(
        late_body,
        [((rank, 6 * rank), BF)],
        lb,
        rb,
        caps,
        tl,
        tr,
        cross_send,
        next_far,
        micros=5,
    )

    def column_body(send, keep2, far, nexts, nexts_far, gram, seen, out):
        side = column_side()
        own, other = send[:, block(side, half)], far[:, block(side, half)]
        for i in range(2):
            out[:, part(i)] = (
                keep2[:, part(i)]
                + far[:, part(2 + i)]
                - dot(nexts[:, span(2 * i + 1)], other)
                - dot(nexts_far[:, span(i)], own)
            ).astype(BF)
        out[:, 2 * half :] = (gram[...] + nexts_far[:, span(2)]).astype(BF)

    (top_send,) = call(
        column_body,
        [((rank, 2 * half + rank), BF)],
        cross_send,
        cross_keep,
        cross_in,
        next_keep,
        next_far,
        gram_pair,
        late,
        micros=0.2,
    )
    top_far = swap(top_send, "top", 2)

    def two_body(x1, send, far, lb, caps, late, seen, x2, z5, z, stack):
        put_rows(stack, tree_side(1), send[:, :cols], far[:, :cols])
        coef = dot(caps[1, 0], stack[...]).astype(BF)
        x2[...] = (x1[...] - dot(lb[1, 0], coef)).astype(BF)
        z5[...] = dot_t(lb[1, 0], x2[...]) * s2
        z[:, :cols] = z5[...].astype(BF)
        z[:, cols : 2 * cols] = (dot_t(lb[0, 0], x2[...]) * s1).astype(BF)
        z[:, 2 * cols :] = late[...]

    state2, down5, down_send = call(
        two_body,
        [(tall, BF), (wide, f32), ((rank, 2 * cols + 6 * rank), BF)],
        state1,
        cross_send,
        cross_in,
        lb,
        caps,
        late,
        top_send,
        scratch=[pltpu.VMEM((2 * rank, cols), BF)],
        micros=0.1,
    )
    down_in = swap(down_send, "leaf", 1)
    top_near = swap(after(top_send, state2), "top", 1)
    top_parts = top_send, top_near, top_far, swap(top_far, "top", 1)

    def under_body(x2, rb, tl, tr, inv, out2, under):
        for c in range(blocks):
            column = inv[c * rank :, span(c)]
            out2[span(c), :] = dot_t(column, x2[c * rank :, :])
            for i, basis in enumerate((tl[0], tr[0], rb[1, 0], rb[0, 0])):
                under[span(c), span(i)] = dot_t(column, basis[c * rank :, :]).astype(BF)

    out2, under = call(
        under_body,
        [(tall, f32), ((rows, 4 * rank), BF)],
        state2,
        rb,
        tl,
        tr,
        inverse,
    )

    def top_body(a, b, c, d, caps, seen, out, up, down):
        pieces = (a, b, c, d)
        for i, piece in enumerate(pieces):
            up[span(i), :] = piece[:, part(0)]
        coef = dot(caps[...], up[...]).astype(BF)
        for i, piece in enumerate(pieces):
            down[span(i), :] = (
                piece[:, part(1)] - dot(piece[:, 2 * half :], coef[span(i), :])
            ).astype(BF)
        out[:, part(0)] = coef[:rank, :]
        out[:, part(1)] = dot(caps[:rank, :], down[...]).astype(BF)

    (back_send,) = call(
        top_body,
        [(wide, BF)],
        *top_parts,
        caps_all,
        out2,
        scratch=[pltpu.VMEM((4 * rank, half), BF)] * 2,
    )
    back_in = swap(back_send, "leaf", 1)

    def down_body(back, back_sib, down5, z, z_sib, both, send):
        side = column_side()
        for i in range(2):
            put_columns(both.at[span(i), :], side, back[:, part(i)], back_sib[:, part(i)])
        at = slice(2 * cols + 4 * rank, 2 * cols + 6 * rank)
        gram = (z[:, at].astype(f32) + z_sib[:, at]).astype(BF)
        send[...] = (down5[...] + z_sib[:, :cols] - dot(gram, both[...])).astype(BF)

    both, half5 = call(
        down_body,
        [((2 * rank, cols), BF), (wide, BF)],
        back_send,
        back_in,
        down5,
        down_send,
        down_in,
        micros=0.3,
    )
    half5_far = swap(half5, "leaf", 3)

    def part_body(out2, under, both, z, z_sib, seen, proj, out3):
        def down(zs):
            return zs[:, cols : 2 * cols] - dot(zs[:, 2 * cols : 2 * cols + 2 * rank], both[...])

        put_rows(proj, tree_side(0), down(z), down(z_sib))
        out3[...] = out2[...] - dot(under[:, span(0, 2)], both[...])

    proj6, out3 = call(
        part_body,
        [((2 * rank, cols), f32), (tall, f32)],
        out2,
        under,
        both,
        down_send,
        down_in,
        half5,
        micros=0.3,
    )

    def last_body(
        out3, under, half5, half5_far, z, z_sib, proj6, caps, out,
        coefs, stack, grams, out_v, sems,
    ):
        put_rows(stack, tree_side(1), half5[...], half5_far[...])
        at = slice(2 * cols + 2 * rank, 2 * cols + 4 * rank)
        put_rows(grams, tree_side(0), z[:, at], z_sib[:, at])
        proj = (proj6[...] - dot(grams[...], stack[...])).astype(BF)
        coefs[span(0), :] = dot(caps[1, 0], stack[...]).astype(BF)
        coefs[span(1), :] = dot(caps[0, 0], proj).astype(BF)
        copies = []
        for c in range(blocks):
            out_v[span(c), :] = out3[span(c), :] - dot(under[span(c), span(2, 2)], coefs[...])
            copy = pltpu.make_async_copy(out_v.at[span(c), :], out.at[0, span(c), :], sems.at[c])
            copy.start()
            copies.append(copy)
        for copy in copies:
            copy.wait()

    (out,) = call(
        last_body,
        [((1, rows, cols), f32)],
        out3,
        under,
        half5,
        half5_far,
        down_send,
        down_in,
        proj6,
        caps,
        hbm_out=True,
        scratch=[
            pltpu.VMEM((2 * rank, cols), BF),
            pltpu.VMEM((2 * rank, cols), BF),
            pltpu.VMEM((2 * rank, 2 * rank), BF),
            pltpu.VMEM(tall, f32),
            pltpu.SemaphoreType.DMA((blocks,)),
        ],
    )
    return out


def on_device(*args):
    levels = args[2].shape[0]
    sizes = lax.axis_size("leaf"), lax.axis_size("top")
    if levels == 2 and sizes == (4, 4):
        return two_levels(*args)
    return step_by_step(*args)


def solution(mesh):
    rows = P(("parts", "top"), "leaf", None)
    level_rows = P(None, ("parts", "top"), "leaf", None)
    return jax.shard_map(
        on_device,
        mesh=mesh,
        in_specs=(
            rows,
            rows,
            level_rows,
            level_rows,
            level_rows,
            rows,
            rows,
            P(("parts", "top"), None),
        ),
        out_specs=rows,
        check_vma=False,
    )
```

```python
import math

import jax
import jax.numpy as jnp
from jax import lax
from jax.experimental import pallas as pl
from jax.experimental.pallas import tpu as pltpu
from jax.sharding import PartitionSpec as P

BF = jnp.bfloat16
VMEM_LIMIT = 8 * 2**20
FLOPS_PER_MICRO = 1e9


def swap(value, axis, mask):
    pairs = [(source, source ^ mask) for source in range(lax.axis_size(axis))]
    return lax.ppermute(value, axis, pairs)


def dot(a, b):
    return jnp.dot(a, b, preferred_element_type=jnp.float32)


def dot_t(a, b):
    return lax.dot_general(a, b, (((0,), (0,)), ((), ())), preferred_element_type=jnp.float32)


def ordered(upper_side, own, other):
    return jnp.where(
        upper_side, jnp.concatenate([other, own], 0), jnp.concatenate([own, other], 0)
    )


def level_step(current, project_basis, update_basis, caps_rows, level_num):
    leaf_rows = current.shape[0]
    shift_bits = level_num - 1
    partial_value = dot_t(project_basis, current.astype(BF)) * (
        1.0 / math.sqrt(leaf_rows * 2**shift_bits)
    )
    for bit_index in range(shift_bits):
        partial_value = partial_value + swap(partial_value, "leaf", 2**bit_index)
    own = partial_value.astype(BF)
    other = swap(own, "leaf", 2**shift_bits)
    upper_side = (lax.axis_index("leaf") >> shift_bits) & 1 == 1
    stacked = ordered(upper_side, own, other)
    weights = dot(caps_rows, stacked).astype(BF)
    return current - dot(update_basis, weights)


def top_step(current, project_basis, update_basis, caps_rows):
    leaf_count = lax.axis_size("leaf")
    partial_value = dot_t(project_basis, current.astype(BF)) * (
        1.0 / math.sqrt(leaf_count * current.shape[0])
    )
    column_total = lax.psum(partial_value, "leaf")
    stacked = lax.all_gather(column_total.astype(BF), "top", axis=0, tiled=True)
    weights = dot(caps_rows, stacked).astype(BF)
    return current - dot(update_basis, weights)


def step_by_step(
    right_side, leaf_inverse, left_basis, right_basis, level_caps, top_left, top_right, top_caps
):
    levels = left_basis.shape[0]
    lefts = [left_basis[k, 0] for k in range(levels)]
    rights = [right_basis[k, 0] for k in range(levels)]
    current = dot(leaf_inverse[0], right_side[0].astype(BF))
    for k in range(levels):
        current = level_step(current, rights[k], lefts[k], level_caps[k, 0], k + 1)
    current = top_step(current, top_right[0], top_left[0], top_caps)
    current = top_step(current, top_left[0], top_right[0], top_caps)
    for k in reversed(range(levels)):
        current = level_step(current, lefts[k], rights[k], level_caps[k, 0], k + 1)
    return dot_t(leaf_inverse[0], current.astype(BF))[None]


def in_hbm(value):
    return pltpu.with_memory_space_constraint(value, pltpu.HBM)


def in_vmem(value):
    return pltpu.with_memory_space_constraint(value, pltpu.VMEM)


def call(body, outs, *args, scratch=(), hbm=(), hbm_out=False, micros=1):
    vmem = pl.BlockSpec(memory_space=pltpu.VMEM)
    anywhere = pl.BlockSpec(memory_space=pl.ANY)
    return pl.pallas_call(
        body,
        out_shape=[
            jax.ShapeDtypeStruct(shape, dtype) if hbm_out else pltpu.VMEM(shape, dtype)
            for shape, dtype in outs
        ],
        in_specs=[anywhere if i in hbm else vmem for i in range(len(args))],
        out_specs=[anywhere if hbm_out else vmem] * len(outs),
        scratch_shapes=list(scratch),
        compiler_params=pltpu.CompilerParams(vmem_limit_bytes=VMEM_LIMIT),
        cost_estimate=pl.CostEstimate(
            flops=int(micros * FLOPS_PER_MICRO), bytes_accessed=0, transcendentals=0
        ),
    )(*[in_hbm(a) if i in hbm else in_vmem(a) for i, a in enumerate(args)])


def after(value, *others):
    return lax.optimization_barrier((value, *others))[0]


def tree_side(bit):
    return (lax.axis_index("leaf") >> bit) & 1


def column_side():
    leaf = lax.axis_index("leaf")
    return (leaf ^ (leaf >> 1)) & 1


def block(index, width):
    return pl.ds(pl.multiple_of(index * width, width), width)


def put_rows(scratch, upper, own, other):
    rows = own.shape[0]
    scratch[block(upper, rows), :] = own
    scratch[block(1 - upper, rows), :] = other


def two_levels(
    right_side, leaf_inverse, left_basis, right_basis, level_caps, top_left, top_right, top_caps
):
    rows, cols = right_side.shape[1:]
    rank = top_left.shape[2]
    f32 = jnp.float32
    s1 = 1.0 / math.sqrt(rows)
    s2 = 1.0 / math.sqrt(rows * 2)
    st = 1.0 / math.sqrt(rows * 4)
    blocks = rows // rank
    square, wide, tall = (rank, rank), (rank, cols), (rows, cols)

    def span(i, n=1):
        return slice(i * rank, (i + n) * rank)

    def start_body(
        rhs_hbm, inv_hbm, lb_hbm, rb_hbm, caps_hbm, tl_hbm, tr_hbm,
        x_ref, send, inv_ref, lb, rb, caps, tl, tr, rhs_v, sems,
    ):
        def load(source, target, *at):
            copy = pltpu.make_async_copy(source, target, sems.at[at])
            copy.start()
            return copy

        copies = []
        for i in range(blocks):
            copies.append(load(rhs_hbm.at[0, span(i), :], rhs_v.at[span(i), :], 0, i))
            copies.append(
                load(
                    inv_hbm.at[0, span(i), span(0, i + 1)],
                    inv_ref.at[span(i), span(0, i + 1)],
                    1,
                    i,
                )
            )
        pairs = ((rb_hbm, rb), (lb_hbm, lb), (tl_hbm, tl), (tr_hbm, tr), (caps_hbm, caps))
        bases = [load(source, target, 2, i) for i, (source, target) in enumerate(pairs)]
        for i in range(blocks):
            copies[2 * i].wait()
            copies[2 * i + 1].wait()
            x_ref[span(i), :] = dot(
                inv_ref[span(i), span(0, i + 1)], rhs_v[span(0, i + 1), :].astype(BF)
            )
        bases[0].wait()
        send[...] = (dot_t(rb[0, 0], x_ref[...].astype(BF)) * s1).astype(BF)
        for copy in bases[1:]:
            copy.wait()

    state0, proj1, inverse, lb, rb, caps, tl, tr = call(
        start_body,
        [(tall, f32), (wide, BF), ((rows, rows), BF)]
        + [(a.shape, a.dtype) for a in (left_basis, right_basis, level_caps, top_left, top_right)],
        right_side,
        leaf_inverse,
        left_basis,
        right_basis,
        level_caps,
        top_left,
        top_right,
        hbm=range(7),
        scratch=[pltpu.VMEM(tall, f32), pltpu.SemaphoreType.DMA((3, max(blocks, 5)))],
    )
    proj1_sib = swap(proj1, "leaf", 1)
    caps_here = after(top_caps, proj1)
    caps_near = swap(caps_here, "top", 1)

    def early_body(lb, caps, tl, tr, seen, send, keep, scratch):
        side = column_side()
        for i, basis in enumerate((tr, tl)):
            gram = (dot_t(basis[0], lb[1, 0]) * st).astype(BF)
            scratch[i] = dot(gram, caps[1, 0]).astype(BF)
        send[:, : 2 * rank] = scratch[1 - side]
        send[:, span(2)] = (dot_t(tl[0], tl[0]) * st).astype(BF)
        keep[...] = scratch[side]

    early, early_keep = call(
        early_body,
        [((rank, 3 * rank), BF), ((rank, 2 * rank), BF)],
        lb,
        caps,
        tl,
        tr,
        caps_near,
        scratch=[pltpu.VMEM((2, rank, 2 * rank), BF)],
        micros=10,
    )
    early_sib = swap(early, "leaf", 1)

    def one_body(x0, p, p_sib, lb, rb, caps, tl, tr, seen, x1, send, keep, stack, scratch):
        side = column_side()
        put_rows(stack, tree_side(0), p[...], p_sib[...])
        coef = dot(caps[0, 0], stack[...]).astype(BF)
        x1[...] = x0[...] - dot(lb[0, 0], coef)
        state = x1[...].astype(BF)
        keep[:, :cols] = dot_t(rb[1, 0], state) * s2
        send[:, :cols] = keep[:, :cols].astype(BF)
        for i, basis in enumerate((tr, tl)):
            scratch[i] = dot_t(basis[0], state) * st
        send[:, cols:] = scratch[1 - side].astype(BF)
        keep[:, cols:] = scratch[side]

    state1, pair_send, pair_keep = call(
        one_body,
        [(tall, f32), ((rank, 2 * cols), BF), ((rank, 2 * cols), f32)],
        state0,
        proj1,
        proj1_sib,
        lb,
        rb,
        caps,
        tl,
        tr,
        early,
        scratch=[pltpu.VMEM((2 * rank, cols), BF), pltpu.VMEM((2, rank, cols), f32)],
        micros=3,
    )
    pair_in = swap(pair_send, "leaf", 1)

    def pair_body(mine, own, sib, seen, send, keep, gram, scratch):
        upper = tree_side(1)
        scratch[...] = (mine[...].astype(f32) + sib[:, : 2 * rank]).astype(BF)
        keep[:, span(0)] = scratch[:, block(upper, rank)]
        keep[:, span(1)] = scratch[:, block(1 - upper, rank)]
        send[:, span(0)] = keep[:, span(1)]
        gram[...] = own[:, span(2)].astype(f32) + sib[:, span(2)]
        send[:, span(1)] = gram[...].astype(BF)

    next_send, next_keep, gram_pair = call(
        pair_body,
        [((rank, 2 * rank), BF), ((rank, 2 * rank), BF), (square, f32)],
        early_keep,
        early,
        early_sib,
        state1,
        scratch=[pltpu.VMEM((rank, 2 * rank), BF)],
        micros=1,
    )
    next_far = swap(next_send, "leaf", 3)
    def half_body(keep, pair, nexts, send, keep2):
        send[:, :cols] = (keep[:, :cols] + pair[:, :cols]).astype(BF)
        keep2[...] = keep[:, cols:] + pair[:, cols:] - dot(nexts[:, span(0)], send[:, :cols])
        send[:, cols:] = keep2[...].astype(BF)

    cross_send, cross_keep = call(
        half_body,
        [((rank, 2 * cols), BF), (wide, f32)],
        pair_keep,
        pair_in,
        next_keep,
        micros=5,
    )
    cross_in = swap(cross_send, "leaf", 3)

    caps_far = swap(after(top_caps, cross_send), "top", 2)
    caps_far_near = swap(caps_far, "top", 1)

    def order_body(a, b, c, d, out):
        here = lax.axis_index("top")
        for i, piece in enumerate((a, b, c, d)):
            for k in range(4):
                out[span(i), span(k)] = piece[:, block(here ^ k, rank)]

    (caps_all,) = call(
        order_body,
        [((4 * rank, 4 * rank), BF)],
        top_caps,
        caps_near,
        caps_far,
        caps_far_near,
        micros=0.1,
    )

    def late_body(lb, rb, caps, tl, tr, seen, seen2, out):
        for i, basis in enumerate((tl[0], tr[0])):
            out[:, span(i)] = (dot_t(lb[0, 0], basis) * s1).astype(BF)
            out[:, span(4 + i)] = (dot_t(lb[1, 0], basis) * s2).astype(BF)
        gram = (dot_t(lb[0, 0], rb[1, 0]) * s1).astype(BF)
        out[:, span(2, 2)] = dot(gram, caps[1, 0]).astype(BF)

    (late,) = call(
        late_body,
        [((rank, 6 * rank), BF)],
        lb,
        rb,
        caps,
        tl,
        tr,
        cross_send,
        next_far,
        micros=5,
    )

    late_sib = swap(late, "leaf", 1)

    def column_body(send, keep2, far, nexts, nexts_far, gram, seen, out):
        out[:, :cols] = (
            keep2[...]
            + far[:, cols:]
            - dot(nexts[:, span(1)], far[:, :cols])
            - dot(nexts_far[:, span(0)], send[:, :cols])
        ).astype(BF)
        out[:, cols:] = (gram[...] + nexts_far[:, span(1)]).astype(BF)

    (top_send,) = call(
        column_body,
        [((rank, cols + rank), BF)],
        cross_send,
        cross_keep,
        cross_in,
        next_keep,
        next_far,
        gram_pair,
        late,
        micros=0.2,
    )
    top_far = swap(top_send, "top", 2)

    def two_body(x1, send, far, lb, caps, seen, x2, z5, z, stack):
        put_rows(stack, tree_side(1), send[:, :cols], far[:, :cols])
        coef = dot(caps[1, 0], stack[...]).astype(BF)
        x2[...] = (x1[...] - dot(lb[1, 0], coef)).astype(BF)
        z5[...] = dot_t(lb[1, 0], x2[...]) * s2
        z[:, :cols] = z5[...].astype(BF)
        z[:, cols:] = (dot_t(lb[0, 0], x2[...]) * s1).astype(BF)

    state2, down5, down_send = call(
        two_body,
        [(tall, BF), (wide, f32), ((rank, 2 * cols), BF)],
        state1,
        cross_send,
        cross_in,
        lb,
        caps,
        top_send,
        scratch=[pltpu.VMEM((2 * rank, cols), BF)],
        micros=0.1,
    )
    down_in = swap(down_send, "leaf", 1)
    top_near = swap(after(top_send, state2), "top", 1)
    top_parts = top_send, top_near, top_far, swap(top_far, "top", 1)

    def under_body(x2, rb, tl, tr, inv, seen, out2, under):
        for c in range(blocks):
            column = inv[c * rank :, span(c)]
            out2[span(c), :] = dot_t(column, x2[c * rank :, :])
            for i, basis in enumerate((tl[0], tr[0], rb[1, 0], rb[0, 0])):
                under[span(c), span(i)] = dot_t(column, basis[c * rank :, :]).astype(BF)

    out2, under = call(
        under_body,
        [(tall, f32), ((rows, 4 * rank), BF)],
        state2,
        rb,
        tl,
        tr,
        inverse,
        late_sib,
    )

    def top_body(a, b, c, d, caps, seen, out, up, down):
        pieces = (a, b, c, d)
        for i, piece in enumerate(pieces):
            up[span(i), :] = piece[:, :cols]
        coef = dot(caps[...], up[...]).astype(BF)
        for i, piece in enumerate(pieces):
            down[span(i), :] = dot(piece[:, cols:], coef[span(i), :]).astype(BF)
        out[:, :cols] = coef[:rank, :]
        out[:, cols:] = dot(caps[:rank, :], down[...]).astype(BF)

    (back_send,) = call(
        top_body,
        [((rank, 2 * cols), BF)],
        *top_parts,
        caps_all,
        out2,
        scratch=[pltpu.VMEM((4 * rank, cols), BF)] * 2,
    )
    back_in = swap(back_send, "leaf", 1)

    def down_body(back, back_sib, down5, z_sib, late, late_sib, both, send, pieces):
        side = column_side()
        pieces[side] = back[...]
        pieces[1 - side] = back_sib[...]
        both[span(0), :] = pieces[0, :, :cols]
        both[span(1), :] = (pieces[1, :, :cols].astype(f32) - pieces[0, :, cols:]).astype(BF)
        gram = (late[:, span(4, 2)].astype(f32) + late_sib[:, span(4, 2)]).astype(BF)
        send[...] = (down5[...] + z_sib[:, :cols] - dot(gram, both[...])).astype(BF)

    both, half5 = call(
        down_body,
        [((2 * rank, cols), BF), (wide, BF)],
        back_send,
        back_in,
        down5,
        down_in,
        late,
        late_sib,
        scratch=[pltpu.VMEM((2, rank, 2 * cols), BF)],
        micros=0.3,
    )
    half5_far = swap(half5, "leaf", 3)

    def part_body(out2, under, both, z, z_sib, late, late_sib, seen, proj, out3):
        def down(zs, gram):
            return zs[:, cols:] - dot(gram[:, span(0, 2)], both[...])

        put_rows(proj, tree_side(0), down(z, late), down(z_sib, late_sib))
        out3[...] = out2[...] - dot(under[:, span(0, 2)], both[...])

    proj6, out3 = call(
        part_body,
        [((2 * rank, cols), f32), (tall, f32)],
        out2,
        under,
        both,
        down_send,
        down_in,
        late,
        late_sib,
        half5,
        micros=0.3,
    )

    def last_body(
        out3, under, half5, half5_far, late, late_sib, proj6, caps, out,
        coefs, stack, grams, out_v, sems,
    ):
        put_rows(stack, tree_side(1), half5[...], half5_far[...])
        put_rows(grams, tree_side(0), late[:, span(2, 2)], late_sib[:, span(2, 2)])
        proj = (proj6[...] - dot(grams[...], stack[...])).astype(BF)
        coefs[span(0), :] = dot(caps[1, 0], stack[...]).astype(BF)
        coefs[span(1), :] = dot(caps[0, 0], proj).astype(BF)
        copies = []
        for c in range(blocks):
            out_v[span(c), :] = out3[span(c), :] - dot(under[span(c), span(2, 2)], coefs[...])
            copy = pltpu.make_async_copy(out_v.at[span(c), :], out.at[0, span(c), :], sems.at[c])
            copy.start()
            copies.append(copy)
        for copy in copies:
            copy.wait()

    (out,) = call(
        last_body,
        [((1, rows, cols), f32)],
        out3,
        under,
        half5,
        half5_far,
        late,
        late_sib,
        proj6,
        caps,
        hbm_out=True,
        scratch=[
            pltpu.VMEM((2 * rank, cols), BF),
            pltpu.VMEM((2 * rank, cols), BF),
            pltpu.VMEM((2 * rank, 2 * rank), BF),
            pltpu.VMEM(tall, f32),
            pltpu.SemaphoreType.DMA((blocks,)),
        ],
    )
    return out


def on_device(*args):
    levels = args[2].shape[0]
    sizes = lax.axis_size("leaf"), lax.axis_size("top")
    if levels == 2 and sizes == (4, 4):
        return two_levels(*args)
    return step_by_step(*args)


def solution(mesh):
    rows = P(("parts", "top"), "leaf", None)
    level_rows = P(None, ("parts", "top"), "leaf", None)
    return jax.shard_map(
        on_device,
        mesh=mesh,
        in_specs=(
            rows,
            rows,
            level_rows,
            level_rows,
            level_rows,
            rows,
            rows,
            P(("parts", "top"), None),
        ),
        out_specs=rows,
        check_vma=False,
    )
```

```python
import math

import jax
import jax.numpy as jnp
from jax import lax
from jax.experimental import pallas as pl
from jax.experimental.pallas import tpu as pltpu
from jax.sharding import PartitionSpec as P

BF = jnp.bfloat16
VMEM_LIMIT = 8 * 2**20
FLOPS_PER_MICRO = 1e9


def swap(value, axis, mask):
    pairs = [(source, source ^ mask) for source in range(lax.axis_size(axis))]
    return lax.ppermute(value, axis, pairs)


def dot(a, b):
    return jnp.dot(a, b, preferred_element_type=jnp.float32)


def dot_t(a, b):
    return lax.dot_general(a, b, (((0,), (0,)), ((), ())), preferred_element_type=jnp.float32)


def ordered(upper_side, own, other):
    return jnp.where(
        upper_side, jnp.concatenate([other, own], 0), jnp.concatenate([own, other], 0)
    )


def level_step(current, project_basis, update_basis, caps_rows, level_num):
    leaf_rows = current.shape[0]
    shift_bits = level_num - 1
    partial_value = dot_t(project_basis, current.astype(BF)) * (
        1.0 / math.sqrt(leaf_rows * 2**shift_bits)
    )
    for bit_index in range(shift_bits):
        partial_value = partial_value + swap(partial_value, "leaf", 2**bit_index)
    own = partial_value.astype(BF)
    other = swap(own, "leaf", 2**shift_bits)
    upper_side = (lax.axis_index("leaf") >> shift_bits) & 1 == 1
    stacked = ordered(upper_side, own, other)
    weights = dot(caps_rows, stacked).astype(BF)
    return current - dot(update_basis, weights)


def top_step(current, project_basis, update_basis, caps_rows):
    leaf_count = lax.axis_size("leaf")
    partial_value = dot_t(project_basis, current.astype(BF)) * (
        1.0 / math.sqrt(leaf_count * current.shape[0])
    )
    column_total = lax.psum(partial_value, "leaf")
    stacked = lax.all_gather(column_total.astype(BF), "top", axis=0, tiled=True)
    weights = dot(caps_rows, stacked).astype(BF)
    return current - dot(update_basis, weights)


def step_by_step(
    right_side, leaf_inverse, left_basis, right_basis, level_caps, top_left, top_right, top_caps
):
    levels = left_basis.shape[0]
    lefts = [left_basis[k, 0] for k in range(levels)]
    rights = [right_basis[k, 0] for k in range(levels)]
    current = dot(leaf_inverse[0], right_side[0].astype(BF))
    for k in range(levels):
        current = level_step(current, rights[k], lefts[k], level_caps[k, 0], k + 1)
    current = top_step(current, top_right[0], top_left[0], top_caps)
    current = top_step(current, top_left[0], top_right[0], top_caps)
    for k in reversed(range(levels)):
        current = level_step(current, lefts[k], rights[k], level_caps[k, 0], k + 1)
    return dot_t(leaf_inverse[0], current.astype(BF))[None]


def in_hbm(value):
    return pltpu.with_memory_space_constraint(value, pltpu.HBM)


def in_vmem(value):
    return pltpu.with_memory_space_constraint(value, pltpu.VMEM)


def call(body, outs, *args, scratch=(), hbm=(), hbm_out=False, micros=1):
    vmem = pl.BlockSpec(memory_space=pltpu.VMEM)
    anywhere = pl.BlockSpec(memory_space=pl.ANY)
    return pl.pallas_call(
        body,
        out_shape=[
            jax.ShapeDtypeStruct(shape, dtype) if hbm_out else pltpu.VMEM(shape, dtype)
            for shape, dtype in outs
        ],
        in_specs=[anywhere if i in hbm else vmem for i in range(len(args))],
        out_specs=[anywhere if hbm_out else vmem] * len(outs),
        scratch_shapes=list(scratch),
        compiler_params=pltpu.CompilerParams(vmem_limit_bytes=VMEM_LIMIT),
        cost_estimate=pl.CostEstimate(
            flops=int(micros * FLOPS_PER_MICRO), bytes_accessed=0, transcendentals=0
        ),
    )(*[in_hbm(a) if i in hbm else in_vmem(a) for i, a in enumerate(args)])


def after(value, *others):
    return lax.optimization_barrier((value, *others))[0]


def tree_side(bit):
    return (lax.axis_index("leaf") >> bit) & 1


def column_side():
    leaf = lax.axis_index("leaf")
    return (leaf ^ (leaf >> 1)) & 1


def block(index, width):
    return pl.ds(pl.multiple_of(index * width, width), width)


def put_rows(scratch, upper, own, other):
    rows = own.shape[0]
    scratch[block(upper, rows), :] = own
    scratch[block(1 - upper, rows), :] = other


def two_levels(
    right_side, leaf_inverse, left_basis, right_basis, level_caps, top_left, top_right, top_caps
):
    rows, cols = right_side.shape[1:]
    rank = top_left.shape[2]
    f32 = jnp.float32
    s1 = 1.0 / math.sqrt(rows)
    s2 = 1.0 / math.sqrt(rows * 2)
    st = 1.0 / math.sqrt(rows * 4)
    blocks = rows // rank
    square, wide, tall = (rank, rank), (rank, cols), (rows, cols)

    def span(i, n=1):
        return slice(i * rank, (i + n) * rank)

    def start_body(
        rhs_hbm, inv_hbm, lb_hbm, rb_hbm, caps_hbm, tl_hbm, tr_hbm,
        x_ref, send, inv_ref, lb, rb, caps, tl, tr, rhs_v, sems,
    ):
        def load(source, target, *at):
            copy = pltpu.make_async_copy(source, target, sems.at[at])
            copy.start()
            return copy

        copies = []
        for i in range(blocks):
            copies.append(load(rhs_hbm.at[0, span(i), :], rhs_v.at[span(i), :], 0, i))
            copies.append(
                load(
                    inv_hbm.at[0, span(i), span(0, i + 1)],
                    inv_ref.at[span(i), span(0, i + 1)],
                    1,
                    i,
                )
            )
        pairs = ((rb_hbm, rb), (lb_hbm, lb), (tl_hbm, tl), (tr_hbm, tr), (caps_hbm, caps))
        bases = [load(source, target, 2, i) for i, (source, target) in enumerate(pairs)]
        for i in range(blocks):
            copies[2 * i].wait()
            copies[2 * i + 1].wait()
            x_ref[span(i), :] = dot(
                inv_ref[span(i), span(0, i + 1)], rhs_v[span(0, i + 1), :].astype(BF)
            )
        bases[0].wait()
        send[...] = (dot_t(rb[0, 0], x_ref[...].astype(BF)) * s1).astype(BF)
        for copy in bases[1:]:
            copy.wait()

    state0, proj1, inverse, lb, rb, caps, tl, tr = call(
        start_body,
        [(tall, f32), (wide, BF), ((rows, rows), BF)]
        + [(a.shape, a.dtype) for a in (left_basis, right_basis, level_caps, top_left, top_right)],
        right_side,
        leaf_inverse,
        left_basis,
        right_basis,
        level_caps,
        top_left,
        top_right,
        hbm=range(7),
        scratch=[pltpu.VMEM(tall, f32), pltpu.SemaphoreType.DMA((3, max(blocks, 5)))],
    )
    proj1_sib = swap(proj1, "leaf", 1)
    proj1_near = swap(proj1, "top", 1)

    def early_body(lb, caps, tl, tr, seen, send, keep, scratch):
        side = column_side()
        for i, basis in enumerate((tr, tl)):
            gram = (dot_t(basis[0], lb[1, 0]) * st).astype(BF)
            scratch[i] = dot(gram, caps[1, 0]).astype(BF)
        send[:, : 2 * rank] = scratch[1 - side]
        send[:, span(2)] = (dot_t(tl[0], tl[0]) * st).astype(BF)
        keep[...] = scratch[side]

    early, early_keep = call(
        early_body,
        [((rank, 3 * rank), BF), ((rank, 2 * rank), BF)],
        lb,
        caps,
        tl,
        tr,
        proj1_near,
        scratch=[pltpu.VMEM((2, rank, 2 * rank), BF)],
        micros=10,
    )
    early_sib = swap(early, "leaf", 1)

    def one_body(x0, p, p_sib, lb, rb, caps, tl, tr, seen, x1, send, keep, stack, scratch):
        side = column_side()
        put_rows(stack, tree_side(0), p[...], p_sib[...])
        coef = dot(caps[0, 0], stack[...]).astype(BF)
        x1[...] = x0[...] - dot(lb[0, 0], coef)
        state = x1[...].astype(BF)
        keep[:, :cols] = dot_t(rb[1, 0], state) * s2
        send[:, :cols] = keep[:, :cols].astype(BF)
        for i, basis in enumerate((tr, tl)):
            scratch[i] = dot_t(basis[0], state) * st
        send[:, cols:] = scratch[1 - side].astype(BF)
        keep[:, cols:] = scratch[side]

    state1, pair_send, pair_keep = call(
        one_body,
        [(tall, f32), ((rank, 2 * cols), BF), ((rank, 2 * cols), f32)],
        state0,
        proj1,
        proj1_sib,
        lb,
        rb,
        caps,
        tl,
        tr,
        early,
        scratch=[pltpu.VMEM((2 * rank, cols), BF), pltpu.VMEM((2, rank, cols), f32)],
        micros=3,
    )
    pair_in = swap(pair_send, "leaf", 1)

    def pair_body(mine, own, sib, seen, send, keep, gram, scratch):
        upper = tree_side(1)
        scratch[...] = (mine[...].astype(f32) + sib[:, : 2 * rank]).astype(BF)
        keep[:, span(0)] = scratch[:, block(upper, rank)]
        keep[:, span(1)] = scratch[:, block(1 - upper, rank)]
        send[:, span(0)] = keep[:, span(1)]
        gram[...] = own[:, span(2)].astype(f32) + sib[:, span(2)]
        send[:, span(1)] = gram[...].astype(BF)

    next_send, next_keep, gram_pair = call(
        pair_body,
        [((rank, 2 * rank), BF), ((rank, 2 * rank), BF), (square, f32)],
        early_keep,
        early,
        early_sib,
        state1,
        scratch=[pltpu.VMEM((rank, 2 * rank), BF)],
        micros=1,
    )
    next_far = swap(next_send, "leaf", 3)
    def half_body(keep, pair, nexts, send, keep2):
        send[:, :cols] = (keep[:, :cols] + pair[:, :cols]).astype(BF)
        keep2[...] = keep[:, cols:] + pair[:, cols:] - dot(nexts[:, span(0)], send[:, :cols])
        send[:, cols:] = keep2[...].astype(BF)

    cross_send, cross_keep = call(
        half_body,
        [((rank, 2 * cols), BF), (wide, f32)],
        pair_keep,
        pair_in,
        next_keep,
        micros=5,
    )
    cross_in = swap(cross_send, "leaf", 3)

    def turn_body(gram, far, caps, seen, out):
        whole = (gram[...] + far[:, span(1)]).astype(BF)
        out[...] = dot(whole, caps[...]).astype(BF)

    (turn,) = call(
        turn_body, [(top_caps.shape, BF)], gram_pair, next_far, top_caps, cross_send, micros=0.1
    )
    turn_far = swap(turn, "top", 2)
    turn_near = swap(turn, "top", 1)
    def late_body(lb, rb, caps, tl, tr, seen, seen2, out):
        for i, basis in enumerate((tl[0], tr[0])):
            out[:, span(i)] = (dot_t(lb[0, 0], basis) * s1).astype(BF)
            out[:, span(4 + i)] = (dot_t(lb[1, 0], basis) * s2).astype(BF)
        gram = (dot_t(lb[0, 0], rb[1, 0]) * s1).astype(BF)
        out[:, span(2, 2)] = dot(gram, caps[1, 0]).astype(BF)

    (late,) = call(
        late_body,
        [((rank, 6 * rank), BF)],
        lb,
        rb,
        caps,
        tl,
        tr,
        cross_send,
        next_far,
        micros=5,
    )

    late_sib = swap(late, "leaf", 1)

    def column_body(send, keep2, far, nexts, nexts_far, seen, out):
        out[...] = (
            keep2[...]
            + far[:, cols:]
            - dot(nexts[:, span(1)], far[:, :cols])
            - dot(nexts_far[:, span(0)], send[:, :cols])
        ).astype(BF)

    (top_send,) = call(
        column_body,
        [(wide, BF)],
        cross_send,
        cross_keep,
        cross_in,
        next_keep,
        next_far,
        late,
        micros=0.2,
    )
    top_far = swap(top_send, "top", 2)

    def two_body(x1, send, far, lb, caps, seen, x2, z5, z, stack):
        put_rows(stack, tree_side(1), send[:, :cols], far[:, :cols])
        coef = dot(caps[1, 0], stack[...]).astype(BF)
        x2[...] = (x1[...] - dot(lb[1, 0], coef)).astype(BF)
        z5[...] = dot_t(lb[1, 0], x2[...]) * s2
        z[:, :cols] = z5[...].astype(BF)
        z[:, cols:] = (dot_t(lb[0, 0], x2[...]) * s1).astype(BF)

    state2, down5, down_send = call(
        two_body,
        [(tall, BF), (wide, f32), ((rank, 2 * cols), BF)],
        state1,
        cross_send,
        cross_in,
        lb,
        caps,
        top_send,
        scratch=[pltpu.VMEM((2 * rank, cols), BF)],
        micros=0.1,
    )
    down_in = swap(down_send, "leaf", 1)
    top_near = swap(after(top_send, state2), "top", 1)
    top_parts = top_send, top_near, top_far, swap(top_far, "top", 1)

    turn_far_near = swap(after(turn_far, top_far), "top", 1)

    def order_body(a, b, c, d, caps, out, row):
        here = lax.axis_index("top")
        for k in range(4):
            for i, piece in enumerate((a, b, c, d)):
                out[span(i), span(k)] = piece[:, block(here ^ k, rank)]
            row[:, span(k)] = caps[:, block(here ^ k, rank)]

    turn_all, caps_row = call(
        order_body,
        [((4 * rank, 4 * rank), BF), ((rank, 4 * rank), BF)],
        turn,
        turn_near,
        turn_far,
        turn_far_near,
        top_caps,
        micros=0.1,
    )

    def under_body(x2, rb, tl, tr, inv, seen, out2, under):
        for c in range(blocks):
            column = inv[c * rank :, span(c)]
            out2[span(c), :] = dot_t(column, x2[c * rank :, :])
            for i, basis in enumerate((tl[0], tr[0], rb[1, 0], rb[0, 0])):
                under[span(c), span(i)] = dot_t(column, basis[c * rank :, :]).astype(BF)

    out2, under = call(
        under_body,
        [(tall, f32), ((rows, 4 * rank), BF)],
        state2,
        rb,
        tl,
        tr,
        inverse,
        late_sib,
        micros=3,
    )

    def top_body(a, b, c, d, turns, row, seen, out, up):
        for i, piece in enumerate((a, b, c, d)):
            up[span(i), :] = piece[...]
        turned = dot(turns[...], up[...]).astype(BF)
        out[:, :cols] = dot(row[...], up[...]).astype(BF)
        out[:, cols:] = dot(row[...], turned).astype(BF)

    (back_send,) = call(
        top_body,
        [((rank, 2 * cols), BF)],
        *top_parts,
        turn_all,
        caps_row,
        out2,
        scratch=[pltpu.VMEM((4 * rank, cols), BF)],
        micros=1,
    )
    back_in = swap(back_send, "leaf", 1)

    def down_body(back, back_sib, down5, z_sib, late, late_sib, both, send, pieces):
        side = column_side()
        pieces[side] = back[...]
        pieces[1 - side] = back_sib[...]
        both[span(0), :] = pieces[0, :, :cols]
        both[span(1), :] = (pieces[1, :, :cols].astype(f32) - pieces[0, :, cols:]).astype(BF)
        gram = (late[:, span(4, 2)].astype(f32) + late_sib[:, span(4, 2)]).astype(BF)
        send[...] = (down5[...] + z_sib[:, :cols] - dot(gram, both[...])).astype(BF)

    both, half5 = call(
        down_body,
        [((2 * rank, cols), BF), (wide, BF)],
        back_send,
        back_in,
        down5,
        down_in,
        late,
        late_sib,
        scratch=[pltpu.VMEM((2, rank, 2 * cols), BF)],
        micros=0.3,
    )
    half5_far = swap(half5, "leaf", 3)

    def part_body(out2, under, both, z, z_sib, late, late_sib, seen, proj, out3):
        def down(zs, gram):
            return zs[:, cols:] - dot(gram[:, span(0, 2)], both[...])

        put_rows(proj, tree_side(0), down(z, late), down(z_sib, late_sib))
        out3[...] = out2[...] - dot(under[:, span(0, 2)], both[...])

    proj6, out3 = call(
        part_body,
        [((2 * rank, cols), f32), (tall, f32)],
        out2,
        under,
        both,
        down_send,
        down_in,
        late,
        late_sib,
        half5,
        micros=0.3,
    )

    def last_body(
        out3, under, half5, half5_far, late, late_sib, proj6, caps, out,
        coefs, stack, grams, out_v, sems,
    ):
        put_rows(stack, tree_side(1), half5[...], half5_far[...])
        put_rows(grams, tree_side(0), late[:, span(2, 2)], late_sib[:, span(2, 2)])
        proj = (proj6[...] - dot(grams[...], stack[...])).astype(BF)
        coefs[span(0), :] = dot(caps[1, 0], stack[...]).astype(BF)
        coefs[span(1), :] = dot(caps[0, 0], proj).astype(BF)
        copies = []
        for c in range(blocks):
            out_v[span(c), :] = out3[span(c), :] - dot(under[span(c), span(2, 2)], coefs[...])
            copy = pltpu.make_async_copy(out_v.at[span(c), :], out.at[0, span(c), :], sems.at[c])
            copy.start()
            copies.append(copy)
        for copy in copies:
            copy.wait()

    (out,) = call(
        last_body,
        [((1, rows, cols), f32)],
        out3,
        under,
        half5,
        half5_far,
        late,
        late_sib,
        proj6,
        caps,
        hbm_out=True,
        scratch=[
            pltpu.VMEM((2 * rank, cols), BF),
            pltpu.VMEM((2 * rank, cols), BF),
            pltpu.VMEM((2 * rank, 2 * rank), BF),
            pltpu.VMEM(tall, f32),
            pltpu.SemaphoreType.DMA((blocks,)),
        ],
    )
    return out


def on_device(*args):
    levels = args[2].shape[0]
    sizes = lax.axis_size("leaf"), lax.axis_size("top")
    if levels == 2 and sizes == (4, 4):
        return two_levels(*args)
    return step_by_step(*args)


def solution(mesh):
    rows = P(("parts", "top"), "leaf", None)
    level_rows = P(None, ("parts", "top"), "leaf", None)
    return jax.shard_map(
        on_device,
        mesh=mesh,
        in_specs=(
            rows,
            rows,
            level_rows,
            level_rows,
            level_rows,
            rows,
            rows,
            P(("parts", "top"), None),
        ),
        out_specs=rows,
        check_vma=False,
    )
```

```python
import math

import jax
import jax.numpy as jnp
from jax import lax
from jax.experimental import pallas as pl
from jax.experimental.pallas import tpu as pltpu
from jax.sharding import PartitionSpec as P

BF = jnp.bfloat16
VMEM_LIMIT = 8 * 2**20
FLOPS_PER_MICRO = 1e9


def swap(value, axis, mask):
    pairs = [(source, source ^ mask) for source in range(lax.axis_size(axis))]
    return lax.ppermute(value, axis, pairs)


def dot(a, b):
    return jnp.dot(a, b, preferred_element_type=jnp.float32)


def dot_t(a, b):
    return lax.dot_general(a, b, (((0,), (0,)), ((), ())), preferred_element_type=jnp.float32)


def ordered(upper_side, own, other):
    return jnp.where(
        upper_side, jnp.concatenate([other, own], 0), jnp.concatenate([own, other], 0)
    )


def level_step(current, project_basis, update_basis, caps_rows, level_num):
    leaf_rows = current.shape[0]
    shift_bits = level_num - 1
    partial_value = dot_t(project_basis, current.astype(BF)) * (
        1.0 / math.sqrt(leaf_rows * 2**shift_bits)
    )
    for bit_index in range(shift_bits):
        partial_value = partial_value + swap(partial_value, "leaf", 2**bit_index)
    own = partial_value.astype(BF)
    other = swap(own, "leaf", 2**shift_bits)
    upper_side = (lax.axis_index("leaf") >> shift_bits) & 1 == 1
    stacked = ordered(upper_side, own, other)
    weights = dot(caps_rows, stacked).astype(BF)
    return current - dot(update_basis, weights)


def top_step(current, project_basis, update_basis, caps_rows):
    leaf_count = lax.axis_size("leaf")
    partial_value = dot_t(project_basis, current.astype(BF)) * (
        1.0 / math.sqrt(leaf_count * current.shape[0])
    )
    column_total = lax.psum(partial_value, "leaf")
    stacked = lax.all_gather(column_total.astype(BF), "top", axis=0, tiled=True)
    weights = dot(caps_rows, stacked).astype(BF)
    return current - dot(update_basis, weights)


def step_by_step(
    right_side, leaf_inverse, left_basis, right_basis, level_caps, top_left, top_right, top_caps
):
    levels = left_basis.shape[0]
    lefts = [left_basis[k, 0] for k in range(levels)]
    rights = [right_basis[k, 0] for k in range(levels)]
    current = dot(leaf_inverse[0], right_side[0].astype(BF))
    for k in range(levels):
        current = level_step(current, rights[k], lefts[k], level_caps[k, 0], k + 1)
    current = top_step(current, top_right[0], top_left[0], top_caps)
    current = top_step(current, top_left[0], top_right[0], top_caps)
    for k in reversed(range(levels)):
        current = level_step(current, lefts[k], rights[k], level_caps[k, 0], k + 1)
    return dot_t(leaf_inverse[0], current.astype(BF))[None]


def in_hbm(value):
    return pltpu.with_memory_space_constraint(value, pltpu.HBM)


def in_vmem(value):
    return pltpu.with_memory_space_constraint(value, pltpu.VMEM)


def call(body, outs, *args, scratch=(), hbm=(), hbm_out=False, micros=1):
    vmem = pl.BlockSpec(memory_space=pltpu.VMEM)
    anywhere = pl.BlockSpec(memory_space=pl.ANY)
    return pl.pallas_call(
        body,
        out_shape=[
            jax.ShapeDtypeStruct(shape, dtype) if hbm_out else pltpu.VMEM(shape, dtype)
            for shape, dtype in outs
        ],
        in_specs=[anywhere if i in hbm else vmem for i in range(len(args))],
        out_specs=[anywhere if hbm_out else vmem] * len(outs),
        scratch_shapes=list(scratch),
        compiler_params=pltpu.CompilerParams(vmem_limit_bytes=VMEM_LIMIT),
        cost_estimate=pl.CostEstimate(
            flops=int(micros * FLOPS_PER_MICRO), bytes_accessed=0, transcendentals=0
        ),
    )(*[in_hbm(a) if i in hbm else in_vmem(a) for i, a in enumerate(args)])


def after(value, *others):
    return lax.optimization_barrier((value, *others))[0]


def tree_side(bit):
    return (lax.axis_index("leaf") >> bit) & 1


def column_side():
    leaf = lax.axis_index("leaf")
    return (leaf ^ (leaf >> 1)) & 1


def block(index, width):
    return pl.ds(pl.multiple_of(index * width, width), width)


def put_rows(scratch, upper, own, other):
    rows = own.shape[0]
    scratch[block(upper, rows), :] = own
    scratch[block(1 - upper, rows), :] = other


def two_levels(
    right_side, leaf_inverse, left_basis, right_basis, level_caps, top_left, top_right, top_caps
):
    rows, cols = right_side.shape[1:]
    rank = top_left.shape[2]
    f32 = jnp.float32
    s1 = 1.0 / math.sqrt(rows)
    s2 = 1.0 / math.sqrt(rows * 2)
    st = 1.0 / math.sqrt(rows * 4)
    blocks = rows // rank
    square, wide, tall = (rank, rank), (rank, cols), (rows, cols)

    def span(i, n=1):
        return slice(i * rank, (i + n) * rank)

    def start_body(
        rhs_hbm, inv_hbm, lb_hbm, rb_hbm, caps_hbm, tl_hbm, tr_hbm,
        x_ref, send, inv_ref, lb, rb, caps, tl, tr, rhs_v, sems,
    ):
        def load(source, target, *at):
            copy = pltpu.make_async_copy(source, target, sems.at[at])
            copy.start()
            return copy

        copies = []
        for i in range(blocks):
            copies.append(load(rhs_hbm.at[0, span(i), :], rhs_v.at[span(i), :], 0, i))
            copies.append(
                load(
                    inv_hbm.at[0, span(i), span(0, i + 1)],
                    inv_ref.at[span(i), span(0, i + 1)],
                    1,
                    i,
                )
            )
        pairs = ((rb_hbm, rb), (lb_hbm, lb), (tl_hbm, tl), (tr_hbm, tr), (caps_hbm, caps))
        bases = [load(source, target, 2, i) for i, (source, target) in enumerate(pairs)]
        for i in range(blocks):
            copies[2 * i].wait()
            copies[2 * i + 1].wait()
            x_ref[span(i), :] = dot(
                inv_ref[span(i), span(0, i + 1)], rhs_v[span(0, i + 1), :].astype(BF)
            )
        bases[0].wait()
        send[...] = (dot_t(rb[0, 0], x_ref[...].astype(BF)) * s1).astype(BF)
        for copy in bases[1:]:
            copy.wait()

    state0, proj1, inverse, lb, rb, caps, tl, tr = call(
        start_body,
        [(tall, f32), (wide, BF), ((rows, rows), BF)]
        + [(a.shape, a.dtype) for a in (left_basis, right_basis, level_caps, top_left, top_right)],
        right_side,
        leaf_inverse,
        left_basis,
        right_basis,
        level_caps,
        top_left,
        top_right,
        hbm=range(7),
        scratch=[pltpu.VMEM(tall, f32), pltpu.SemaphoreType.DMA((3, max(blocks, 5)))],
    )
    proj1_sib = swap(proj1, "leaf", 1)
    proj1_near = swap(proj1, "top", 1)

    def early_body(lb, caps, tl, tr, seen, send, keep, scratch):
        side = column_side()
        for i, basis in enumerate((tr, tl)):
            gram = (dot_t(basis[0], lb[1, 0]) * st).astype(BF)
            scratch[i] = dot(gram, caps[1, 0]).astype(BF)
        send[:, : 2 * rank] = scratch[1 - side]
        send[:, span(2)] = (dot_t(tl[0], tl[0]) * st).astype(BF)
        keep[...] = scratch[side]

    early, early_keep = call(
        early_body,
        [((rank, 3 * rank), BF), ((rank, 2 * rank), BF)],
        lb,
        caps,
        tl,
        tr,
        proj1_near,
        scratch=[pltpu.VMEM((2, rank, 2 * rank), BF)],
        micros=10,
    )
    early_sib = swap(early, "leaf", 1)

    def one_body(x0, p, p_sib, lb, rb, caps, tl, tr, seen, x1, send, keep, stack, scratch):
        side = column_side()
        put_rows(stack, tree_side(0), p[...], p_sib[...])
        coef = dot(caps[0, 0], stack[...]).astype(BF)
        x1[...] = x0[...] - dot(lb[0, 0], coef)
        state = x1[...].astype(BF)
        keep[:, :cols] = dot_t(rb[1, 0], state) * s2
        send[:, :cols] = keep[:, :cols].astype(BF)
        for i, basis in enumerate((tr, tl)):
            scratch[i] = dot_t(basis[0], state) * st
        send[:, cols:] = scratch[1 - side].astype(BF)
        keep[:, cols:] = scratch[side]

    state1, pair_send, pair_keep = call(
        one_body,
        [(tall, f32), ((rank, 2 * cols), BF), ((rank, 2 * cols), f32)],
        state0,
        proj1,
        proj1_sib,
        lb,
        rb,
        caps,
        tl,
        tr,
        early,
        scratch=[pltpu.VMEM((2 * rank, cols), BF), pltpu.VMEM((2, rank, cols), f32)],
        micros=3,
    )
    pair_in = swap(pair_send, "leaf", 1)

    def pair_body(mine, own, sib, seen, send, keep, gram, scratch):
        upper = tree_side(1)
        scratch[...] = (mine[...].astype(f32) + sib[:, : 2 * rank]).astype(BF)
        keep[:, span(0)] = scratch[:, block(upper, rank)]
        keep[:, span(1)] = scratch[:, block(1 - upper, rank)]
        send[:, span(0)] = keep[:, span(1)]
        gram[...] = own[:, span(2)].astype(f32) + sib[:, span(2)]
        send[:, span(1)] = gram[...].astype(BF)

    next_send, next_keep, gram_pair = call(
        pair_body,
        [((rank, 2 * rank), BF), ((rank, 2 * rank), BF), (square, f32)],
        early_keep,
        early,
        early_sib,
        state1,
        scratch=[pltpu.VMEM((rank, 2 * rank), BF)],
        micros=1,
    )
    next_far = swap(next_send, "leaf", 3)
    def late_body(lb, rb, caps, tl, tr, seen, out):
        for i, basis in enumerate((tl[0], tr[0])):
            out[:, span(i)] = (dot_t(lb[0, 0], basis) * s1).astype(BF)
            out[:, span(4 + i)] = (dot_t(lb[1, 0], basis) * s2).astype(BF)
        gram = (dot_t(lb[0, 0], rb[1, 0]) * s1).astype(BF)
        out[:, span(2, 2)] = dot(gram, caps[1, 0]).astype(BF)

    (late,) = call(
        late_body,
        [((rank, 6 * rank), BF)],
        lb,
        rb,
        caps,
        tl,
        tr,
        next_send,
        micros=0.5,
    )

    def half_body(keep, pair, nexts, seen, send, keep2):
        send[:, :cols] = (keep[:, :cols] + pair[:, :cols]).astype(BF)
        keep2[...] = keep[:, cols:] + pair[:, cols:] - dot(nexts[:, span(0)], send[:, :cols])
        send[:, cols:] = keep2[...].astype(BF)

    cross_send, cross_keep = call(
        half_body,
        [((rank, 2 * cols), BF), (wide, f32)],
        pair_keep,
        pair_in,
        next_keep,
        late,
        micros=5,
    )
    cross_in = swap(cross_send, "leaf", 3)

    def turn_body(gram, far, caps, seen, out):
        whole = (gram[...] + far[:, span(1)]).astype(BF)
        out[...] = dot(whole, caps[...]).astype(BF)

    (turn,) = call(
        turn_body, [(top_caps.shape, BF)], gram_pair, next_far, top_caps, cross_send, micros=5
    )
    turn_far = swap(turn, "top", 2)
    turn_near = swap(turn, "top", 1)
    late_sib = swap(after(late, cross_send), "leaf", 1)

    def column_body(send, keep2, far, nexts, nexts_far, seen, out):
        out[...] = (
            keep2[...]
            + far[:, cols:]
            - dot(nexts[:, span(1)], far[:, :cols])
            - dot(nexts_far[:, span(0)], send[:, :cols])
        ).astype(BF)

    (top_send,) = call(
        column_body,
        [(wide, BF)],
        cross_send,
        cross_keep,
        cross_in,
        next_keep,
        next_far,
        turn,
        micros=0.2,
    )
    top_far = swap(top_send, "top", 2)

    def two_body(x1, send, far, lb, caps, seen, x2, z5, z, stack):
        put_rows(stack, tree_side(1), send[:, :cols], far[:, :cols])
        coef = dot(caps[1, 0], stack[...]).astype(BF)
        x2[...] = (x1[...] - dot(lb[1, 0], coef)).astype(BF)
        z5[...] = dot_t(lb[1, 0], x2[...]) * s2
        z[:, :cols] = z5[...].astype(BF)
        z[:, cols:] = (dot_t(lb[0, 0], x2[...]) * s1).astype(BF)

    state2, down5, down_send = call(
        two_body,
        [(tall, BF), (wide, f32), ((rank, 2 * cols), BF)],
        state1,
        cross_send,
        cross_in,
        lb,
        caps,
        top_send,
        scratch=[pltpu.VMEM((2 * rank, cols), BF)],
        micros=0.1,
    )
    down_in = swap(down_send, "leaf", 1)
    top_near = swap(after(top_send, state2), "top", 1)
    top_parts = top_send, top_near, top_far, swap(top_far, "top", 1)

    turn_far_near = swap(after(turn_far, top_far), "top", 1)

    def order_body(a, b, c, d, caps, out, row):
        here = lax.axis_index("top")
        for k in range(4):
            for i, piece in enumerate((a, b, c, d)):
                out[span(i), span(k)] = piece[:, block(here ^ k, rank)]
            row[:, span(k)] = caps[:, block(here ^ k, rank)]

    turn_all, caps_row = call(
        order_body,
        [((4 * rank, 4 * rank), BF), ((rank, 4 * rank), BF)],
        turn,
        turn_near,
        turn_far,
        turn_far_near,
        top_caps,
        micros=0.1,
    )

    def under_body(x2, rb, tl, tr, inv, seen, out2, under):
        for c in range(blocks):
            column = inv[c * rank :, span(c)]
            out2[span(c), :] = dot_t(column, x2[c * rank :, :])
            for i, basis in enumerate((tl[0], tr[0], rb[1, 0], rb[0, 0])):
                under[span(c), span(i)] = dot_t(column, basis[c * rank :, :]).astype(BF)

    out2, under = call(
        under_body,
        [(tall, f32), ((rows, 4 * rank), BF)],
        state2,
        rb,
        tl,
        tr,
        inverse,
        late_sib,
        micros=3,
    )

    def top_body(a, b, c, d, turns, row, seen, out, up):
        for i, piece in enumerate((a, b, c, d)):
            up[span(i), :] = piece[...]
        turned = dot(turns[...], up[...]).astype(BF)
        out[:, :cols] = dot(row[...], up[...]).astype(BF)
        out[:, cols:] = dot(row[...], turned).astype(BF)

    (back_send,) = call(
        top_body,
        [((rank, 2 * cols), BF)],
        *top_parts,
        turn_all,
        caps_row,
        out2,
        scratch=[pltpu.VMEM((4 * rank, cols), BF)],
        micros=1,
    )
    back_in = swap(back_send, "leaf", 1)

    def down_body(back, back_sib, down5, z_sib, late, late_sib, both, send, pieces):
        side = column_side()
        pieces[side] = back[...]
        pieces[1 - side] = back_sib[...]
        both[span(0), :] = pieces[0, :, :cols]
        both[span(1), :] = (pieces[1, :, :cols].astype(f32) - pieces[0, :, cols:]).astype(BF)
        gram = (late[:, span(4, 2)].astype(f32) + late_sib[:, span(4, 2)]).astype(BF)
        send[...] = (down5[...] + z_sib[:, :cols] - dot(gram, both[...])).astype(BF)

    both, half5 = call(
        down_body,
        [((2 * rank, cols), BF), (wide, BF)],
        back_send,
        back_in,
        down5,
        down_in,
        late,
        late_sib,
        scratch=[pltpu.VMEM((2, rank, 2 * cols), BF)],
        micros=0.3,
    )
    half5_far = swap(half5, "leaf", 3)

    def part_body(out2, under, both, z, z_sib, late, late_sib, seen, proj, out3):
        def down(zs, gram):
            return zs[:, cols:] - dot(gram[:, span(0, 2)], both[...])

        put_rows(proj, tree_side(0), down(z, late), down(z_sib, late_sib))
        out3[...] = out2[...] - dot(under[:, span(0, 2)], both[...])

    proj6, out3 = call(
        part_body,
        [((2 * rank, cols), f32), (tall, f32)],
        out2,
        under,
        both,
        down_send,
        down_in,
        late,
        late_sib,
        half5,
        micros=0.3,
    )

    def last_body(
        out3, under, half5, half5_far, late, late_sib, proj6, caps, out,
        coefs, stack, grams, out_v, sems,
    ):
        put_rows(stack, tree_side(1), half5[...], half5_far[...])
        put_rows(grams, tree_side(0), late[:, span(2, 2)], late_sib[:, span(2, 2)])
        proj = (proj6[...] - dot(grams[...], stack[...])).astype(BF)
        coefs[span(0), :] = dot(caps[1, 0], stack[...]).astype(BF)
        coefs[span(1), :] = dot(caps[0, 0], proj).astype(BF)
        copies = []
        for c in range(blocks):
            out_v[span(c), :] = out3[span(c), :] - dot(under[span(c), span(2, 2)], coefs[...])
            copy = pltpu.make_async_copy(out_v.at[span(c), :], out.at[0, span(c), :], sems.at[c])
            copy.start()
            copies.append(copy)
        for copy in copies:
            copy.wait()

    (out,) = call(
        last_body,
        [((1, rows, cols), f32)],
        out3,
        under,
        half5,
        half5_far,
        late,
        late_sib,
        proj6,
        caps,
        hbm_out=True,
        scratch=[
            pltpu.VMEM((2 * rank, cols), BF),
            pltpu.VMEM((2 * rank, cols), BF),
            pltpu.VMEM((2 * rank, 2 * rank), BF),
            pltpu.VMEM(tall, f32),
            pltpu.SemaphoreType.DMA((blocks,)),
        ],
    )
    return out


def on_device(*args):
    levels = args[2].shape[0]
    sizes = lax.axis_size("leaf"), lax.axis_size("top")
    if levels == 2 and sizes == (4, 4):
        return two_levels(*args)
    return step_by_step(*args)


def solution(mesh):
    rows = P(("parts", "top"), "leaf", None)
    level_rows = P(None, ("parts", "top"), "leaf", None)
    return jax.shard_map(
        on_device,
        mesh=mesh,
        in_specs=(
            rows,
            rows,
            level_rows,
            level_rows,
            level_rows,
            rows,
            rows,
            P(("parts", "top"), None),
        ),
        out_specs=rows,
        check_vma=False,
    )
```

```python
import math

import jax
import jax.numpy as jnp
from jax import lax
from jax.experimental import pallas as pl
from jax.experimental.pallas import tpu as pltpu
from jax.sharding import PartitionSpec as P

BF = jnp.bfloat16
VMEM_LIMIT = 8 * 2**20
FLOPS_PER_MICRO = 1e9


def swap(value, axis, mask):
    pairs = [(source, source ^ mask) for source in range(lax.axis_size(axis))]
    return lax.ppermute(value, axis, pairs)


def dot(a, b):
    return jnp.dot(a, b, preferred_element_type=jnp.float32)


def dot_t(a, b):
    return lax.dot_general(a, b, (((0,), (0,)), ((), ())), preferred_element_type=jnp.float32)


def ordered(upper_side, own, other):
    return jnp.where(
        upper_side, jnp.concatenate([other, own], 0), jnp.concatenate([own, other], 0)
    )


def level_step(current, project_basis, update_basis, caps_rows, level_num):
    leaf_rows = current.shape[0]
    shift_bits = level_num - 1
    partial_value = dot_t(project_basis, current.astype(BF)) * (
        1.0 / math.sqrt(leaf_rows * 2**shift_bits)
    )
    for bit_index in range(shift_bits):
        partial_value = partial_value + swap(partial_value, "leaf", 2**bit_index)
    own = partial_value.astype(BF)
    other = swap(own, "leaf", 2**shift_bits)
    upper_side = (lax.axis_index("leaf") >> shift_bits) & 1 == 1
    stacked = ordered(upper_side, own, other)
    weights = dot(caps_rows, stacked).astype(BF)
    return current - dot(update_basis, weights)


def top_step(current, project_basis, update_basis, caps_rows):
    leaf_count = lax.axis_size("leaf")
    partial_value = dot_t(project_basis, current.astype(BF)) * (
        1.0 / math.sqrt(leaf_count * current.shape[0])
    )
    column_total = lax.psum(partial_value, "leaf")
    stacked = lax.all_gather(column_total.astype(BF), "top", axis=0, tiled=True)
    weights = dot(caps_rows, stacked).astype(BF)
    return current - dot(update_basis, weights)


def step_by_step(
    right_side, leaf_inverse, left_basis, right_basis, level_caps, top_left, top_right, top_caps
):
    levels = left_basis.shape[0]
    lefts = [left_basis[k, 0] for k in range(levels)]
    rights = [right_basis[k, 0] for k in range(levels)]
    current = dot(leaf_inverse[0], right_side[0].astype(BF))
    for k in range(levels):
        current = level_step(current, rights[k], lefts[k], level_caps[k, 0], k + 1)
    current = top_step(current, top_right[0], top_left[0], top_caps)
    current = top_step(current, top_left[0], top_right[0], top_caps)
    for k in reversed(range(levels)):
        current = level_step(current, lefts[k], rights[k], level_caps[k, 0], k + 1)
    return dot_t(leaf_inverse[0], current.astype(BF))[None]


def in_hbm(value):
    return pltpu.with_memory_space_constraint(value, pltpu.HBM)


def in_vmem(value):
    return pltpu.with_memory_space_constraint(value, pltpu.VMEM)


def call(body, outs, *args, scratch=(), hbm=(), hbm_out=False, micros=1):
    vmem = pl.BlockSpec(memory_space=pltpu.VMEM)
    anywhere = pl.BlockSpec(memory_space=pl.ANY)
    return pl.pallas_call(
        body,
        out_shape=[
            jax.ShapeDtypeStruct(shape, dtype) if hbm_out else pltpu.VMEM(shape, dtype)
            for shape, dtype in outs
        ],
        in_specs=[anywhere if i in hbm else vmem for i in range(len(args))],
        out_specs=[anywhere if hbm_out else vmem] * len(outs),
        scratch_shapes=list(scratch),
        compiler_params=pltpu.CompilerParams(vmem_limit_bytes=VMEM_LIMIT),
        cost_estimate=pl.CostEstimate(
            flops=int(micros * FLOPS_PER_MICRO), bytes_accessed=0, transcendentals=0
        ),
    )(*[in_hbm(a) if i in hbm else in_vmem(a) for i, a in enumerate(args)])


def after(value, *others):
    return lax.optimization_barrier((value, *others))[0]


def tree_side(bit):
    return (lax.axis_index("leaf") >> bit) & 1


def column_side():
    leaf = lax.axis_index("leaf")
    return (leaf ^ (leaf >> 1)) & 1


def block(index, width):
    return pl.ds(pl.multiple_of(index * width, width), width)


def put_rows(scratch, upper, own, other):
    rows = own.shape[0]
    scratch[block(upper, rows), :] = own
    scratch[block(1 - upper, rows), :] = other


def two_levels(
    right_side, leaf_inverse, left_basis, right_basis, level_caps, top_left, top_right, top_caps
):
    rows, cols = right_side.shape[1:]
    rank = top_left.shape[2]
    f32 = jnp.float32
    s1 = 1.0 / math.sqrt(rows)
    s2 = 1.0 / math.sqrt(rows * 2)
    st = 1.0 / math.sqrt(rows * 4)
    blocks = rows // rank
    square, wide, tall = (rank, rank), (rank, cols), (rows, cols)

    def span(i, n=1):
        return slice(i * rank, (i + n) * rank)

    def start_body(
        rhs_hbm, inv_hbm, lb_hbm, rb_hbm, caps_hbm, tl_hbm, tr_hbm,
        x_ref, send, inv_ref, lb, rb, caps, tl, tr, rhs_v, sems,
    ):
        def load(source, target, *at):
            copy = pltpu.make_async_copy(source, target, sems.at[at])
            copy.start()
            return copy

        copies = []
        for i in range(blocks):
            copies.append(load(rhs_hbm.at[0, span(i), :], rhs_v.at[span(i), :], 0, i))
            copies.append(
                load(
                    inv_hbm.at[0, span(i), span(0, i + 1)],
                    inv_ref.at[span(i), span(0, i + 1)],
                    1,
                    i,
                )
            )
        pairs = ((rb_hbm, rb), (lb_hbm, lb), (tl_hbm, tl), (tr_hbm, tr), (caps_hbm, caps))
        bases = [load(source, target, 2, i) for i, (source, target) in enumerate(pairs)]
        for i in range(blocks):
            copies[2 * i].wait()
            copies[2 * i + 1].wait()
            x_ref[span(i), :] = dot(
                inv_ref[span(i), span(0, i + 1)], rhs_v[span(0, i + 1), :].astype(BF)
            )
        bases[0].wait()
        send[...] = (dot_t(rb[0, 0], x_ref[...].astype(BF)) * s1).astype(BF)
        for copy in bases[1:]:
            copy.wait()

    state0, proj1, inverse, lb, rb, caps, tl, tr = call(
        start_body,
        [(tall, f32), (wide, BF), ((rows, rows), BF)]
        + [(a.shape, a.dtype) for a in (left_basis, right_basis, level_caps, top_left, top_right)],
        right_side,
        leaf_inverse,
        left_basis,
        right_basis,
        level_caps,
        top_left,
        top_right,
        hbm=range(7),
        scratch=[pltpu.VMEM(tall, f32), pltpu.SemaphoreType.DMA((3, max(blocks, 5)))],
    )
    proj1_sib = swap(proj1, "leaf", 1)
    proj1_near = swap(proj1, "top", 1)

    def early_body(lb, caps, tl, tr, seen, send, keep, scratch):
        side = column_side()
        for i, basis in enumerate((tr, tl)):
            gram = (dot_t(basis[0], lb[1, 0]) * st).astype(BF)
            scratch[i] = dot(gram, caps[1, 0]).astype(BF)
        send[:, : 2 * rank] = scratch[1 - side]
        send[:, span(2)] = (dot_t(tl[0], tl[0]) * st).astype(BF)
        keep[...] = scratch[side]

    early, early_keep = call(
        early_body,
        [((rank, 3 * rank), BF), ((rank, 2 * rank), BF)],
        lb,
        caps,
        tl,
        tr,
        proj1_near,
        scratch=[pltpu.VMEM((2, rank, 2 * rank), BF)],
        micros=10,
    )
    early_sib = swap(early, "leaf", 1)

    def one_body(x0, p, p_sib, lb, rb, caps, tl, tr, seen, x1, send, keep, stack, scratch):
        side = column_side()
        put_rows(stack, tree_side(0), p[...], p_sib[...])
        coef = dot(caps[0, 0], stack[...]).astype(BF)
        x1[...] = x0[...] - dot(lb[0, 0], coef)
        state = x1[...].astype(BF)
        keep[:, :cols] = dot_t(rb[1, 0], state) * s2
        send[:, :cols] = keep[:, :cols].astype(BF)
        for i, basis in enumerate((tr, tl)):
            scratch[i] = dot_t(basis[0], state) * st
        send[:, cols:] = scratch[1 - side].astype(BF)
        keep[:, cols:] = scratch[side]

    state1, pair_send, pair_keep = call(
        one_body,
        [(tall, f32), ((rank, 2 * cols), BF), ((rank, 2 * cols), f32)],
        state0,
        proj1,
        proj1_sib,
        lb,
        rb,
        caps,
        tl,
        tr,
        early,
        scratch=[pltpu.VMEM((2 * rank, cols), BF), pltpu.VMEM((2, rank, cols), f32)],
        micros=3,
    )
    pair_in = swap(pair_send, "leaf", 1)

    def pair_body(mine, own, sib, seen, send, keep, gram, scratch):
        upper = tree_side(1)
        scratch[...] = (mine[...].astype(f32) + sib[:, : 2 * rank]).astype(BF)
        keep[:, span(0)] = scratch[:, block(upper, rank)]
        keep[:, span(1)] = scratch[:, block(1 - upper, rank)]
        send[:, span(0)] = keep[:, span(1)]
        gram[...] = own[:, span(2)].astype(f32) + sib[:, span(2)]
        send[:, span(1)] = gram[...].astype(BF)

    next_send, next_keep, gram_pair = call(
        pair_body,
        [((rank, 2 * rank), BF), ((rank, 2 * rank), BF), (square, f32)],
        early_keep,
        early,
        early_sib,
        state1,
        scratch=[pltpu.VMEM((rank, 2 * rank), BF)],
        micros=1,
    )
    next_far = swap(next_send, "leaf", 3)
    def half_body(keep, pair, nexts, send, keep2):
        send[:, :cols] = (keep[:, :cols] + pair[:, :cols]).astype(BF)
        keep2[...] = keep[:, cols:] + pair[:, cols:] - dot(nexts[:, span(0)], send[:, :cols])
        send[:, cols:] = keep2[...].astype(BF)

    cross_send, cross_keep = call(
        half_body,
        [((rank, 2 * cols), BF), (wide, f32)],
        pair_keep,
        pair_in,
        next_keep,
        micros=5,
    )
    cross_in = swap(cross_send, "leaf", 3)

    def turn_body(gram, far, caps, seen, out):
        whole = (gram[...] + far[:, span(1)]).astype(BF)
        out[...] = dot(whole, caps[...]).astype(BF)

    (turn,) = call(
        turn_body, [(top_caps.shape, BF)], gram_pair, next_far, top_caps, cross_send, micros=0.1
    )
    turn_far = swap(turn, "top", 2)
    turn_near = swap(turn, "top", 1)
    def late_body(lb, rb, caps, tl, tr, seen, seen2, out):
        for i, basis in enumerate((tl[0], tr[0])):
            out[:, span(i)] = (dot_t(lb[0, 0], basis) * s1).astype(BF)
            out[:, span(4 + i)] = (dot_t(lb[1, 0], basis) * s2).astype(BF)
        gram = (dot_t(lb[0, 0], rb[1, 0]) * s1).astype(BF)
        out[:, span(2, 2)] = dot(gram, caps[1, 0]).astype(BF)

    (late,) = call(
        late_body,
        [((rank, 6 * rank), BF)],
        lb,
        rb,
        caps,
        tl,
        tr,
        cross_send,
        next_far,
        micros=5,
    )

    late_sib = swap(late, "leaf", 1)

    def column_body(send, keep2, far, nexts, nexts_far, seen, out):
        out[...] = (
            keep2[...]
            + far[:, cols:]
            - dot(nexts[:, span(1)], far[:, :cols])
            - dot(nexts_far[:, span(0)], send[:, :cols])
        ).astype(BF)

    (top_send,) = call(
        column_body,
        [(wide, BF)],
        cross_send,
        cross_keep,
        cross_in,
        next_keep,
        next_far,
        late,
        micros=0.2,
    )
    top_far = swap(top_send, "top", 2)

    def two_body(x1, send, far, lb, caps, seen, x2, z5, z5_b, z6, stack):
        put_rows(stack, tree_side(1), send[:, :cols], far[:, :cols])
        coef = dot(caps[1, 0], stack[...]).astype(BF)
        x2[...] = (x1[...] - dot(lb[1, 0], coef)).astype(BF)
        z5[...] = dot_t(lb[1, 0], x2[...]) * s2
        z5_b[...] = z5[...].astype(BF)
        z6[...] = (dot_t(lb[0, 0], x2[...]) * s1).astype(BF)

    state2, down5, down5_send, down6 = call(
        two_body,
        [(tall, BF), (wide, f32), (wide, BF), (wide, BF)],
        state1,
        cross_send,
        cross_in,
        lb,
        caps,
        top_send,
        scratch=[pltpu.VMEM((2 * rank, cols), BF)],
        micros=0.1,
    )
    down_in = swap(down5_send, "leaf", 1)
    top_near = swap(after(top_send, state2), "top", 1)
    top_parts = top_send, top_near, top_far, swap(top_far, "top", 1)

    turn_far_near = swap(after(turn_far, top_far), "top", 1)

    def order_body(a, b, c, d, caps, out, row):
        here = lax.axis_index("top")
        for k in range(4):
            for i, piece in enumerate((a, b, c, d)):
                out[span(i), span(k)] = piece[:, block(here ^ k, rank)]
            row[:, span(k)] = caps[:, block(here ^ k, rank)]

    turn_all, caps_row = call(
        order_body,
        [((4 * rank, 4 * rank), BF), ((rank, 4 * rank), BF)],
        turn,
        turn_near,
        turn_far,
        turn_far_near,
        top_caps,
        micros=0.1,
    )

    def under_body(x2, rb, tl, tr, inv, seen, out2, under):
        for c in range(blocks):
            column = inv[c * rank :, span(c)]
            out2[span(c), :] = dot_t(column, x2[c * rank :, :])
            for i, basis in enumerate((tl[0], tr[0], rb[1, 0], rb[0, 0])):
                under[span(c), span(i)] = dot_t(column, basis[c * rank :, :]).astype(BF)

    out2, under = call(
        under_body,
        [(tall, f32), ((rows, 4 * rank), BF)],
        state2,
        rb,
        tl,
        tr,
        inverse,
        late_sib,
        micros=3,
    )

    def top_body(a, b, c, d, turns, row, seen, seen2, out, up):
        for i, piece in enumerate((a, b, c, d)):
            up[span(i), :] = piece[...]
        turned = dot(turns[...], up[...]).astype(BF)
        out[:, :cols] = dot(row[...], up[...]).astype(BF)
        out[:, cols:] = dot(row[...], turned).astype(BF)

    (back_send,) = call(
        top_body,
        [((rank, 2 * cols), BF)],
        *top_parts,
        turn_all,
        caps_row,
        out2,
        down_in,
        scratch=[pltpu.VMEM((4 * rank, cols), BF)],
        micros=1,
    )
    back_in = swap(back_send, "leaf", 1)

    def down_body(back, back_sib, down5, z_sib, late, late_sib, both, send, pieces):
        side = column_side()
        pieces[side] = back[...]
        pieces[1 - side] = back_sib[...]
        both[span(0), :] = pieces[0, :, :cols]
        both[span(1), :] = (pieces[1, :, :cols].astype(f32) - pieces[0, :, cols:]).astype(BF)
        gram = (late[:, span(4, 2)].astype(f32) + late_sib[:, span(4, 2)]).astype(BF)
        send[...] = (down5[...] + z_sib[...] - dot(gram, both[...])).astype(BF)

    both, half5 = call(
        down_body,
        [((2 * rank, cols), BF), (wide, BF)],
        back_send,
        back_in,
        down5,
        down_in,
        late,
        late_sib,
        scratch=[pltpu.VMEM((2, rank, 2 * cols), BF)],
        micros=0.3,
    )
    down6_sib = swap(after(down6, half5), "leaf", 1)
    half5_far = swap(half5, "leaf", 3)

    def part_body(out2, under, both, late, late_sib, seen, proj, out3):
        def down(gram):
            return dot(gram[:, span(0, 2)], both[...])

        put_rows(proj, tree_side(0), down(late), down(late_sib))
        out3[...] = out2[...] - dot(under[:, span(0, 2)], both[...])

    proj6, out3 = call(
        part_body,
        [((2 * rank, cols), f32), (tall, f32)],
        out2,
        under,
        both,
        late,
        late_sib,
        half5,
        micros=0.3,
    )

    def last_body(
        out3, under, half5, half5_far, late, late_sib, proj6, z, z_sib, caps, out,
        coefs, stack, grams, zs, out_v, sems,
    ):
        put_rows(stack, tree_side(1), half5[...], half5_far[...])
        put_rows(grams, tree_side(0), late[:, span(2, 2)], late_sib[:, span(2, 2)])
        put_rows(zs, tree_side(0), z[...], z_sib[...])
        proj = (zs[...] - proj6[...] - dot(grams[...], stack[...])).astype(BF)
        coefs[span(0), :] = dot(caps[1, 0], stack[...]).astype(BF)
        coefs[span(1), :] = dot(caps[0, 0], proj).astype(BF)
        copies = []
        for c in range(blocks):
            out_v[span(c), :] = out3[span(c), :] - dot(under[span(c), span(2, 2)], coefs[...])
            copy = pltpu.make_async_copy(out_v.at[span(c), :], out.at[0, span(c), :], sems.at[c])
            copy.start()
            copies.append(copy)
        for copy in copies:
            copy.wait()

    (out,) = call(
        last_body,
        [((1, rows, cols), f32)],
        out3,
        under,
        half5,
        half5_far,
        late,
        late_sib,
        proj6,
        down6,
        down6_sib,
        caps,
        hbm_out=True,
        scratch=[
            pltpu.VMEM((2 * rank, cols), BF),
            pltpu.VMEM((2 * rank, cols), BF),
            pltpu.VMEM((2 * rank, 2 * rank), BF),
            pltpu.VMEM((2 * rank, cols), BF),
            pltpu.VMEM(tall, f32),
            pltpu.SemaphoreType.DMA((blocks,)),
        ],
    )
    return out


def on_device(*args):
    levels = args[2].shape[0]
    sizes = lax.axis_size("leaf"), lax.axis_size("top")
    if levels == 2 and sizes == (4, 4):
        return two_levels(*args)
    return step_by_step(*args)


def solution(mesh):
    rows = P(("parts", "top"), "leaf", None)
    level_rows = P(None, ("parts", "top"), "leaf", None)
    return jax.shard_map(
        on_device,
        mesh=mesh,
        in_specs=(
            rows,
            rows,
            level_rows,
            level_rows,
            level_rows,
            rows,
            rows,
            P(("parts", "top"), None),
        ),
        out_specs=rows,
        check_vma=False,
    )
```

```python
import math

import jax
import jax.numpy as jnp
from jax import lax
from jax.experimental import pallas as pl
from jax.experimental.pallas import tpu as pltpu
from jax.sharding import PartitionSpec as P

BF = jnp.bfloat16
VMEM_LIMIT = 8 * 2**20
FLOPS_PER_MICRO = 1e9


def swap(value, axis, mask):
    pairs = [(source, source ^ mask) for source in range(lax.axis_size(axis))]
    return lax.ppermute(value, axis, pairs)


def dot(a, b):
    return jnp.dot(a, b, preferred_element_type=jnp.float32)


def dot_t(a, b):
    return lax.dot_general(a, b, (((0,), (0,)), ((), ())), preferred_element_type=jnp.float32)


def ordered(upper_side, own, other):
    return jnp.where(
        upper_side, jnp.concatenate([other, own], 0), jnp.concatenate([own, other], 0)
    )


def level_step(current, project_basis, update_basis, caps_rows, level_num):
    leaf_rows = current.shape[0]
    shift_bits = level_num - 1
    partial_value = dot_t(project_basis, current.astype(BF)) * (
        1.0 / math.sqrt(leaf_rows * 2**shift_bits)
    )
    for bit_index in range(shift_bits):
        partial_value = partial_value + swap(partial_value, "leaf", 2**bit_index)
    own = partial_value.astype(BF)
    other = swap(own, "leaf", 2**shift_bits)
    upper_side = (lax.axis_index("leaf") >> shift_bits) & 1 == 1
    stacked = ordered(upper_side, own, other)
    weights = dot(caps_rows, stacked).astype(BF)
    return current - dot(update_basis, weights)


def top_step(current, project_basis, update_basis, caps_rows):
    leaf_count = lax.axis_size("leaf")
    partial_value = dot_t(project_basis, current.astype(BF)) * (
        1.0 / math.sqrt(leaf_count * current.shape[0])
    )
    column_total = lax.psum(partial_value, "leaf")
    stacked = lax.all_gather(column_total.astype(BF), "top", axis=0, tiled=True)
    weights = dot(caps_rows, stacked).astype(BF)
    return current - dot(update_basis, weights)


def step_by_step(
    right_side, leaf_inverse, left_basis, right_basis, level_caps, top_left, top_right, top_caps
):
    levels = left_basis.shape[0]
    lefts = [left_basis[k, 0] for k in range(levels)]
    rights = [right_basis[k, 0] for k in range(levels)]
    current = dot(leaf_inverse[0], right_side[0].astype(BF))
    for k in range(levels):
        current = level_step(current, rights[k], lefts[k], level_caps[k, 0], k + 1)
    current = top_step(current, top_right[0], top_left[0], top_caps)
    current = top_step(current, top_left[0], top_right[0], top_caps)
    for k in reversed(range(levels)):
        current = level_step(current, lefts[k], rights[k], level_caps[k, 0], k + 1)
    return dot_t(leaf_inverse[0], current.astype(BF))[None]


def in_hbm(value):
    return pltpu.with_memory_space_constraint(value, pltpu.HBM)


def in_vmem(value):
    return pltpu.with_memory_space_constraint(value, pltpu.VMEM)


def call(body, outs, *args, scratch=(), hbm=(), hbm_out=False, micros=1):
    vmem = pl.BlockSpec(memory_space=pltpu.VMEM)
    anywhere = pl.BlockSpec(memory_space=pl.ANY)
    return pl.pallas_call(
        body,
        out_shape=[
            jax.ShapeDtypeStruct(shape, dtype) if hbm_out else pltpu.VMEM(shape, dtype)
            for shape, dtype in outs
        ],
        in_specs=[anywhere if i in hbm else vmem for i in range(len(args))],
        out_specs=[anywhere if hbm_out else vmem] * len(outs),
        scratch_shapes=list(scratch),
        compiler_params=pltpu.CompilerParams(vmem_limit_bytes=VMEM_LIMIT),
        cost_estimate=pl.CostEstimate(
            flops=int(micros * FLOPS_PER_MICRO), bytes_accessed=0, transcendentals=0
        ),
    )(*[in_hbm(a) if i in hbm else in_vmem(a) for i, a in enumerate(args)])


def after(value, *others):
    return lax.optimization_barrier((value, *others))[0]


def tree_side(bit):
    return (lax.axis_index("leaf") >> bit) & 1


def column_side():
    leaf = lax.axis_index("leaf")
    return (leaf ^ (leaf >> 1)) & 1


def block(index, width):
    return pl.ds(pl.multiple_of(index * width, width), width)


def put_rows(scratch, upper, own, other):
    rows = own.shape[0]
    scratch[block(upper, rows), :] = own
    scratch[block(1 - upper, rows), :] = other


def two_levels(
    right_side, leaf_inverse, left_basis, right_basis, level_caps, top_left, top_right, top_caps
):
    rows, cols = right_side.shape[1:]
    rank = top_left.shape[2]
    f32 = jnp.float32
    s1 = 1.0 / math.sqrt(rows)
    s2 = 1.0 / math.sqrt(rows * 2)
    st = 1.0 / math.sqrt(rows * 4)
    blocks = rows // rank
    square, wide, tall = (rank, rank), (rank, cols), (rows, cols)

    def span(i, n=1):
        return slice(i * rank, (i + n) * rank)

    def start_body(
        rhs_hbm, inv_hbm, lb_hbm, rb_hbm, caps_hbm, tl_hbm, tr_hbm,
        x_ref, send, inv_ref, lb, rb, caps, tl, tr, rhs_v, basis_t, sems,
    ):
        def load(source, target, *at):
            copy = pltpu.make_async_copy(source, target, sems.at[at])
            copy.start()
            return copy

        first = load(rb_hbm.at[0], rb.at[0], 2, 0)
        copies = []
        for i in range(blocks):
            copies.append(load(rhs_hbm.at[0, span(i), :], rhs_v.at[span(i), :], 0, i))
            copies.append(
                load(
                    inv_hbm.at[0, span(i), span(0, i + 1)],
                    inv_ref.at[span(i), span(0, i + 1)],
                    1,
                    i,
                )
            )
        pairs = (rb_hbm.at[1], rb.at[1]), (lb_hbm, lb), (tl_hbm, tl), (tr_hbm, tr), (caps_hbm, caps)
        bases = [load(source, target, 2, 1 + i) for i, (source, target) in enumerate(pairs)]
        first.wait()
        basis_t[...] = rb[0, 0].T
        for i in range(blocks):
            copies[2 * i].wait()
            copies[2 * i + 1].wait()
            x_ref[span(i), :] = dot(
                inv_ref[span(i), span(0, i + 1)], rhs_v[span(0, i + 1), :].astype(BF)
            )
        send[...] = (dot(basis_t[...], x_ref[...].astype(BF)) * s1).astype(BF)
        for copy in bases:
            copy.wait()

    state0, proj1, inverse, lb, rb, caps, tl, tr = call(
        start_body,
        [(tall, f32), (wide, BF), ((rows, rows), BF)]
        + [(a.shape, a.dtype) for a in (left_basis, right_basis, level_caps, top_left, top_right)],
        right_side,
        leaf_inverse,
        left_basis,
        right_basis,
        level_caps,
        top_left,
        top_right,
        hbm=range(7),
        scratch=[
            pltpu.VMEM(tall, f32),
            pltpu.VMEM((rank, rows), BF),
            pltpu.SemaphoreType.DMA((3, max(blocks, 6))),
        ],
    )
    proj1_sib = swap(proj1, "leaf", 1)
    proj1_near = swap(proj1, "top", 1)

    def early_body(lb, caps, tl, tr, seen, send, keep, scratch):
        side = column_side()
        for i, basis in enumerate((tr, tl)):
            gram = (dot_t(basis[0], lb[1, 0]) * st).astype(BF)
            scratch[i] = dot(gram, caps[1, 0]).astype(BF)
        send[:, : 2 * rank] = scratch[1 - side]
        send[:, span(2)] = (dot_t(tl[0], tl[0]) * st).astype(BF)
        keep[...] = scratch[side]

    early, early_keep = call(
        early_body,
        [((rank, 3 * rank), BF), ((rank, 2 * rank), BF)],
        lb,
        caps,
        tl,
        tr,
        proj1_near,
        scratch=[pltpu.VMEM((2, rank, 2 * rank), BF)],
        micros=10,
    )
    early_sib = swap(early, "leaf", 1)

    def flip_body(rb, tl, tr, seen, out):
        for i, basis in enumerate((rb[1, 0], tr[0], tl[0])):
            out[span(i), :] = basis.T

    (bases_t,) = call(flip_body, [((3 * rank, rows), BF)], rb, tl, tr, early, micros=0.2)

    def one_body(x0, p, p_sib, lb, caps, bases_t, x1, send, keep, stack, seen):
        side = column_side()
        put_rows(stack, tree_side(0), p[...], p_sib[...])
        coef = dot(caps[0, 0], stack[...]).astype(BF)
        x1[...] = x0[...] - dot(lb[0, 0], coef)
        seen[...] = dot(bases_t[...], x1[...].astype(BF))
        keep[:, :cols] = seen[span(0), :] * s2
        send[:, :cols] = keep[:, :cols].astype(BF)
        send[:, cols:] = (seen[block(2 - side, rank), :] * st).astype(BF)
        keep[:, cols:] = seen[block(1 + side, rank), :] * st

    state1, pair_send, pair_keep = call(
        one_body,
        [(tall, f32), ((rank, 2 * cols), BF), ((rank, 2 * cols), f32)],
        state0,
        proj1,
        proj1_sib,
        lb,
        caps,
        bases_t,
        scratch=[pltpu.VMEM((2 * rank, cols), BF), pltpu.VMEM((3 * rank, cols), f32)],
        micros=3,
    )
    pair_in = swap(pair_send, "leaf", 1)

    def pair_body(mine, own, sib, seen, send, keep, gram, scratch):
        upper = tree_side(1)
        scratch[...] = (mine[...].astype(f32) + sib[:, : 2 * rank]).astype(BF)
        keep[:, span(0)] = scratch[:, block(upper, rank)]
        keep[:, span(1)] = scratch[:, block(1 - upper, rank)]
        send[:, span(0)] = keep[:, span(1)]
        gram[...] = own[:, span(2)].astype(f32) + sib[:, span(2)]
        send[:, span(1)] = gram[...].astype(BF)

    next_send, next_keep, gram_pair = call(
        pair_body,
        [((rank, 2 * rank), BF), ((rank, 2 * rank), BF), (square, f32)],
        early_keep,
        early,
        early_sib,
        state1,
        scratch=[pltpu.VMEM((rank, 2 * rank), BF)],
        micros=1,
    )
    next_far = swap(next_send, "leaf", 3)
    def half_body(keep, pair, nexts, send, keep2):
        send[:, :cols] = (keep[:, :cols] + pair[:, :cols]).astype(BF)
        keep2[...] = keep[:, cols:] + pair[:, cols:] - dot(nexts[:, span(0)], send[:, :cols])
        send[:, cols:] = keep2[...].astype(BF)

    cross_send, cross_keep = call(
        half_body,
        [((rank, 2 * cols), BF), (wide, f32)],
        pair_keep,
        pair_in,
        next_keep,
        micros=5,
    )
    cross_in = swap(cross_send, "leaf", 3)

    def turn_body(gram, far, caps, seen, out):
        whole = (gram[...] + far[:, span(1)]).astype(BF)
        out[...] = dot(whole, caps[...]).astype(BF)

    (turn,) = call(
        turn_body, [(top_caps.shape, BF)], gram_pair, next_far, top_caps, cross_send, micros=0.1
    )
    turn_far = swap(turn, "top", 2)
    turn_near = swap(turn, "top", 1)
    def late_body(lb, rb, caps, tl, tr, seen, seen2, out):
        for i, basis in enumerate((tl[0], tr[0])):
            out[:, span(i)] = (dot_t(lb[0, 0], basis) * s1).astype(BF)
            out[:, span(4 + i)] = (dot_t(lb[1, 0], basis) * s2).astype(BF)
        gram = (dot_t(lb[0, 0], rb[1, 0]) * s1).astype(BF)
        out[:, span(2, 2)] = dot(gram, caps[1, 0]).astype(BF)

    (late,) = call(
        late_body,
        [((rank, 6 * rank), BF)],
        lb,
        rb,
        caps,
        tl,
        tr,
        cross_send,
        next_far,
        micros=5,
    )

    late_sib = swap(late, "leaf", 1)

    def column_body(send, keep2, far, nexts, nexts_far, seen, out):
        out[...] = (
            keep2[...]
            + far[:, cols:]
            - dot(nexts[:, span(1)], far[:, :cols])
            - dot(nexts_far[:, span(0)], send[:, :cols])
        ).astype(BF)

    (top_send,) = call(
        column_body,
        [(wide, BF)],
        cross_send,
        cross_keep,
        cross_in,
        next_keep,
        next_far,
        late,
        micros=0.2,
    )
    top_far = swap(top_send, "top", 2)

    def two_body(x1, send, far, lb, caps, seen, x2, z5, z, stack):
        put_rows(stack, tree_side(1), send[:, :cols], far[:, :cols])
        coef = dot(caps[1, 0], stack[...]).astype(BF)
        x2[...] = (x1[...] - dot(lb[1, 0], coef)).astype(BF)
        z5[...] = dot_t(lb[1, 0], x2[...]) * s2
        z[:, :cols] = z5[...].astype(BF)
        z[:, cols:] = (dot_t(lb[0, 0], x2[...]) * s1).astype(BF)

    state2, down5, down_send = call(
        two_body,
        [(tall, BF), (wide, f32), ((rank, 2 * cols), BF)],
        state1,
        cross_send,
        cross_in,
        lb,
        caps,
        top_send,
        scratch=[pltpu.VMEM((2 * rank, cols), BF)],
        micros=0.1,
    )
    down_in = swap(down_send, "leaf", 1)
    top_near = swap(after(top_send, state2), "top", 1)
    top_parts = top_send, top_near, top_far, swap(top_far, "top", 1)

    turn_far_near = swap(after(turn_far, top_far), "top", 1)

    def order_body(a, b, c, d, caps, out, row):
        here = lax.axis_index("top")
        for k in range(4):
            for i, piece in enumerate((a, b, c, d)):
                out[span(i), span(k)] = piece[:, block(here ^ k, rank)]
            row[:, span(k)] = caps[:, block(here ^ k, rank)]

    turn_all, caps_row = call(
        order_body,
        [((4 * rank, 4 * rank), BF), ((rank, 4 * rank), BF)],
        turn,
        turn_near,
        turn_far,
        turn_far_near,
        top_caps,
        micros=0.1,
    )

    def under_body(x2, rb, tl, tr, inv, seen, out2, under):
        for c in range(blocks):
            column = inv[c * rank :, span(c)]
            out2[span(c), :] = dot_t(column, x2[c * rank :, :])
            for i, basis in enumerate((tl[0], tr[0], rb[1, 0], rb[0, 0])):
                under[span(c), span(i)] = dot_t(column, basis[c * rank :, :]).astype(BF)

    out2, under = call(
        under_body,
        [(tall, f32), ((rows, 4 * rank), BF)],
        state2,
        rb,
        tl,
        tr,
        inverse,
        late_sib,
        micros=3,
    )

    def top_body(a, b, c, d, turns, row, seen, out, up):
        for i, piece in enumerate((a, b, c, d)):
            up[span(i), :] = piece[...]
        turned = dot(turns[...], up[...]).astype(BF)
        out[:, :cols] = dot(row[...], up[...]).astype(BF)
        out[:, cols:] = dot(row[...], turned).astype(BF)

    (back_send,) = call(
        top_body,
        [((rank, 2 * cols), BF)],
        *top_parts,
        turn_all,
        caps_row,
        out2,
        scratch=[pltpu.VMEM((4 * rank, cols), BF)],
        micros=1,
    )
    back_in = swap(back_send, "leaf", 1)

    def down_body(back, back_sib, down5, z_sib, late, late_sib, both, send, pieces):
        side = column_side()
        pieces[side] = back[...]
        pieces[1 - side] = back_sib[...]
        both[span(0), :] = pieces[0, :, :cols]
        both[span(1), :] = (pieces[1, :, :cols].astype(f32) - pieces[0, :, cols:]).astype(BF)
        gram = (late[:, span(4, 2)].astype(f32) + late_sib[:, span(4, 2)]).astype(BF)
        send[...] = (down5[...] + z_sib[:, :cols] - dot(gram, both[...])).astype(BF)

    both, half5 = call(
        down_body,
        [((2 * rank, cols), BF), (wide, BF)],
        back_send,
        back_in,
        down5,
        down_in,
        late,
        late_sib,
        scratch=[pltpu.VMEM((2, rank, 2 * cols), BF)],
        micros=0.3,
    )
    half5_far = swap(half5, "leaf", 3)

    def part_body(out2, under, both, z, z_sib, late, late_sib, seen, proj, out3):
        def down(zs, gram):
            return zs[:, cols:] - dot(gram[:, span(0, 2)], both[...])

        put_rows(proj, tree_side(0), down(z, late), down(z_sib, late_sib))
        out3[...] = out2[...] - dot(under[:, span(0, 2)], both[...])

    proj6, out3 = call(
        part_body,
        [((2 * rank, cols), f32), (tall, f32)],
        out2,
        under,
        both,
        down_send,
        down_in,
        late,
        late_sib,
        half5,
        micros=0.3,
    )

    def last_body(
        out3, under, half5, half5_far, late, late_sib, proj6, caps, out,
        coefs, stack, grams, out_v, sems,
    ):
        put_rows(stack, tree_side(1), half5[...], half5_far[...])
        put_rows(grams, tree_side(0), late[:, span(2, 2)], late_sib[:, span(2, 2)])
        proj = (proj6[...] - dot(grams[...], stack[...])).astype(BF)
        coefs[span(0), :] = dot(caps[1, 0], stack[...]).astype(BF)
        coefs[span(1), :] = dot(caps[0, 0], proj).astype(BF)
        copies = []
        for c in range(blocks):
            out_v[span(c), :] = out3[span(c), :] - dot(under[span(c), span(2, 2)], coefs[...])
            copy = pltpu.make_async_copy(out_v.at[span(c), :], out.at[0, span(c), :], sems.at[c])
            copy.start()
            copies.append(copy)
        for copy in copies:
            copy.wait()

    (out,) = call(
        last_body,
        [((1, rows, cols), f32)],
        out3,
        under,
        half5,
        half5_far,
        late,
        late_sib,
        proj6,
        caps,
        hbm_out=True,
        scratch=[
            pltpu.VMEM((2 * rank, cols), BF),
            pltpu.VMEM((2 * rank, cols), BF),
            pltpu.VMEM((2 * rank, 2 * rank), BF),
            pltpu.VMEM(tall, f32),
            pltpu.SemaphoreType.DMA((blocks,)),
        ],
    )
    return out


def on_device(*args):
    levels = args[2].shape[0]
    sizes = lax.axis_size("leaf"), lax.axis_size("top")
    if levels == 2 and sizes == (4, 4):
        return two_levels(*args)
    return step_by_step(*args)


def solution(mesh):
    rows = P(("parts", "top"), "leaf", None)
    level_rows = P(None, ("parts", "top"), "leaf", None)
    return jax.shard_map(
        on_device,
        mesh=mesh,
        in_specs=(
            rows,
            rows,
            level_rows,
            level_rows,
            level_rows,
            rows,
            rows,
            P(("parts", "top"), None),
        ),
        out_specs=rows,
        check_vma=False,
    )
```

```python
import math

import jax
import jax.numpy as jnp
from jax import lax
from jax.experimental import pallas as pl
from jax.experimental.pallas import tpu as pltpu
from jax.sharding import PartitionSpec as P

BF = jnp.bfloat16
VMEM_LIMIT = 8 * 2**20
FLOPS_PER_MICRO = 1e9


def swap(value, axis, mask):
    pairs = [(source, source ^ mask) for source in range(lax.axis_size(axis))]
    return lax.ppermute(value, axis, pairs)


def dot(a, b):
    return jnp.dot(a, b, preferred_element_type=jnp.float32)


def dot_t(a, b):
    return lax.dot_general(a, b, (((0,), (0,)), ((), ())), preferred_element_type=jnp.float32)


def ordered(upper_side, own, other):
    return jnp.where(
        upper_side, jnp.concatenate([other, own], 0), jnp.concatenate([own, other], 0)
    )


def level_step(current, project_basis, update_basis, caps_rows, level_num):
    leaf_rows = current.shape[0]
    shift_bits = level_num - 1
    partial_value = dot_t(project_basis, current.astype(BF)) * (
        1.0 / math.sqrt(leaf_rows * 2**shift_bits)
    )
    for bit_index in range(shift_bits):
        partial_value = partial_value + swap(partial_value, "leaf", 2**bit_index)
    own = partial_value.astype(BF)
    other = swap(own, "leaf", 2**shift_bits)
    upper_side = (lax.axis_index("leaf") >> shift_bits) & 1 == 1
    stacked = ordered(upper_side, own, other)
    weights = dot(caps_rows, stacked).astype(BF)
    return current - dot(update_basis, weights)


def top_step(current, project_basis, update_basis, caps_rows):
    leaf_count = lax.axis_size("leaf")
    partial_value = dot_t(project_basis, current.astype(BF)) * (
        1.0 / math.sqrt(leaf_count * current.shape[0])
    )
    column_total = lax.psum(partial_value, "leaf")
    stacked = lax.all_gather(column_total.astype(BF), "top", axis=0, tiled=True)
    weights = dot(caps_rows, stacked).astype(BF)
    return current - dot(update_basis, weights)


def step_by_step(
    right_side, leaf_inverse, left_basis, right_basis, level_caps, top_left, top_right, top_caps
):
    levels = left_basis.shape[0]
    lefts = [left_basis[k, 0] for k in range(levels)]
    rights = [right_basis[k, 0] for k in range(levels)]
    current = dot(leaf_inverse[0], right_side[0].astype(BF))
    for k in range(levels):
        current = level_step(current, rights[k], lefts[k], level_caps[k, 0], k + 1)
    current = top_step(current, top_right[0], top_left[0], top_caps)
    current = top_step(current, top_left[0], top_right[0], top_caps)
    for k in reversed(range(levels)):
        current = level_step(current, lefts[k], rights[k], level_caps[k, 0], k + 1)
    return dot_t(leaf_inverse[0], current.astype(BF))[None]


def in_hbm(value):
    return pltpu.with_memory_space_constraint(value, pltpu.HBM)


def in_vmem(value):
    return pltpu.with_memory_space_constraint(value, pltpu.VMEM)


def call(body, outs, *args, scratch=(), hbm=(), hbm_out=False, micros=1):
    vmem = pl.BlockSpec(memory_space=pltpu.VMEM)
    anywhere = pl.BlockSpec(memory_space=pl.ANY)
    return pl.pallas_call(
        body,
        out_shape=[
            jax.ShapeDtypeStruct(shape, dtype) if hbm_out else pltpu.VMEM(shape, dtype)
            for shape, dtype in outs
        ],
        in_specs=[anywhere if i in hbm else vmem for i in range(len(args))],
        out_specs=[anywhere if hbm_out else vmem] * len(outs),
        scratch_shapes=list(scratch),
        compiler_params=pltpu.CompilerParams(vmem_limit_bytes=VMEM_LIMIT),
        cost_estimate=pl.CostEstimate(
            flops=int(micros * FLOPS_PER_MICRO), bytes_accessed=0, transcendentals=0
        ),
    )(*[in_hbm(a) if i in hbm else in_vmem(a) for i, a in enumerate(args)])


def after(value, *others):
    return lax.optimization_barrier((value, *others))[0]


def tree_side(bit):
    return (lax.axis_index("leaf") >> bit) & 1


def column_side():
    leaf = lax.axis_index("leaf")
    return (leaf ^ (leaf >> 1)) & 1


def block(index, width):
    return pl.ds(pl.multiple_of(index * width, width), width)


def put_rows(scratch, upper, own, other):
    rows = own.shape[0]
    scratch[block(upper, rows), :] = own
    scratch[block(1 - upper, rows), :] = other


def two_levels(
    right_side, leaf_inverse, left_basis, right_basis, level_caps, top_left, top_right, top_caps
):
    rows, cols = right_side.shape[1:]
    rank = top_left.shape[2]
    f32 = jnp.float32
    s1 = 1.0 / math.sqrt(rows)
    s2 = 1.0 / math.sqrt(rows * 2)
    st = 1.0 / math.sqrt(rows * 4)
    blocks = rows // rank
    square, wide, tall = (rank, rank), (rank, cols), (rows, cols)

    def span(i, n=1):
        return slice(i * rank, (i + n) * rank)

    def start_body(
        rhs_hbm, inv_hbm, lb_hbm, rb_hbm, caps_hbm, tl_hbm, tr_hbm,
        x_ref, send, inv_ref, lb, rb, caps, tl, tr, rhs_v, basis_t, sems,
    ):
        def load(source, target, *at):
            copy = pltpu.make_async_copy(source, target, sems.at[at])
            copy.start()
            return copy

        first = load(rb_hbm.at[0], rb.at[0], 2, 0)
        groups = [(i, min(2, blocks - i)) for i in range(0, blocks, 2)]
        copies = []
        for i, n in groups:
            copies.append(load(rhs_hbm.at[0, span(i, n), :], rhs_v.at[span(i, n), :], 0, i))
            copies.append(
                load(
                    inv_hbm.at[0, span(i, n), span(0, i + n)],
                    inv_ref.at[span(i, n), span(0, i + n)],
                    1,
                    i,
                )
            )
        pairs = (rb_hbm.at[1], rb.at[1]), (lb_hbm, lb), (tl_hbm, tl), (tr_hbm, tr), (caps_hbm, caps)
        bases = [load(source, target, 2, 1 + i) for i, (source, target) in enumerate(pairs)]
        first.wait()
        basis_t[...] = rb[0, 0].T
        for i, n in groups:
            copies[i].wait()
            copies[i + 1].wait()
            x_ref[span(i, n), :] = dot(
                inv_ref[span(i, n), span(0, i + n)], rhs_v[span(0, i + n), :].astype(BF)
            )
        send[...] = (dot(basis_t[...], x_ref[...].astype(BF)) * s1).astype(BF)
        for copy in bases:
            copy.wait()

    state0, proj1, inverse, lb, rb, caps, tl, tr = call(
        start_body,
        [(tall, f32), (wide, BF), ((rows, rows), BF)]
        + [(a.shape, a.dtype) for a in (left_basis, right_basis, level_caps, top_left, top_right)],
        right_side,
        leaf_inverse,
        left_basis,
        right_basis,
        level_caps,
        top_left,
        top_right,
        hbm=range(7),
        scratch=[
            pltpu.VMEM(tall, f32),
            pltpu.VMEM((rank, rows), BF),
            pltpu.SemaphoreType.DMA((3, max(blocks, 6))),
        ],
    )
    proj1_sib = swap(proj1, "leaf", 1)
    proj1_near = swap(proj1, "top", 1)

    def early_body(lb, caps, tl, tr, seen, send, keep, scratch):
        side = column_side()
        for i, basis in enumerate((tr, tl)):
            gram = (dot_t(basis[0], lb[1, 0]) * st).astype(BF)
            scratch[i] = dot(gram, caps[1, 0]).astype(BF)
        send[:, : 2 * rank] = scratch[1 - side]
        send[:, span(2)] = (dot_t(tl[0], tl[0]) * st).astype(BF)
        keep[...] = scratch[side]

    early, early_keep = call(
        early_body,
        [((rank, 3 * rank), BF), ((rank, 2 * rank), BF)],
        lb,
        caps,
        tl,
        tr,
        proj1_near,
        scratch=[pltpu.VMEM((2, rank, 2 * rank), BF)],
        micros=10,
    )
    early_sib = swap(early, "leaf", 1)

    def flip_body(lb, rb, tl, tr, seen, out, out2):
        for i, basis in enumerate((rb[1, 0], tr[0], tl[0])):
            out[span(i), :] = basis.T
        for i, basis in enumerate((lb[1, 0], lb[0, 0])):
            out2[span(i), :] = basis.T

    bases_t, lefts_t = call(
        flip_body,
        [((3 * rank, rows), BF), ((2 * rank, rows), BF)],
        lb,
        rb,
        tl,
        tr,
        early,
        micros=0.2,
    )

    def one_body(x0, p, p_sib, lb, caps, bases_t, x1, send, keep, stack, seen):
        side = column_side()
        put_rows(stack, tree_side(0), p[...], p_sib[...])
        coef = dot(caps[0, 0], stack[...]).astype(BF)
        x1[...] = x0[...] - dot(lb[0, 0], coef)
        seen[...] = dot(bases_t[...], x1[...].astype(BF))
        keep[:, :cols] = seen[span(0), :] * s2
        send[:, :cols] = keep[:, :cols].astype(BF)
        send[:, cols:] = (seen[block(2 - side, rank), :] * st).astype(BF)
        keep[:, cols:] = seen[block(1 + side, rank), :] * st

    state1, pair_send, pair_keep = call(
        one_body,
        [(tall, f32), ((rank, 2 * cols), BF), ((rank, 2 * cols), f32)],
        state0,
        proj1,
        proj1_sib,
        lb,
        caps,
        bases_t,
        scratch=[pltpu.VMEM((2 * rank, cols), BF), pltpu.VMEM((3 * rank, cols), f32)],
        micros=3,
    )
    pair_in = swap(pair_send, "leaf", 1)

    def pair_body(mine, own, sib, seen, send, keep, gram, scratch):
        upper = tree_side(1)
        scratch[...] = (mine[...].astype(f32) + sib[:, : 2 * rank]).astype(BF)
        keep[:, span(0)] = scratch[:, block(upper, rank)]
        keep[:, span(1)] = scratch[:, block(1 - upper, rank)]
        send[:, span(0)] = keep[:, span(1)]
        gram[...] = own[:, span(2)].astype(f32) + sib[:, span(2)]
        send[:, span(1)] = gram[...].astype(BF)

    next_send, next_keep, gram_pair = call(
        pair_body,
        [((rank, 2 * rank), BF), ((rank, 2 * rank), BF), (square, f32)],
        early_keep,
        early,
        early_sib,
        state1,
        scratch=[pltpu.VMEM((rank, 2 * rank), BF)],
        micros=1,
    )
    next_far = swap(next_send, "leaf", 3)
    def half_body(keep, pair, nexts, send, keep2):
        send[:, :cols] = (keep[:, :cols] + pair[:, :cols]).astype(BF)
        keep2[...] = keep[:, cols:] + pair[:, cols:] - dot(nexts[:, span(0)], send[:, :cols])
        send[:, cols:] = keep2[...].astype(BF)

    cross_send, cross_keep = call(
        half_body,
        [((rank, 2 * cols), BF), (wide, f32)],
        pair_keep,
        pair_in,
        next_keep,
        micros=5,
    )
    cross_in = swap(cross_send, "leaf", 3)

    def turn_body(gram, far, caps, seen, out):
        whole = (gram[...] + far[:, span(1)]).astype(BF)
        out[...] = dot(whole, caps[...]).astype(BF)

    (turn,) = call(
        turn_body, [(top_caps.shape, BF)], gram_pair, next_far, top_caps, cross_send, micros=0.1
    )
    turn_far = swap(turn, "top", 2)
    turn_near = swap(turn, "top", 1)
    def late_body(lb, rb, caps, tl, tr, seen, seen2, out):
        for i, basis in enumerate((tl[0], tr[0])):
            out[:, span(i)] = (dot_t(lb[0, 0], basis) * s1).astype(BF)
            out[:, span(4 + i)] = (dot_t(lb[1, 0], basis) * s2).astype(BF)
        gram = (dot_t(lb[0, 0], rb[1, 0]) * s1).astype(BF)
        out[:, span(2, 2)] = dot(gram, caps[1, 0]).astype(BF)

    (late,) = call(
        late_body,
        [((rank, 6 * rank), BF)],
        lb,
        rb,
        caps,
        tl,
        tr,
        cross_send,
        next_far,
        micros=5,
    )

    late_sib = swap(late, "leaf", 1)

    def column_body(send, keep2, far, nexts, nexts_far, seen, out):
        out[...] = (
            keep2[...]
            + far[:, cols:]
            - dot(nexts[:, span(1)], far[:, :cols])
            - dot(nexts_far[:, span(0)], send[:, :cols])
        ).astype(BF)

    (top_send,) = call(
        column_body,
        [(wide, BF)],
        cross_send,
        cross_keep,
        cross_in,
        next_keep,
        next_far,
        late,
        micros=0.2,
    )
    top_far = swap(top_send, "top", 2)

    def two_body(x1, send, far, lb, caps, lefts_t, seen, x2, z5, z, stack, both):
        put_rows(stack, tree_side(1), send[:, :cols], far[:, :cols])
        coef = dot(caps[1, 0], stack[...]).astype(BF)
        x2[...] = (x1[...] - dot(lb[1, 0], coef)).astype(BF)
        both[...] = dot(lefts_t[...], x2[...])
        z5[...] = both[span(0), :] * s2
        z[:, :cols] = z5[...].astype(BF)
        z[:, cols:] = (both[span(1), :] * s1).astype(BF)

    state2, down5, down_send = call(
        two_body,
        [(tall, BF), (wide, f32), ((rank, 2 * cols), BF)],
        state1,
        cross_send,
        cross_in,
        lb,
        caps,
        lefts_t,
        top_send,
        scratch=[pltpu.VMEM((2 * rank, cols), BF), pltpu.VMEM((2 * rank, cols), f32)],
        micros=0.1,
    )
    down_in = swap(down_send, "leaf", 1)
    top_near = swap(after(top_send, state2), "top", 1)
    top_parts = top_send, top_near, top_far, swap(top_far, "top", 1)

    turn_far_near = swap(after(turn_far, top_far), "top", 1)

    def order_body(a, b, c, d, caps, out, row):
        here = lax.axis_index("top")
        for k in range(4):
            for i, piece in enumerate((a, b, c, d)):
                out[span(i), span(k)] = piece[:, block(here ^ k, rank)]
            row[:, span(k)] = caps[:, block(here ^ k, rank)]

    turn_all, caps_row = call(
        order_body,
        [((4 * rank, 4 * rank), BF), ((rank, 4 * rank), BF)],
        turn,
        turn_near,
        turn_far,
        turn_far_near,
        top_caps,
        micros=0.1,
    )

    def under_body(x2, rb, tl, tr, inv, seen, out2, under):
        for c in range(blocks):
            column = inv[c * rank :, span(c)]
            out2[span(c), :] = dot_t(column, x2[c * rank :, :])
            for i, basis in enumerate((tl[0], tr[0], rb[1, 0], rb[0, 0])):
                under[span(c), span(i)] = dot_t(column, basis[c * rank :, :]).astype(BF)

    out2, under = call(
        under_body,
        [(tall, f32), ((rows, 4 * rank), BF)],
        state2,
        rb,
        tl,
        tr,
        inverse,
        late_sib,
        micros=3,
    )

    def top_body(a, b, c, d, turns, row, seen, out, up):
        for i, piece in enumerate((a, b, c, d)):
            up[span(i), :] = piece[...]
        turned = dot(turns[...], up[...]).astype(BF)
        out[:, :cols] = dot(row[...], up[...]).astype(BF)
        out[:, cols:] = dot(row[...], turned).astype(BF)

    (back_send,) = call(
        top_body,
        [((rank, 2 * cols), BF)],
        *top_parts,
        turn_all,
        caps_row,
        out2,
        scratch=[pltpu.VMEM((4 * rank, cols), BF)],
        micros=1,
    )
    back_in = swap(back_send, "leaf", 1)

    def down_body(back, back_sib, down5, z_sib, late, late_sib, both, send, pieces):
        side = column_side()
        pieces[side] = back[...]
        pieces[1 - side] = back_sib[...]
        both[span(0), :] = pieces[0, :, :cols]
        both[span(1), :] = (pieces[1, :, :cols].astype(f32) - pieces[0, :, cols:]).astype(BF)
        gram = (late[:, span(4, 2)].astype(f32) + late_sib[:, span(4, 2)]).astype(BF)
        send[...] = (down5[...] + z_sib[:, :cols] - dot(gram, both[...])).astype(BF)

    both, half5 = call(
        down_body,
        [((2 * rank, cols), BF), (wide, BF)],
        back_send,
        back_in,
        down5,
        down_in,
        late,
        late_sib,
        scratch=[pltpu.VMEM((2, rank, 2 * cols), BF)],
        micros=0.3,
    )
    half5_far = swap(half5, "leaf", 3)

    def part_body(out2, under, both, z, z_sib, late, late_sib, seen, proj, out3):
        def down(zs, gram):
            return zs[:, cols:] - dot(gram[:, span(0, 2)], both[...])

        put_rows(proj, tree_side(0), down(z, late), down(z_sib, late_sib))
        out3[...] = out2[...] - dot(under[:, span(0, 2)], both[...])

    proj6, out3 = call(
        part_body,
        [((2 * rank, cols), f32), (tall, f32)],
        out2,
        under,
        both,
        down_send,
        down_in,
        late,
        late_sib,
        half5,
        micros=0.3,
    )

    def last_body(
        out3, under, half5, half5_far, late, late_sib, proj6, caps, out,
        coefs, stack, grams, out_v, sems,
    ):
        put_rows(stack, tree_side(1), half5[...], half5_far[...])
        put_rows(grams, tree_side(0), late[:, span(2, 2)], late_sib[:, span(2, 2)])
        proj = (proj6[...] - dot(grams[...], stack[...])).astype(BF)
        coefs[span(0), :] = dot(caps[1, 0], stack[...]).astype(BF)
        coefs[span(1), :] = dot(caps[0, 0], proj).astype(BF)
        copies = []
        for c in range(blocks):
            out_v[span(c), :] = out3[span(c), :] - dot(under[span(c), span(2, 2)], coefs[...])
            copy = pltpu.make_async_copy(out_v.at[span(c), :], out.at[0, span(c), :], sems.at[c])
            copy.start()
            copies.append(copy)
        for copy in copies:
            copy.wait()

    (out,) = call(
        last_body,
        [((1, rows, cols), f32)],
        out3,
        under,
        half5,
        half5_far,
        late,
        late_sib,
        proj6,
        caps,
        hbm_out=True,
        scratch=[
            pltpu.VMEM((2 * rank, cols), BF),
            pltpu.VMEM((2 * rank, cols), BF),
            pltpu.VMEM((2 * rank, 2 * rank), BF),
            pltpu.VMEM(tall, f32),
            pltpu.SemaphoreType.DMA((blocks,)),
        ],
    )
    return out


def on_device(*args):
    levels = args[2].shape[0]
    sizes = lax.axis_size("leaf"), lax.axis_size("top")
    if levels == 2 and sizes == (4, 4):
        return two_levels(*args)
    return step_by_step(*args)


def solution(mesh):
    rows = P(("parts", "top"), "leaf", None)
    level_rows = P(None, ("parts", "top"), "leaf", None)
    return jax.shard_map(
        on_device,
        mesh=mesh,
        in_specs=(
            rows,
            rows,
            level_rows,
            level_rows,
            level_rows,
            rows,
            rows,
            P(("parts", "top"), None),
        ),
        out_specs=rows,
        check_vma=False,
    )
```

```python
import math

import jax
import jax.numpy as jnp
from jax import lax
from jax.experimental import pallas as pl
from jax.experimental.pallas import tpu as pltpu
from jax.sharding import PartitionSpec as P

BF = jnp.bfloat16
VMEM_LIMIT = 8 * 2**20
FLOPS_PER_MICRO = 1e9


def swap(value, axis, mask):
    pairs = [(source, source ^ mask) for source in range(lax.axis_size(axis))]
    return lax.ppermute(value, axis, pairs)


def dot(a, b):
    return jnp.dot(a, b, preferred_element_type=jnp.float32)


def dot_t(a, b):
    return lax.dot_general(a, b, (((0,), (0,)), ((), ())), preferred_element_type=jnp.float32)


def ordered(upper_side, own, other):
    return jnp.where(
        upper_side, jnp.concatenate([other, own], 0), jnp.concatenate([own, other], 0)
    )


def level_step(current, project_basis, update_basis, caps_rows, level_num):
    leaf_rows = current.shape[0]
    shift_bits = level_num - 1
    partial_value = dot_t(project_basis, current.astype(BF)) * (
        1.0 / math.sqrt(leaf_rows * 2**shift_bits)
    )
    for bit_index in range(shift_bits):
        partial_value = partial_value + swap(partial_value, "leaf", 2**bit_index)
    own = partial_value.astype(BF)
    other = swap(own, "leaf", 2**shift_bits)
    upper_side = (lax.axis_index("leaf") >> shift_bits) & 1 == 1
    stacked = ordered(upper_side, own, other)
    weights = dot(caps_rows, stacked).astype(BF)
    return current - dot(update_basis, weights)


def top_step(current, project_basis, update_basis, caps_rows):
    leaf_count = lax.axis_size("leaf")
    partial_value = dot_t(project_basis, current.astype(BF)) * (
        1.0 / math.sqrt(leaf_count * current.shape[0])
    )
    column_total = lax.psum(partial_value, "leaf")
    stacked = lax.all_gather(column_total.astype(BF), "top", axis=0, tiled=True)
    weights = dot(caps_rows, stacked).astype(BF)
    return current - dot(update_basis, weights)


def step_by_step(
    right_side, leaf_inverse, left_basis, right_basis, level_caps, top_left, top_right, top_caps
):
    levels = left_basis.shape[0]
    lefts = [left_basis[k, 0] for k in range(levels)]
    rights = [right_basis[k, 0] for k in range(levels)]
    current = dot(leaf_inverse[0], right_side[0].astype(BF))
    for k in range(levels):
        current = level_step(current, rights[k], lefts[k], level_caps[k, 0], k + 1)
    current = top_step(current, top_right[0], top_left[0], top_caps)
    current = top_step(current, top_left[0], top_right[0], top_caps)
    for k in reversed(range(levels)):
        current = level_step(current, lefts[k], rights[k], level_caps[k, 0], k + 1)
    return dot_t(leaf_inverse[0], current.astype(BF))[None]


def in_hbm(value):
    return pltpu.with_memory_space_constraint(value, pltpu.HBM)


def in_vmem(value):
    return pltpu.with_memory_space_constraint(value, pltpu.VMEM)


def call(body, outs, *args, scratch=(), hbm=(), hbm_out=False, micros=1):
    vmem = pl.BlockSpec(memory_space=pltpu.VMEM)
    anywhere = pl.BlockSpec(memory_space=pl.ANY)
    return pl.pallas_call(
        body,
        out_shape=[
            jax.ShapeDtypeStruct(shape, dtype) if hbm_out else pltpu.VMEM(shape, dtype)
            for shape, dtype in outs
        ],
        in_specs=[anywhere if i in hbm else vmem for i in range(len(args))],
        out_specs=[anywhere if hbm_out else vmem] * len(outs),
        scratch_shapes=list(scratch),
        compiler_params=pltpu.CompilerParams(vmem_limit_bytes=VMEM_LIMIT),
        cost_estimate=pl.CostEstimate(
            flops=int(micros * FLOPS_PER_MICRO), bytes_accessed=0, transcendentals=0
        ),
    )(*[in_hbm(a) if i in hbm else in_vmem(a) for i, a in enumerate(args)])


def after(value, *others):
    return lax.optimization_barrier((value, *others))[0]


def tree_side(bit):
    return (lax.axis_index("leaf") >> bit) & 1


def column_side():
    leaf = lax.axis_index("leaf")
    return (leaf ^ (leaf >> 1)) & 1


def block(index, width):
    return pl.ds(pl.multiple_of(index * width, width), width)


def put_rows(scratch, upper, own, other):
    rows = own.shape[0]
    scratch[block(upper, rows), :] = own
    scratch[block(1 - upper, rows), :] = other


def two_levels(
    right_side, leaf_inverse, left_basis, right_basis, level_caps, top_left, top_right, top_caps
):
    rows, cols = right_side.shape[1:]
    rank = top_left.shape[2]
    f32 = jnp.float32
    s1 = 1.0 / math.sqrt(rows)
    s2 = 1.0 / math.sqrt(rows * 2)
    st = 1.0 / math.sqrt(rows * 4)
    blocks = rows // rank
    upper = (blocks + 1) // 2
    groups = [(i, n) for i, n in ((0, upper), (upper, blocks - upper)) if n]
    square, wide, tall = (rank, rank), (rank, cols), (rows, cols)

    def span(i, n=1):
        return slice(i * rank, (i + n) * rank)

    def start_body(
        rhs_hbm, inv_hbm, lb_hbm, rb_hbm, caps_hbm, tl_hbm, tr_hbm,
        x_ref, send, inv_ref, lb, rb, caps, tl, tr, rhs_v, basis_t, sems,
    ):
        def load(source, target, *at):
            copy = pltpu.make_async_copy(source, target, sems.at[at])
            copy.start()
            return copy

        first = load(rb_hbm.at[0], rb.at[0], 2, 0)
        copies = []
        for i, n in groups:
            copies.append(load(rhs_hbm.at[0, span(i, n), :], rhs_v.at[span(i, n), :], 0, i))
            copies.append(
                load(
                    inv_hbm.at[0, span(i, n), span(0, i + n)],
                    inv_ref.at[span(i, n), span(0, i + n)],
                    1,
                    i,
                )
            )
        pairs = (rb_hbm.at[1], rb.at[1]), (lb_hbm, lb), (tl_hbm, tl), (tr_hbm, tr), (caps_hbm, caps)
        bases = [load(source, target, 2, 1 + i) for i, (source, target) in enumerate(pairs)]
        first.wait()
        basis_t[...] = rb[0, 0].T
        for (i, n), k in zip(groups, range(0, len(copies), 2)):
            copies[k].wait()
            copies[k + 1].wait()
            x_ref[span(i, n), :] = dot(
                inv_ref[span(i, n), span(0, i + n)], rhs_v[span(0, i + n), :].astype(BF)
            )
        send[...] = (dot(basis_t[...], x_ref[...].astype(BF)) * s1).astype(BF)
        for copy in bases:
            copy.wait()

    state0, proj1, inverse, lb, rb, caps, tl, tr = call(
        start_body,
        [(tall, f32), (wide, BF), ((rows, rows), BF)]
        + [(a.shape, a.dtype) for a in (left_basis, right_basis, level_caps, top_left, top_right)],
        right_side,
        leaf_inverse,
        left_basis,
        right_basis,
        level_caps,
        top_left,
        top_right,
        hbm=range(7),
        scratch=[
            pltpu.VMEM(tall, f32),
            pltpu.VMEM((rank, rows), BF),
            pltpu.SemaphoreType.DMA((3, max(blocks, 6))),
        ],
    )
    proj1_sib = swap(proj1, "leaf", 1)
    proj1_near = swap(proj1, "top", 1)

    def early_body(lb, caps, tl, tr, seen, send, keep, scratch):
        side = column_side()
        for i, basis in enumerate((tr, tl)):
            gram = (dot_t(basis[0], lb[1, 0]) * st).astype(BF)
            scratch[i] = dot(gram, caps[1, 0]).astype(BF)
        send[:, : 2 * rank] = scratch[1 - side]
        send[:, span(2)] = (dot_t(tl[0], tl[0]) * st).astype(BF)
        keep[...] = scratch[side]

    early, early_keep = call(
        early_body,
        [((rank, 3 * rank), BF), ((rank, 2 * rank), BF)],
        lb,
        caps,
        tl,
        tr,
        proj1_near,
        scratch=[pltpu.VMEM((2, rank, 2 * rank), BF)],
        micros=10,
    )
    early_sib = swap(early, "leaf", 1)

    def flip_body(lb, rb, tl, tr, seen, out, out2, out3):
        for i, basis in enumerate((rb[1, 0], tr[0], tl[0])):
            out[span(i), :] = basis.T
        for i, basis in enumerate((lb[1, 0], lb[0, 0])):
            out2[span(i), :] = basis.T
        for i, basis in enumerate((tl[0], tr[0], rb[1, 0], rb[0, 0])):
            out3[:, span(i)] = basis

    bases_t, lefts_t, updates = call(
        flip_body,
        [((3 * rank, rows), BF), ((2 * rank, rows), BF), ((rows, 4 * rank), BF)],
        lb,
        rb,
        tl,
        tr,
        early,
        micros=0.2,
    )

    def one_body(x0, p, p_sib, lb, caps, bases_t, x1, send, keep, stack, seen):
        side = column_side()
        put_rows(stack, tree_side(0), p[...], p_sib[...])
        coef = dot(caps[0, 0], stack[...]).astype(BF)
        x1[...] = x0[...] - dot(lb[0, 0], coef)
        seen[...] = dot(bases_t[...], x1[...].astype(BF))
        keep[:, :cols] = seen[span(0), :] * s2
        send[:, :cols] = keep[:, :cols].astype(BF)
        send[:, cols:] = (seen[block(2 - side, rank), :] * st).astype(BF)
        keep[:, cols:] = seen[block(1 + side, rank), :] * st

    state1, pair_send, pair_keep = call(
        one_body,
        [(tall, f32), ((rank, 2 * cols), BF), ((rank, 2 * cols), f32)],
        state0,
        proj1,
        proj1_sib,
        lb,
        caps,
        bases_t,
        scratch=[pltpu.VMEM((2 * rank, cols), BF), pltpu.VMEM((3 * rank, cols), f32)],
        micros=3,
    )
    pair_in = swap(pair_send, "leaf", 1)

    def pair_body(mine, own, sib, seen, send, keep, gram, scratch):
        upper = tree_side(1)
        scratch[...] = (mine[...].astype(f32) + sib[:, : 2 * rank]).astype(BF)
        keep[:, span(0)] = scratch[:, block(upper, rank)]
        keep[:, span(1)] = scratch[:, block(1 - upper, rank)]
        send[:, span(0)] = keep[:, span(1)]
        gram[...] = own[:, span(2)].astype(f32) + sib[:, span(2)]
        send[:, span(1)] = gram[...].astype(BF)

    next_send, next_keep, gram_pair = call(
        pair_body,
        [((rank, 2 * rank), BF), ((rank, 2 * rank), BF), (square, f32)],
        early_keep,
        early,
        early_sib,
        state1,
        scratch=[pltpu.VMEM((rank, 2 * rank), BF)],
        micros=1,
    )
    next_far = swap(next_send, "leaf", 3)
    def half_body(keep, pair, nexts, send, keep2):
        send[:, :cols] = (keep[:, :cols] + pair[:, :cols]).astype(BF)
        keep2[...] = keep[:, cols:] + pair[:, cols:] - dot(nexts[:, span(0)], send[:, :cols])
        send[:, cols:] = keep2[...].astype(BF)

    cross_send, cross_keep = call(
        half_body,
        [((rank, 2 * cols), BF), (wide, f32)],
        pair_keep,
        pair_in,
        next_keep,
        micros=5,
    )
    cross_in = swap(cross_send, "leaf", 3)

    def turn_body(gram, far, caps, seen, out):
        whole = (gram[...] + far[:, span(1)]).astype(BF)
        out[...] = dot(whole, caps[...]).astype(BF)

    (turn,) = call(
        turn_body, [(top_caps.shape, BF)], gram_pair, next_far, top_caps, cross_send, micros=0.1
    )
    turn_far = swap(turn, "top", 2)
    turn_near = swap(turn, "top", 1)
    def late_body(lb, rb, caps, tl, tr, seen, seen2, out):
        for i, basis in enumerate((tl[0], tr[0])):
            out[:, span(i)] = (dot_t(lb[0, 0], basis) * s1).astype(BF)
            out[:, span(4 + i)] = (dot_t(lb[1, 0], basis) * s2).astype(BF)
        gram = (dot_t(lb[0, 0], rb[1, 0]) * s1).astype(BF)
        out[:, span(2, 2)] = dot(gram, caps[1, 0]).astype(BF)

    (late,) = call(
        late_body,
        [((rank, 6 * rank), BF)],
        lb,
        rb,
        caps,
        tl,
        tr,
        cross_send,
        next_far,
        micros=5,
    )

    late_sib = swap(late, "leaf", 1)

    def column_body(send, keep2, far, nexts, nexts_far, seen, out):
        out[...] = (
            keep2[...]
            + far[:, cols:]
            - dot(nexts[:, span(1)], far[:, :cols])
            - dot(nexts_far[:, span(0)], send[:, :cols])
        ).astype(BF)

    (top_send,) = call(
        column_body,
        [(wide, BF)],
        cross_send,
        cross_keep,
        cross_in,
        next_keep,
        next_far,
        late,
        micros=0.2,
    )
    top_far = swap(top_send, "top", 2)

    def two_body(x1, send, far, lb, caps, lefts_t, seen, x2, z5, z, stack, both):
        put_rows(stack, tree_side(1), send[:, :cols], far[:, :cols])
        coef = dot(caps[1, 0], stack[...]).astype(BF)
        x2[...] = (x1[...] - dot(lb[1, 0], coef)).astype(BF)
        both[...] = dot(lefts_t[...], x2[...])
        z5[...] = both[span(0), :] * s2
        z[:, :cols] = z5[...].astype(BF)
        z[:, cols:] = (both[span(1), :] * s1).astype(BF)

    state2, down5, down_send = call(
        two_body,
        [(tall, BF), (wide, f32), ((rank, 2 * cols), BF)],
        state1,
        cross_send,
        cross_in,
        lb,
        caps,
        lefts_t,
        top_send,
        scratch=[pltpu.VMEM((2 * rank, cols), BF), pltpu.VMEM((2 * rank, cols), f32)],
        micros=0.1,
    )
    down_in = swap(down_send, "leaf", 1)
    top_near = swap(after(top_send, state2), "top", 1)
    top_parts = top_send, top_near, top_far, swap(top_far, "top", 1)

    turn_far_near = swap(after(turn_far, top_far), "top", 1)

    def order_body(a, b, c, d, caps, out, row):
        here = lax.axis_index("top")
        for k in range(4):
            for i, piece in enumerate((a, b, c, d)):
                out[span(i), span(k)] = piece[:, block(here ^ k, rank)]
            row[:, span(k)] = caps[:, block(here ^ k, rank)]

    turn_all, caps_row = call(
        order_body,
        [((4 * rank, 4 * rank), BF), ((rank, 4 * rank), BF)],
        turn,
        turn_near,
        turn_far,
        turn_far_near,
        top_caps,
        micros=0.1,
    )

    def under_body(x2, updates, inv, seen, out2, under):
        for i, n in groups:
            column = inv[i * rank :, span(i, n)]
            out2[span(i, n), :] = dot_t(column, x2[i * rank :, :])
            under[span(i, n), :] = dot_t(column, updates[i * rank :, :]).astype(BF)

    out2, under = call(
        under_body,
        [(tall, f32), ((rows, 4 * rank), BF)],
        state2,
        updates,
        inverse,
        late_sib,
        micros=3,
    )

    def top_body(a, b, c, d, turns, row, seen, out, up):
        for i, piece in enumerate((a, b, c, d)):
            up[span(i), :] = piece[...]
        turned = dot(turns[...], up[...]).astype(BF)
        out[:, :cols] = dot(row[...], up[...]).astype(BF)
        out[:, cols:] = dot(row[...], turned).astype(BF)

    (back_send,) = call(
        top_body,
        [((rank, 2 * cols), BF)],
        *top_parts,
        turn_all,
        caps_row,
        out2,
        scratch=[pltpu.VMEM((4 * rank, cols), BF)],
        micros=1,
    )
    back_in = swap(back_send, "leaf", 1)

    def down_body(back, back_sib, down5, z_sib, late, late_sib, both, send, pieces):
        side = column_side()
        pieces[side] = back[...]
        pieces[1 - side] = back_sib[...]
        both[span(0), :] = pieces[0, :, :cols]
        both[span(1), :] = (pieces[1, :, :cols].astype(f32) - pieces[0, :, cols:]).astype(BF)
        gram = (late[:, span(4, 2)].astype(f32) + late_sib[:, span(4, 2)]).astype(BF)
        send[...] = (down5[...] + z_sib[:, :cols] - dot(gram, both[...])).astype(BF)

    both, half5 = call(
        down_body,
        [((2 * rank, cols), BF), (wide, BF)],
        back_send,
        back_in,
        down5,
        down_in,
        late,
        late_sib,
        scratch=[pltpu.VMEM((2, rank, 2 * cols), BF)],
        micros=0.3,
    )
    half5_far = swap(half5, "leaf", 3)

    def part_body(out2, under, both, z, z_sib, late, late_sib, seen, proj, out3):
        def down(zs, gram):
            return zs[:, cols:] - dot(gram[:, span(0, 2)], both[...])

        put_rows(proj, tree_side(0), down(z, late), down(z_sib, late_sib))
        out3[...] = out2[...] - dot(under[:, span(0, 2)], both[...])

    proj6, out3 = call(
        part_body,
        [((2 * rank, cols), f32), (tall, f32)],
        out2,
        under,
        both,
        down_send,
        down_in,
        late,
        late_sib,
        half5,
        micros=0.3,
    )

    def last_body(
        out3, under, half5, half5_far, late, late_sib, proj6, caps, out,
        coefs, stack, grams, out_v, sems,
    ):
        put_rows(stack, tree_side(1), half5[...], half5_far[...])
        put_rows(grams, tree_side(0), late[:, span(2, 2)], late_sib[:, span(2, 2)])
        proj = (proj6[...] - dot(grams[...], stack[...])).astype(BF)
        coefs[span(0), :] = dot(caps[1, 0], stack[...]).astype(BF)
        coefs[span(1), :] = dot(caps[0, 0], proj).astype(BF)
        copies = []
        for c in range(blocks):
            out_v[span(c), :] = out3[span(c), :] - dot(under[span(c), span(2, 2)], coefs[...])
            copy = pltpu.make_async_copy(out_v.at[span(c), :], out.at[0, span(c), :], sems.at[c])
            copy.start()
            copies.append(copy)
        for copy in copies:
            copy.wait()

    (out,) = call(
        last_body,
        [((1, rows, cols), f32)],
        out3,
        under,
        half5,
        half5_far,
        late,
        late_sib,
        proj6,
        caps,
        hbm_out=True,
        scratch=[
            pltpu.VMEM((2 * rank, cols), BF),
            pltpu.VMEM((2 * rank, cols), BF),
            pltpu.VMEM((2 * rank, 2 * rank), BF),
            pltpu.VMEM(tall, f32),
            pltpu.SemaphoreType.DMA((blocks,)),
        ],
    )
    return out


def on_device(*args):
    levels = args[2].shape[0]
    sizes = lax.axis_size("leaf"), lax.axis_size("top")
    if levels == 2 and sizes == (4, 4):
        return two_levels(*args)
    return step_by_step(*args)


def solution(mesh):
    rows = P(("parts", "top"), "leaf", None)
    level_rows = P(None, ("parts", "top"), "leaf", None)
    return jax.shard_map(
        on_device,
        mesh=mesh,
        in_specs=(
            rows,
            rows,
            level_rows,
            level_rows,
            level_rows,
            rows,
            rows,
            P(("parts", "top"), None),
        ),
        out_specs=rows,
        check_vma=False,
    )
```

```python
import math

import jax
import jax.numpy as jnp
from jax import lax
from jax.experimental import pallas as pl
from jax.experimental.pallas import tpu as pltpu
from jax.sharding import PartitionSpec as P

BF = jnp.bfloat16
VMEM_LIMIT = 8 * 2**20
FLOPS_PER_MICRO = 1e9


def swap(value, axis, mask):
    pairs = [(source, source ^ mask) for source in range(lax.axis_size(axis))]
    return lax.ppermute(value, axis, pairs)


def dot(a, b):
    return jnp.dot(a, b, preferred_element_type=jnp.float32)


def dot_t(a, b):
    return lax.dot_general(a, b, (((0,), (0,)), ((), ())), preferred_element_type=jnp.float32)


def ordered(upper_side, own, other):
    return jnp.where(
        upper_side, jnp.concatenate([other, own], 0), jnp.concatenate([own, other], 0)
    )


def level_step(current, project_basis, update_basis, caps_rows, level_num):
    leaf_rows = current.shape[0]
    shift_bits = level_num - 1
    partial_value = dot_t(project_basis, current.astype(BF)) * (
        1.0 / math.sqrt(leaf_rows * 2**shift_bits)
    )
    for bit_index in range(shift_bits):
        partial_value = partial_value + swap(partial_value, "leaf", 2**bit_index)
    own = partial_value.astype(BF)
    other = swap(own, "leaf", 2**shift_bits)
    upper_side = (lax.axis_index("leaf") >> shift_bits) & 1 == 1
    stacked = ordered(upper_side, own, other)
    weights = dot(caps_rows, stacked).astype(BF)
    return current - dot(update_basis, weights)


def top_step(current, project_basis, update_basis, caps_rows):
    leaf_count = lax.axis_size("leaf")
    partial_value = dot_t(project_basis, current.astype(BF)) * (
        1.0 / math.sqrt(leaf_count * current.shape[0])
    )
    column_total = lax.psum(partial_value, "leaf")
    stacked = lax.all_gather(column_total.astype(BF), "top", axis=0, tiled=True)
    weights = dot(caps_rows, stacked).astype(BF)
    return current - dot(update_basis, weights)


def step_by_step(
    right_side, leaf_inverse, left_basis, right_basis, level_caps, top_left, top_right, top_caps
):
    levels = left_basis.shape[0]
    lefts = [left_basis[k, 0] for k in range(levels)]
    rights = [right_basis[k, 0] for k in range(levels)]
    current = dot(leaf_inverse[0], right_side[0].astype(BF))
    for k in range(levels):
        current = level_step(current, rights[k], lefts[k], level_caps[k, 0], k + 1)
    current = top_step(current, top_right[0], top_left[0], top_caps)
    current = top_step(current, top_left[0], top_right[0], top_caps)
    for k in reversed(range(levels)):
        current = level_step(current, lefts[k], rights[k], level_caps[k, 0], k + 1)
    return dot_t(leaf_inverse[0], current.astype(BF))[None]


def in_hbm(value):
    return pltpu.with_memory_space_constraint(value, pltpu.HBM)


def in_vmem(value):
    return pltpu.with_memory_space_constraint(value, pltpu.VMEM)


def call(body, outs, *args, scratch=(), hbm=(), hbm_out=False, micros=1):
    vmem = pl.BlockSpec(memory_space=pltpu.VMEM)
    anywhere = pl.BlockSpec(memory_space=pl.ANY)
    return pl.pallas_call(
        body,
        out_shape=[
            jax.ShapeDtypeStruct(shape, dtype) if hbm_out else pltpu.VMEM(shape, dtype)
            for shape, dtype in outs
        ],
        in_specs=[anywhere if i in hbm else vmem for i in range(len(args))],
        out_specs=[anywhere if hbm_out else vmem] * len(outs),
        scratch_shapes=list(scratch),
        compiler_params=pltpu.CompilerParams(vmem_limit_bytes=VMEM_LIMIT),
        cost_estimate=pl.CostEstimate(
            flops=int(micros * FLOPS_PER_MICRO), bytes_accessed=0, transcendentals=0
        ),
    )(*[in_hbm(a) if i in hbm else in_vmem(a) for i, a in enumerate(args)])


def after(value, *others):
    return lax.optimization_barrier((value, *others))[0]


def tree_side(bit):
    return (lax.axis_index("leaf") >> bit) & 1


def column_side():
    leaf = lax.axis_index("leaf")
    return (leaf ^ (leaf >> 1)) & 1


def block(index, width):
    return pl.ds(pl.multiple_of(index * width, width), width)


def put_rows(scratch, upper, own, other):
    rows = own.shape[0]
    scratch[block(upper, rows), :] = own
    scratch[block(1 - upper, rows), :] = other


def two_levels(
    right_side, leaf_inverse, left_basis, right_basis, level_caps, top_left, top_right, top_caps
):
    rows, cols = right_side.shape[1:]
    rank = top_left.shape[2]
    f32 = jnp.float32
    s1 = 1.0 / math.sqrt(rows)
    s2 = 1.0 / math.sqrt(rows * 2)
    st = 1.0 / math.sqrt(rows * 4)
    blocks = rows // rank
    square, wide, tall = (rank, rank), (rank, cols), (rows, cols)

    def span(i, n=1):
        return slice(i * rank, (i + n) * rank)

    def start_body(
        rhs_hbm, inv_hbm, lb_hbm, rb_hbm, caps_hbm, tl_hbm, tr_hbm,
        x_ref, send, inv_ref, lb, rb, caps, tl, tr, rhs_v, basis_t, sems,
    ):
        def load(source, target, *at):
            copy = pltpu.make_async_copy(source, target, sems.at[at])
            copy.start()
            return copy

        first = load(rb_hbm.at[0], rb.at[0], 2, 0)
        groups = [(i, min(2, blocks - i)) for i in range(0, blocks, 2)]
        copies = []
        for i, n in groups:
            copies.append(load(rhs_hbm.at[0, span(i, n), :], rhs_v.at[span(i, n), :], 0, i))
            copies.append(
                load(
                    inv_hbm.at[0, span(i, n), span(0, i + n)],
                    inv_ref.at[span(i, n), span(0, i + n)],
                    1,
                    i,
                )
            )
        pairs = (rb_hbm.at[1], rb.at[1]), (lb_hbm, lb), (tl_hbm, tl), (tr_hbm, tr), (caps_hbm, caps)
        bases = [load(source, target, 2, 1 + i) for i, (source, target) in enumerate(pairs)]
        first.wait()
        basis_t[...] = rb[0, 0].T
        for i, n in groups:
            copies[i].wait()
            copies[i + 1].wait()
            x_ref[span(i, n), :] = dot(
                inv_ref[span(i, n), span(0, i + n)], rhs_v[span(0, i + n), :].astype(BF)
            )
        send[...] = (dot(basis_t[...], x_ref[...].astype(BF)) * s1).astype(BF)
        for copy in bases:
            copy.wait()

    state0, proj1, inverse, lb, rb, caps, tl, tr = call(
        start_body,
        [(tall, f32), (wide, BF), ((rows, rows), BF)]
        + [(a.shape, a.dtype) for a in (left_basis, right_basis, level_caps, top_left, top_right)],
        right_side,
        leaf_inverse,
        left_basis,
        right_basis,
        level_caps,
        top_left,
        top_right,
        hbm=range(7),
        scratch=[
            pltpu.VMEM(tall, f32),
            pltpu.VMEM((rank, rows), BF),
            pltpu.SemaphoreType.DMA((3, max(blocks, 6))),
        ],
    )
    proj1_sib = swap(proj1, "leaf", 1)
    proj1_near = swap(proj1, "top", 1)

    def early_body(lb, caps, tl, tr, seen, send, keep, scratch):
        side = column_side()
        for i, basis in enumerate((tr, tl)):
            gram = (dot_t(basis[0], lb[1, 0]) * st).astype(BF)
            scratch[i] = dot(gram, caps[1, 0]).astype(BF)
        send[:, : 2 * rank] = scratch[1 - side]
        send[:, span(2)] = (dot_t(tl[0], tl[0]) * st).astype(BF)
        keep[...] = scratch[side]

    early, early_keep = call(
        early_body,
        [((rank, 3 * rank), BF), ((rank, 2 * rank), BF)],
        lb,
        caps,
        tl,
        tr,
        proj1_near,
        scratch=[pltpu.VMEM((2, rank, 2 * rank), BF)],
        micros=10,
    )
    early_sib = swap(early, "leaf", 1)

    def flip_body(lb, rb, tl, tr, seen, out, out2):
        for i, basis in enumerate((rb[1, 0], tr[0], tl[0])):
            out[span(i), :] = basis.T
        for i, basis in enumerate((lb[1, 0], lb[0, 0])):
            out2[span(i), :] = basis.T

    bases_t, lefts_t = call(
        flip_body,
        [((3 * rank, rows), BF), ((2 * rank, rows), BF)],
        lb,
        rb,
        tl,
        tr,
        early,
        micros=0.2,
    )

    def one_body(x0, p, p_sib, lb, caps, bases_t, x1, send, keep, stack, seen):
        side = column_side()
        put_rows(stack, tree_side(0), p[...], p_sib[...])
        coef = dot(caps[0, 0], stack[...]).astype(BF)
        x1[...] = x0[...] - dot(lb[0, 0], coef)
        seen[...] = dot(bases_t[...], x1[...].astype(BF))
        keep[:, :cols] = seen[span(0), :] * s2
        send[:, :cols] = keep[:, :cols].astype(BF)
        send[:, cols:] = (seen[block(2 - side, rank), :] * st).astype(BF)
        keep[:, cols:] = seen[block(1 + side, rank), :] * st

    state1, pair_send, pair_keep = call(
        one_body,
        [(tall, f32), ((rank, 2 * cols), BF), ((rank, 2 * cols), f32)],
        state0,
        proj1,
        proj1_sib,
        lb,
        caps,
        bases_t,
        scratch=[pltpu.VMEM((2 * rank, cols), BF), pltpu.VMEM((3 * rank, cols), f32)],
        micros=3,
    )
    pair_in = swap(pair_send, "leaf", 1)

    def pair_body(mine, own, sib, seen, send, keep, gram, scratch):
        upper = tree_side(1)
        scratch[...] = (mine[...].astype(f32) + sib[:, : 2 * rank]).astype(BF)
        keep[:, span(0)] = scratch[:, block(upper, rank)]
        keep[:, span(1)] = scratch[:, block(1 - upper, rank)]
        send[:, span(0)] = keep[:, span(1)]
        gram[...] = own[:, span(2)].astype(f32) + sib[:, span(2)]
        send[:, span(1)] = gram[...].astype(BF)

    next_send, next_keep, gram_pair = call(
        pair_body,
        [((rank, 2 * rank), BF), ((rank, 2 * rank), BF), (square, f32)],
        early_keep,
        early,
        early_sib,
        state1,
        scratch=[pltpu.VMEM((rank, 2 * rank), BF)],
        micros=1,
    )
    next_far = swap(next_send, "leaf", 3)
    def half_body(keep, pair, nexts, send, keep2):
        send[:, :cols] = (keep[:, :cols] + pair[:, :cols]).astype(BF)
        keep2[...] = keep[:, cols:] + pair[:, cols:] - dot(nexts[:, span(0)], send[:, :cols])
        send[:, cols:] = keep2[...].astype(BF)

    cross_send, cross_keep = call(
        half_body,
        [((rank, 2 * cols), BF), (wide, f32)],
        pair_keep,
        pair_in,
        next_keep,
        micros=5,
    )
    cross_in = swap(cross_send, "leaf", 3)

    def turn_body(gram, far, caps, seen, out):
        whole = (gram[...] + far[:, span(1)]).astype(BF)
        out[...] = dot(whole, caps[...]).astype(BF)

    (turn,) = call(
        turn_body, [(top_caps.shape, BF)], gram_pair, next_far, top_caps, cross_send, micros=0.1
    )
    turn_far = swap(turn, "top", 2)
    turn_near = swap(turn, "top", 1)
    def late_body(lb, rb, caps, tl, tr, seen, seen2, out):
        for i, basis in enumerate((tl[0], tr[0])):
            out[:, span(i)] = (dot_t(lb[0, 0], basis) * s1).astype(BF)
            out[:, span(4 + i)] = (dot_t(lb[1, 0], basis) * s2).astype(BF)
        gram = (dot_t(lb[0, 0], rb[1, 0]) * s1).astype(BF)
        out[:, span(2, 2)] = dot(gram, caps[1, 0]).astype(BF)

    (late,) = call(
        late_body,
        [((rank, 6 * rank), BF)],
        lb,
        rb,
        caps,
        tl,
        tr,
        cross_send,
        next_far,
        micros=5,
    )

    late_sib = swap(late, "leaf", 1)

    def column_body(send, keep2, far, nexts, nexts_far, seen, out):
        out[...] = (
            keep2[...]
            + far[:, cols:]
            - dot(nexts[:, span(1)], far[:, :cols])
            - dot(nexts_far[:, span(0)], send[:, :cols])
        ).astype(BF)

    (top_send,) = call(
        column_body,
        [(wide, BF)],
        cross_send,
        cross_keep,
        cross_in,
        next_keep,
        next_far,
        late,
        micros=0.2,
    )
    top_far = swap(top_send, "top", 2)

    def two_body(x1, send, far, lb, caps, lefts_t, seen, x2, z5, z, stack, both):
        put_rows(stack, tree_side(1), send[:, :cols], far[:, :cols])
        coef = dot(caps[1, 0], stack[...]).astype(BF)
        x2[...] = (x1[...] - dot(lb[1, 0], coef)).astype(BF)
        both[...] = dot(lefts_t[...], x2[...])
        z5[...] = both[span(0), :] * s2
        z[:, :cols] = z5[...].astype(BF)
        z[:, cols:] = (both[span(1), :] * s1).astype(BF)

    state2, down5, down_send = call(
        two_body,
        [(tall, BF), (wide, f32), ((rank, 2 * cols), BF)],
        state1,
        cross_send,
        cross_in,
        lb,
        caps,
        lefts_t,
        top_send,
        scratch=[pltpu.VMEM((2 * rank, cols), BF), pltpu.VMEM((2 * rank, cols), f32)],
        micros=0.1,
    )
    down_in = swap(down_send, "leaf", 1)
    top_near = swap(after(top_send, state2), "top", 1)
    top_parts = top_send, top_near, top_far, swap(top_far, "top", 1)

    turn_far_near = swap(after(turn_far, top_far), "top", 1)

    def order_body(a, b, c, d, caps, out, row):
        here = lax.axis_index("top")
        for k in range(4):
            for i, piece in enumerate((a, b, c, d)):
                out[span(i), span(k)] = piece[:, block(here ^ k, rank)]
            row[:, span(k)] = caps[:, block(here ^ k, rank)]

    turn_all, caps_row = call(
        order_body,
        [((4 * rank, 4 * rank), BF), ((rank, 4 * rank), BF)],
        turn,
        turn_near,
        turn_far,
        turn_far_near,
        top_caps,
        micros=0.1,
    )

    def under_body(x2, rb, tl, tr, inv, seen, out2, under):
        for c in range(blocks):
            column = inv[c * rank :, span(c)]
            out2[span(c), :] = dot_t(column, x2[c * rank :, :])
            for i, basis in enumerate((tl[0], tr[0], rb[1, 0], rb[0, 0])):
                under[span(c), span(i)] = dot_t(column, basis[c * rank :, :]).astype(BF)

    out2, under = call(
        under_body,
        [(tall, f32), ((rows, 4 * rank), BF)],
        state2,
        rb,
        tl,
        tr,
        inverse,
        late_sib,
        micros=3,
    )

    def top_body(a, b, c, d, turns, row, seen, out, up):
        for i, piece in enumerate((a, b, c, d)):
            up[span(i), :] = piece[...]
        turned = dot(turns[...], up[...]).astype(BF)
        out[:, :cols] = dot(row[...], up[...]).astype(BF)
        out[:, cols:] = dot(row[...], turned).astype(BF)

    (back_send,) = call(
        top_body,
        [((rank, 2 * cols), BF)],
        *top_parts,
        turn_all,
        caps_row,
        out2,
        scratch=[pltpu.VMEM((4 * rank, cols), BF)],
        micros=1,
    )
    back_in = swap(back_send, "leaf", 1)

    def down_body(back, back_sib, down5, z_sib, late, late_sib, both, send, pieces):
        side = column_side()
        pieces[side] = back[...]
        pieces[1 - side] = back_sib[...]
        both[span(0), :] = pieces[0, :, :cols]
        both[span(1), :] = (pieces[1, :, :cols].astype(f32) - pieces[0, :, cols:]).astype(BF)
        gram = (late[:, span(4, 2)].astype(f32) + late_sib[:, span(4, 2)]).astype(BF)
        send[...] = (down5[...] + z_sib[:, :cols] - dot(gram, both[...])).astype(BF)

    both, half5 = call(
        down_body,
        [((2 * rank, cols), BF), (wide, BF)],
        back_send,
        back_in,
        down5,
        down_in,
        late,
        late_sib,
        scratch=[pltpu.VMEM((2, rank, 2 * cols), BF)],
        micros=0.3,
    )
    half5_far = swap(half5, "leaf", 2)

    def part_body(out2, under, both, z, z_sib, late, late_sib, seen, proj, out3):
        def down(zs, gram):
            return zs[:, cols:] - dot(gram[:, span(0, 2)], both[...])

        put_rows(proj, tree_side(0), down(z, late), down(z_sib, late_sib))
        out3[...] = out2[...] - dot(under[:, span(0, 2)], both[...])

    proj6, out3 = call(
        part_body,
        [((2 * rank, cols), f32), (tall, f32)],
        out2,
        under,
        both,
        down_send,
        down_in,
        late,
        late_sib,
        half5,
        micros=0.3,
    )

    def last_body(
        out3, under, half5, half5_far, late, late_sib, proj6, caps, out,
        coefs, stack, grams, out_v, sems,
    ):
        put_rows(stack, tree_side(1), half5[...], half5_far[...])
        put_rows(grams, tree_side(0), late[:, span(2, 2)], late_sib[:, span(2, 2)])
        proj = (proj6[...] - dot(grams[...], stack[...])).astype(BF)
        coefs[span(0), :] = dot(caps[1, 0], stack[...]).astype(BF)
        coefs[span(1), :] = dot(caps[0, 0], proj).astype(BF)
        copies = []
        for c in range(blocks):
            out_v[span(c), :] = out3[span(c), :] - dot(under[span(c), span(2, 2)], coefs[...])
            copy = pltpu.make_async_copy(out_v.at[span(c), :], out.at[0, span(c), :], sems.at[c])
            copy.start()
            copies.append(copy)
        for copy in copies:
            copy.wait()

    (out,) = call(
        last_body,
        [((1, rows, cols), f32)],
        out3,
        under,
        half5,
        half5_far,
        late,
        late_sib,
        proj6,
        caps,
        hbm_out=True,
        scratch=[
            pltpu.VMEM((2 * rank, cols), BF),
            pltpu.VMEM((2 * rank, cols), BF),
            pltpu.VMEM((2 * rank, 2 * rank), BF),
            pltpu.VMEM(tall, f32),
            pltpu.SemaphoreType.DMA((blocks,)),
        ],
    )
    return out


def on_device(*args):
    levels = args[2].shape[0]
    sizes = lax.axis_size("leaf"), lax.axis_size("top")
    if levels == 2 and sizes == (4, 4):
        return two_levels(*args)
    return step_by_step(*args)


def solution(mesh):
    rows = P(("parts", "top"), "leaf", None)
    level_rows = P(None, ("parts", "top"), "leaf", None)
    return jax.shard_map(
        on_device,
        mesh=mesh,
        in_specs=(
            rows,
            rows,
            level_rows,
            level_rows,
            level_rows,
            rows,
            rows,
            P(("parts", "top"), None),
        ),
        out_specs=rows,
        check_vma=False,
    )
```

```python
import math

import jax
import jax.numpy as jnp
from jax import lax
from jax.experimental import pallas as pl
from jax.experimental.pallas import tpu as pltpu
from jax.sharding import PartitionSpec as P

BF = jnp.bfloat16
VMEM_LIMIT = 8 * 2**20
FLOPS_PER_MICRO = 1e9


def swap(value, axis, mask):
    pairs = [(source, source ^ mask) for source in range(lax.axis_size(axis))]
    return lax.ppermute(value, axis, pairs)


def dot(a, b):
    return jnp.dot(a, b, preferred_element_type=jnp.float32)


def dot_t(a, b):
    return lax.dot_general(a, b, (((0,), (0,)), ((), ())), preferred_element_type=jnp.float32)


def ordered(upper_side, own, other):
    return jnp.where(
        upper_side, jnp.concatenate([other, own], 0), jnp.concatenate([own, other], 0)
    )


def level_step(current, project_basis, update_basis, caps_rows, level_num):
    leaf_rows = current.shape[0]
    shift_bits = level_num - 1
    partial_value = dot_t(project_basis, current.astype(BF)) * (
        1.0 / math.sqrt(leaf_rows * 2**shift_bits)
    )
    for bit_index in range(shift_bits):
        partial_value = partial_value + swap(partial_value, "leaf", 2**bit_index)
    own = partial_value.astype(BF)
    other = swap(own, "leaf", 2**shift_bits)
    upper_side = (lax.axis_index("leaf") >> shift_bits) & 1 == 1
    stacked = ordered(upper_side, own, other)
    weights = dot(caps_rows, stacked).astype(BF)
    return current - dot(update_basis, weights)


def top_step(current, project_basis, update_basis, caps_rows):
    leaf_count = lax.axis_size("leaf")
    partial_value = dot_t(project_basis, current.astype(BF)) * (
        1.0 / math.sqrt(leaf_count * current.shape[0])
    )
    column_total = lax.psum(partial_value, "leaf")
    stacked = lax.all_gather(column_total.astype(BF), "top", axis=0, tiled=True)
    weights = dot(caps_rows, stacked).astype(BF)
    return current - dot(update_basis, weights)


def step_by_step(
    right_side, leaf_inverse, left_basis, right_basis, level_caps, top_left, top_right, top_caps
):
    levels = left_basis.shape[0]
    lefts = [left_basis[k, 0] for k in range(levels)]
    rights = [right_basis[k, 0] for k in range(levels)]
    current = dot(leaf_inverse[0], right_side[0].astype(BF))
    for k in range(levels):
        current = level_step(current, rights[k], lefts[k], level_caps[k, 0], k + 1)
    current = top_step(current, top_right[0], top_left[0], top_caps)
    current = top_step(current, top_left[0], top_right[0], top_caps)
    for k in reversed(range(levels)):
        current = level_step(current, lefts[k], rights[k], level_caps[k, 0], k + 1)
    return dot_t(leaf_inverse[0], current.astype(BF))[None]


def in_hbm(value):
    return pltpu.with_memory_space_constraint(value, pltpu.HBM)


def in_vmem(value):
    return pltpu.with_memory_space_constraint(value, pltpu.VMEM)


def call(body, outs, *args, scratch=(), hbm=(), hbm_out=False, micros=1):
    vmem = pl.BlockSpec(memory_space=pltpu.VMEM)
    anywhere = pl.BlockSpec(memory_space=pl.ANY)
    return pl.pallas_call(
        body,
        out_shape=[
            jax.ShapeDtypeStruct(shape, dtype) if hbm_out else pltpu.VMEM(shape, dtype)
            for shape, dtype in outs
        ],
        in_specs=[anywhere if i in hbm else vmem for i in range(len(args))],
        out_specs=[anywhere if hbm_out else vmem] * len(outs),
        scratch_shapes=list(scratch),
        compiler_params=pltpu.CompilerParams(vmem_limit_bytes=VMEM_LIMIT),
        cost_estimate=pl.CostEstimate(
            flops=int(micros * FLOPS_PER_MICRO), bytes_accessed=0, transcendentals=0
        ),
    )(*[in_hbm(a) if i in hbm else in_vmem(a) for i, a in enumerate(args)])


def after(value, *others):
    return lax.optimization_barrier((value, *others))[0]


def tree_side(bit):
    return (lax.axis_index("leaf") >> bit) & 1


def column_side():
    leaf = lax.axis_index("leaf")
    return (leaf ^ (leaf >> 1)) & 1


def block(index, width):
    return pl.ds(pl.multiple_of(index * width, width), width)


def put_rows(scratch, upper, own, other):
    rows = own.shape[0]
    scratch[block(upper, rows), :] = own
    scratch[block(1 - upper, rows), :] = other


def two_levels(
    right_side, leaf_inverse, left_basis, right_basis, level_caps, top_left, top_right, top_caps
):
    rows, cols = right_side.shape[1:]
    rank = top_left.shape[2]
    f32 = jnp.float32
    s1 = 1.0 / math.sqrt(rows)
    s2 = 1.0 / math.sqrt(rows * 2)
    st = 1.0 / math.sqrt(rows * 4)
    blocks = rows // rank
    upper = (blocks + 1) // 2
    groups = [(i, n) for i, n in ((0, upper), (upper, blocks - upper)) if n]
    square, wide, tall = (rank, rank), (rank, cols), (rows, cols)

    def span(i, n=1):
        return slice(i * rank, (i + n) * rank)

    def start_body(
        rhs_hbm, inv_hbm, lb_hbm, rb_hbm, caps_hbm, tl_hbm, tr_hbm,
        x_ref, send, inv_ref, lb, rb, caps, tl, tr, rhs_v, basis_t, sems,
    ):
        def load(source, target, *at):
            copy = pltpu.make_async_copy(source, target, sems.at[at])
            copy.start()
            return copy

        first = load(rb_hbm.at[0], rb.at[0], 2, 0)
        copies = []
        for i, n in groups:
            copies.append(load(rhs_hbm.at[0, span(i, n), :], rhs_v.at[span(i, n), :], 0, i))
            copies.append(
                load(
                    inv_hbm.at[0, span(i, n), span(0, i + n)],
                    inv_ref.at[span(i, n), span(0, i + n)],
                    1,
                    i,
                )
            )
        pairs = (rb_hbm.at[1], rb.at[1]), (lb_hbm, lb), (tl_hbm, tl), (tr_hbm, tr), (caps_hbm, caps)
        bases = [load(source, target, 2, 1 + i) for i, (source, target) in enumerate(pairs)]
        first.wait()
        basis_t[...] = rb[0, 0].T
        for (i, n), k in zip(groups, range(0, len(copies), 2)):
            copies[k].wait()
            copies[k + 1].wait()
            x_ref[span(i, n), :] = dot(
                inv_ref[span(i, n), span(0, i + n)], rhs_v[span(0, i + n), :].astype(BF)
            )
        send[...] = (dot(basis_t[...], x_ref[...].astype(BF)) * s1).astype(BF)
        for copy in bases:
            copy.wait()

    state0, proj1, inverse, lb, rb, caps, tl, tr = call(
        start_body,
        [(tall, f32), (wide, BF), ((rows, rows), BF)]
        + [(a.shape, a.dtype) for a in (left_basis, right_basis, level_caps, top_left, top_right)],
        right_side,
        leaf_inverse,
        left_basis,
        right_basis,
        level_caps,
        top_left,
        top_right,
        hbm=range(7),
        scratch=[
            pltpu.VMEM(tall, f32),
            pltpu.VMEM((rank, rows), BF),
            pltpu.SemaphoreType.DMA((3, max(blocks, 6))),
        ],
    )
    proj1_sib = swap(proj1, "leaf", 1)
    proj1_near = swap(proj1, "top", 1)

    def early_body(lb, caps, tl, tr, seen, send, keep, scratch):
        side = column_side()
        for i, basis in enumerate((tr, tl)):
            gram = (dot_t(basis[0], lb[1, 0]) * st).astype(BF)
            scratch[i] = dot(gram, caps[1, 0]).astype(BF)
        send[:, : 2 * rank] = scratch[1 - side]
        send[:, span(2)] = (dot_t(tl[0], tl[0]) * st).astype(BF)
        keep[...] = scratch[side]

    early, early_keep = call(
        early_body,
        [((rank, 3 * rank), BF), ((rank, 2 * rank), BF)],
        lb,
        caps,
        tl,
        tr,
        proj1_near,
        scratch=[pltpu.VMEM((2, rank, 2 * rank), BF)],
        micros=10,
    )
    early_sib = swap(early, "leaf", 1)

    def flip_body(lb, rb, tl, tr, seen, out, out2, out3):
        for i, basis in enumerate((rb[1, 0], tr[0], tl[0])):
            out[span(i), :] = basis.T
        for i, basis in enumerate((lb[1, 0], lb[0, 0])):
            out2[span(i), :] = basis.T
        for i, basis in enumerate((tl[0], tr[0], rb[1, 0], rb[0, 0])):
            out3[:, span(i)] = basis

    bases_t, lefts_t, updates = call(
        flip_body,
        [((3 * rank, rows), BF), ((2 * rank, rows), BF), ((rows, 4 * rank), BF)],
        lb,
        rb,
        tl,
        tr,
        early,
        micros=0.2,
    )

    def one_body(x0, p, p_sib, lb, caps, bases_t, x1, send, keep, stack, seen):
        side = column_side()
        put_rows(stack, tree_side(0), p[...], p_sib[...])
        coef = dot(caps[0, 0], stack[...]).astype(BF)
        x1[...] = x0[...] - dot(lb[0, 0], coef)
        seen[...] = dot(bases_t[...], x1[...].astype(BF))
        keep[:, :cols] = seen[span(0), :] * s2
        send[:, :cols] = keep[:, :cols].astype(BF)
        send[:, cols:] = (seen[block(2 - side, rank), :] * st).astype(BF)
        keep[:, cols:] = seen[block(1 + side, rank), :] * st

    state1, pair_send, pair_keep = call(
        one_body,
        [(tall, f32), ((rank, 2 * cols), BF), ((rank, 2 * cols), f32)],
        state0,
        proj1,
        proj1_sib,
        lb,
        caps,
        bases_t,
        scratch=[pltpu.VMEM((2 * rank, cols), BF), pltpu.VMEM((3 * rank, cols), f32)],
        micros=3,
    )
    pair_in = swap(pair_send, "leaf", 1)

    def pair_body(mine, own, sib, seen, send, keep, gram, scratch):
        upper = tree_side(1)
        scratch[...] = (mine[...].astype(f32) + sib[:, : 2 * rank]).astype(BF)
        keep[:, span(0)] = scratch[:, block(upper, rank)]
        keep[:, span(1)] = scratch[:, block(1 - upper, rank)]
        send[:, span(0)] = keep[:, span(1)]
        gram[...] = own[:, span(2)].astype(f32) + sib[:, span(2)]
        send[:, span(1)] = gram[...].astype(BF)

    next_send, next_keep, gram_pair = call(
        pair_body,
        [((rank, 2 * rank), BF), ((rank, 2 * rank), BF), (square, f32)],
        early_keep,
        early,
        early_sib,
        state1,
        scratch=[pltpu.VMEM((rank, 2 * rank), BF)],
        micros=1,
    )
    next_far = swap(next_send, "leaf", 3)
    def half_body(keep, pair, nexts, send, keep2):
        send[:, :cols] = (keep[:, :cols] + pair[:, :cols]).astype(BF)
        keep2[...] = keep[:, cols:] + pair[:, cols:] - dot(nexts[:, span(0)], send[:, :cols])
        send[:, cols:] = keep2[...].astype(BF)

    cross_send, cross_keep = call(
        half_body,
        [((rank, 2 * cols), BF), (wide, f32)],
        pair_keep,
        pair_in,
        next_keep,
        micros=5,
    )
    cross_in = swap(cross_send, "leaf", 3)

    def turn_body(gram, far, caps, seen, out):
        whole = (gram[...] + far[:, span(1)]).astype(BF)
        out[...] = dot(whole, caps[...]).astype(BF)

    (turn,) = call(
        turn_body, [(top_caps.shape, BF)], gram_pair, next_far, top_caps, cross_send, micros=0.1
    )
    turn_far = swap(turn, "top", 2)
    turn_near = swap(turn, "top", 1)
    def late_body(lb, rb, caps, tl, tr, seen, seen2, out):
        for i, basis in enumerate((tl[0], tr[0])):
            out[:, span(i)] = (dot_t(lb[0, 0], basis) * s1).astype(BF)
            out[:, span(4 + i)] = (dot_t(lb[1, 0], basis) * s2).astype(BF)
        gram = (dot_t(lb[0, 0], rb[1, 0]) * s1).astype(BF)
        out[:, span(2, 2)] = dot(gram, caps[1, 0]).astype(BF)

    (late,) = call(
        late_body,
        [((rank, 6 * rank), BF)],
        lb,
        rb,
        caps,
        tl,
        tr,
        cross_send,
        next_far,
        micros=5,
    )

    late_sib = swap(late, "leaf", 1)

    def column_body(send, keep2, far, nexts, nexts_far, seen, out):
        out[...] = (
            keep2[...]
            + far[:, cols:]
            - dot(nexts[:, span(1)], far[:, :cols])
            - dot(nexts_far[:, span(0)], send[:, :cols])
        ).astype(BF)

    (top_send,) = call(
        column_body,
        [(wide, BF)],
        cross_send,
        cross_keep,
        cross_in,
        next_keep,
        next_far,
        late,
        micros=0.2,
    )
    top_far = swap(top_send, "top", 2)

    def two_body(x1, send, far, lb, caps, lefts_t, seen, x2, z5, z, stack, both):
        put_rows(stack, tree_side(1), send[:, :cols], far[:, :cols])
        coef = dot(caps[1, 0], stack[...]).astype(BF)
        x2[...] = (x1[...] - dot(lb[1, 0], coef)).astype(BF)
        both[...] = dot(lefts_t[...], x2[...])
        z5[...] = both[span(0), :] * s2
        z[:, :cols] = z5[...].astype(BF)
        z[:, cols:] = (both[span(1), :] * s1).astype(BF)

    state2, down5, down_send = call(
        two_body,
        [(tall, BF), (wide, f32), ((rank, 2 * cols), BF)],
        state1,
        cross_send,
        cross_in,
        lb,
        caps,
        lefts_t,
        top_send,
        scratch=[pltpu.VMEM((2 * rank, cols), BF), pltpu.VMEM((2 * rank, cols), f32)],
        micros=0.1,
    )
    down_in = swap(down_send, "leaf", 1)
    top_near = swap(after(top_send, state2), "top", 1)
    top_parts = top_send, top_near, top_far, swap(top_far, "top", 1)

    turn_far_near = swap(after(turn_far, top_far), "top", 1)

    def order_body(a, b, c, d, caps, out, row):
        here = lax.axis_index("top")
        for k in range(4):
            for i, piece in enumerate((a, b, c, d)):
                out[span(i), span(k)] = piece[:, block(here ^ k, rank)]
            row[:, span(k)] = caps[:, block(here ^ k, rank)]

    turn_all, caps_row = call(
        order_body,
        [((4 * rank, 4 * rank), BF), ((rank, 4 * rank), BF)],
        turn,
        turn_near,
        turn_far,
        turn_far_near,
        top_caps,
        micros=0.1,
    )

    def under_body(x2, updates, inv, seen, out2, under):
        for i, n in groups:
            column = inv[i * rank :, span(i, n)]
            out2[span(i, n), :] = dot_t(column, x2[i * rank :, :])
            under[span(i, n), :] = dot_t(column, updates[i * rank :, :]).astype(BF)

    out2, under = call(
        under_body,
        [(tall, f32), ((rows, 4 * rank), BF)],
        state2,
        updates,
        inverse,
        late_sib,
        micros=3,
    )

    def top_body(a, b, c, d, turns, row, seen, out, up):
        for i, piece in enumerate((a, b, c, d)):
            up[span(i), :] = piece[...]
        turned = dot(turns[...], up[...]).astype(BF)
        out[:, :cols] = dot(row[...], up[...]).astype(BF)
        out[:, cols:] = dot(row[...], turned).astype(BF)

    (back_send,) = call(
        top_body,
        [((rank, 2 * cols), BF)],
        *top_parts,
        turn_all,
        caps_row,
        out2,
        scratch=[pltpu.VMEM((4 * rank, cols), BF)],
        micros=1,
    )
    back_in = swap(back_send, "leaf", 1)

    def down_body(back, back_sib, down5, z_sib, late, late_sib, both, send, pieces):
        side = column_side()
        pieces[side] = back[...]
        pieces[1 - side] = back_sib[...]
        both[span(0), :] = pieces[0, :, :cols]
        both[span(1), :] = (pieces[1, :, :cols].astype(f32) - pieces[0, :, cols:]).astype(BF)
        gram = (late[:, span(4, 2)].astype(f32) + late_sib[:, span(4, 2)]).astype(BF)
        send[...] = (down5[...] + z_sib[:, :cols] - dot(gram, both[...])).astype(BF)

    both, half5 = call(
        down_body,
        [((2 * rank, cols), BF), (wide, BF)],
        back_send,
        back_in,
        down5,
        down_in,
        late,
        late_sib,
        scratch=[pltpu.VMEM((2, rank, 2 * cols), BF)],
        micros=0.3,
    )
    half5_far = swap(half5, "leaf", 2)

    def part_body(out2, under, both, z, z_sib, late, late_sib, seen, proj, out3):
        def down(zs, gram):
            return zs[:, cols:] - dot(gram[:, span(0, 2)], both[...])

        put_rows(proj, tree_side(0), down(z, late), down(z_sib, late_sib))
        out3[...] = out2[...] - dot(under[:, span(0, 2)], both[...])

    proj6, out3 = call(
        part_body,
        [((2 * rank, cols), f32), (tall, f32)],
        out2,
        under,
        both,
        down_send,
        down_in,
        late,
        late_sib,
        half5,
        micros=0.3,
    )

    def last_body(
        out3, under, half5, half5_far, late, late_sib, proj6, caps, out,
        coefs, stack, grams, out_v, sems,
    ):
        put_rows(stack, tree_side(1), half5[...], half5_far[...])
        put_rows(grams, tree_side(0), late[:, span(2, 2)], late_sib[:, span(2, 2)])
        proj = (proj6[...] - dot(grams[...], stack[...])).astype(BF)
        coefs[span(0), :] = dot(caps[1, 0], stack[...]).astype(BF)
        coefs[span(1), :] = dot(caps[0, 0], proj).astype(BF)
        copies = []
        for c in range(blocks):
            out_v[span(c), :] = out3[span(c), :] - dot(under[span(c), span(2, 2)], coefs[...])
            copy = pltpu.make_async_copy(out_v.at[span(c), :], out.at[0, span(c), :], sems.at[c])
            copy.start()
            copies.append(copy)
        for copy in copies:
            copy.wait()

    (out,) = call(
        last_body,
        [((1, rows, cols), f32)],
        out3,
        under,
        half5,
        half5_far,
        late,
        late_sib,
        proj6,
        caps,
        hbm_out=True,
        scratch=[
            pltpu.VMEM((2 * rank, cols), BF),
            pltpu.VMEM((2 * rank, cols), BF),
            pltpu.VMEM((2 * rank, 2 * rank), BF),
            pltpu.VMEM(tall, f32),
            pltpu.SemaphoreType.DMA((blocks,)),
        ],
    )
    return out


def on_device(*args):
    levels = args[2].shape[0]
    sizes = lax.axis_size("leaf"), lax.axis_size("top")
    if levels == 2 and sizes == (4, 4):
        return two_levels(*args)
    return step_by_step(*args)


def solution(mesh):
    rows = P(("parts", "top"), "leaf", None)
    level_rows = P(None, ("parts", "top"), "leaf", None)
    return jax.shard_map(
        on_device,
        mesh=mesh,
        in_specs=(
            rows,
            rows,
            level_rows,
            level_rows,
            level_rows,
            rows,
            rows,
            P(("parts", "top"), None),
        ),
        out_specs=rows,
        check_vma=False,
    )
```

```python
import math

import jax
import jax.numpy as jnp
from jax import lax
from jax.experimental import pallas as pl
from jax.experimental.pallas import tpu as pltpu
from jax.sharding import PartitionSpec as P

BF = jnp.bfloat16
VMEM_LIMIT = 8 * 2**20
FLOPS_PER_MICRO = 1e9


def swap(value, axis, mask):
    pairs = [(source, source ^ mask) for source in range(lax.axis_size(axis))]
    return lax.ppermute(value, axis, pairs)


def dot(a, b):
    return jnp.dot(a, b, preferred_element_type=jnp.float32)


def dot_t(a, b):
    return lax.dot_general(a, b, (((0,), (0,)), ((), ())), preferred_element_type=jnp.float32)


def ordered(upper_side, own, other):
    return jnp.where(
        upper_side, jnp.concatenate([other, own], 0), jnp.concatenate([own, other], 0)
    )


def level_step(current, project_basis, update_basis, caps_rows, level_num):
    leaf_rows = current.shape[0]
    shift_bits = level_num - 1
    partial_value = dot_t(project_basis, current.astype(BF)) * (
        1.0 / math.sqrt(leaf_rows * 2**shift_bits)
    )
    for bit_index in range(shift_bits):
        partial_value = partial_value + swap(partial_value, "leaf", 2**bit_index)
    own = partial_value.astype(BF)
    other = swap(own, "leaf", 2**shift_bits)
    upper_side = (lax.axis_index("leaf") >> shift_bits) & 1 == 1
    stacked = ordered(upper_side, own, other)
    weights = dot(caps_rows, stacked).astype(BF)
    return current - dot(update_basis, weights)


def top_step(current, project_basis, update_basis, caps_rows):
    leaf_count = lax.axis_size("leaf")
    partial_value = dot_t(project_basis, current.astype(BF)) * (
        1.0 / math.sqrt(leaf_count * current.shape[0])
    )
    column_total = lax.psum(partial_value, "leaf")
    stacked = lax.all_gather(column_total.astype(BF), "top", axis=0, tiled=True)
    weights = dot(caps_rows, stacked).astype(BF)
    return current - dot(update_basis, weights)


def step_by_step(
    right_side, leaf_inverse, left_basis, right_basis, level_caps, top_left, top_right, top_caps
):
    levels = left_basis.shape[0]
    lefts = [left_basis[k, 0] for k in range(levels)]
    rights = [right_basis[k, 0] for k in range(levels)]
    current = dot(leaf_inverse[0], right_side[0].astype(BF))
    for k in range(levels):
        current = level_step(current, rights[k], lefts[k], level_caps[k, 0], k + 1)
    current = top_step(current, top_right[0], top_left[0], top_caps)
    current = top_step(current, top_left[0], top_right[0], top_caps)
    for k in reversed(range(levels)):
        current = level_step(current, lefts[k], rights[k], level_caps[k, 0], k + 1)
    return dot_t(leaf_inverse[0], current.astype(BF))[None]


def in_hbm(value):
    return pltpu.with_memory_space_constraint(value, pltpu.HBM)


def in_vmem(value):
    return pltpu.with_memory_space_constraint(value, pltpu.VMEM)


def call(body, outs, *args, scratch=(), hbm=(), hbm_out=False, micros=1):
    vmem = pl.BlockSpec(memory_space=pltpu.VMEM)
    anywhere = pl.BlockSpec(memory_space=pl.ANY)
    return pl.pallas_call(
        body,
        out_shape=[
            jax.ShapeDtypeStruct(shape, dtype) if hbm_out else pltpu.VMEM(shape, dtype)
            for shape, dtype in outs
        ],
        in_specs=[anywhere if i in hbm else vmem for i in range(len(args))],
        out_specs=[anywhere if hbm_out else vmem] * len(outs),
        scratch_shapes=list(scratch),
        compiler_params=pltpu.CompilerParams(vmem_limit_bytes=VMEM_LIMIT),
        cost_estimate=pl.CostEstimate(
            flops=int(micros * FLOPS_PER_MICRO), bytes_accessed=0, transcendentals=0
        ),
    )(*[in_hbm(a) if i in hbm else in_vmem(a) for i, a in enumerate(args)])


def after(value, *others):
    return lax.optimization_barrier((value, *others))[0]


def tree_side(bit):
    return (lax.axis_index("leaf") >> bit) & 1


def column_side():
    leaf = lax.axis_index("leaf")
    return (leaf ^ (leaf >> 1)) & 1


def block(index, width):
    return pl.ds(pl.multiple_of(index * width, width), width)


def put_rows(scratch, upper, own, other):
    rows = own.shape[0]
    scratch[block(upper, rows), :] = own
    scratch[block(1 - upper, rows), :] = other


def two_levels(
    right_side, leaf_inverse, left_basis, right_basis, level_caps, top_left, top_right, top_caps
):
    rows, cols = right_side.shape[1:]
    rank = top_left.shape[2]
    f32 = jnp.float32
    s1 = 1.0 / math.sqrt(rows)
    s2 = 1.0 / math.sqrt(rows * 2)
    st = 1.0 / math.sqrt(rows * 4)
    blocks = rows // rank
    square, wide, tall = (rank, rank), (rank, cols), (rows, cols)

    def span(i, n=1):
        return slice(i * rank, (i + n) * rank)

    def start_body(
        rhs_hbm, inv_hbm, lb_hbm, rb_hbm, caps_hbm, tl_hbm, tr_hbm,
        x_ref, send, inv_ref, lb, rb, caps, tl, tr, rhs_v, basis_t, sems,
    ):
        def load(source, target, *at):
            copy = pltpu.make_async_copy(source, target, sems.at[at])
            copy.start()
            return copy

        first = load(rb_hbm.at[0], rb.at[0], 2, 0)
        groups = [(i, min(2, blocks - i)) for i in range(0, blocks, 2)]
        copies = []
        for i, n in groups:
            copies.append(load(rhs_hbm.at[0, span(i, n), :], rhs_v.at[span(i, n), :], 0, i))
            copies.append(
                load(
                    inv_hbm.at[0, span(i, n), span(0, i + n)],
                    inv_ref.at[span(i, n), span(0, i + n)],
                    1,
                    i,
                )
            )
        pairs = (rb_hbm.at[1], rb.at[1]), (lb_hbm, lb), (tl_hbm, tl), (tr_hbm, tr), (caps_hbm, caps)
        bases = [load(source, target, 2, 1 + i) for i, (source, target) in enumerate(pairs)]
        first.wait()
        basis_t[...] = rb[0, 0].T
        for i, n in groups:
            copies[i].wait()
            copies[i + 1].wait()
            x_ref[span(i, n), :] = dot(
                inv_ref[span(i, n), span(0, i + n)], rhs_v[span(0, i + n), :].astype(BF)
            )
        send[...] = (dot(basis_t[...], x_ref[...].astype(BF)) * s1).astype(BF)
        for copy in bases:
            copy.wait()

    state0, proj1, inverse, lb, rb, caps, tl, tr = call(
        start_body,
        [(tall, f32), (wide, BF), ((rows, rows), BF)]
        + [(a.shape, a.dtype) for a in (left_basis, right_basis, level_caps, top_left, top_right)],
        right_side,
        leaf_inverse,
        left_basis,
        right_basis,
        level_caps,
        top_left,
        top_right,
        hbm=range(7),
        scratch=[
            pltpu.VMEM(tall, f32),
            pltpu.VMEM((rank, rows), BF),
            pltpu.SemaphoreType.DMA((3, max(blocks, 6))),
        ],
    )
    proj1_sib = swap(proj1, "leaf", 1)
    proj1_near = swap(proj1, "top", 1)

    def early_body(lb, caps, tl, tr, seen, send, keep, scratch):
        side = column_side()
        for i, basis in enumerate((tr, tl)):
            gram = (dot_t(basis[0], lb[1, 0]) * st).astype(BF)
            scratch[i] = dot(gram, caps[1, 0]).astype(BF)
        send[:, : 2 * rank] = scratch[1 - side]
        send[:, span(2)] = (dot_t(tl[0], tl[0]) * st).astype(BF)
        keep[...] = scratch[side]

    early, early_keep = call(
        early_body,
        [((rank, 3 * rank), BF), ((rank, 2 * rank), BF)],
        lb,
        caps,
        tl,
        tr,
        proj1_near,
        scratch=[pltpu.VMEM((2, rank, 2 * rank), BF)],
        micros=10,
    )
    early_sib = swap(early, "leaf", 1)

    def flip_body(lb, rb, tl, tr, seen, out, out2):
        for i, basis in enumerate((rb[1, 0], tr[0], tl[0])):
            out[span(i), :] = basis.T
        for i, basis in enumerate((lb[1, 0], lb[0, 0])):
            out2[span(i), :] = basis.T

    bases_t, lefts_t = call(
        flip_body,
        [((3 * rank, rows), BF), ((2 * rank, rows), BF)],
        lb,
        rb,
        tl,
        tr,
        early,
        micros=0.2,
    )

    def one_body(x0, p, p_sib, lb, caps, bases_t, x1, send, keep, stack, seen):
        side = column_side()
        put_rows(stack, tree_side(0), p[...], p_sib[...])
        coef = dot(caps[0, 0], stack[...]).astype(BF)
        x1[...] = x0[...] - dot(lb[0, 0], coef)
        seen[...] = dot(bases_t[...], x1[...].astype(BF))
        keep[:, :cols] = seen[span(0), :] * s2
        send[:, :cols] = keep[:, :cols].astype(BF)
        send[:, cols:] = (seen[block(2 - side, rank), :] * st).astype(BF)
        keep[:, cols:] = seen[block(1 + side, rank), :] * st

    state1, pair_send, pair_keep = call(
        one_body,
        [(tall, f32), ((rank, 2 * cols), BF), ((rank, 2 * cols), f32)],
        state0,
        proj1,
        proj1_sib,
        lb,
        caps,
        bases_t,
        scratch=[pltpu.VMEM((2 * rank, cols), BF), pltpu.VMEM((3 * rank, cols), f32)],
        micros=3,
    )
    pair_in = swap(pair_send, "leaf", 1)

    def pair_body(mine, own, sib, seen, send, keep, gram, scratch):
        upper = tree_side(1)
        scratch[...] = (mine[...].astype(f32) + sib[:, : 2 * rank]).astype(BF)
        keep[:, span(0)] = scratch[:, block(upper, rank)]
        keep[:, span(1)] = scratch[:, block(1 - upper, rank)]
        send[:, span(0)] = keep[:, span(1)]
        gram[...] = own[:, span(2)].astype(f32) + sib[:, span(2)]
        send[:, span(1)] = gram[...].astype(BF)

    next_send, next_keep, gram_pair = call(
        pair_body,
        [((rank, 2 * rank), BF), ((rank, 2 * rank), BF), (square, f32)],
        early_keep,
        early,
        early_sib,
        state1,
        scratch=[pltpu.VMEM((rank, 2 * rank), BF)],
        micros=1,
    )
    next_far = swap(next_send, "leaf", 3)
    def half_body(keep, pair, nexts, send, keep2):
        send[:, :cols] = (keep[:, :cols] + pair[:, :cols]).astype(BF)
        keep2[...] = keep[:, cols:] + pair[:, cols:] - dot(nexts[:, span(0)], send[:, :cols])
        send[:, cols:] = keep2[...].astype(BF)

    cross_send, cross_keep = call(
        half_body,
        [((rank, 2 * cols), BF), (wide, f32)],
        pair_keep,
        pair_in,
        next_keep,
        micros=5,
    )
    cross_in = swap(cross_send, "leaf", 3)

    def turn_body(gram, far, caps, seen, out):
        whole = (gram[...] + far[:, span(1)]).astype(BF)
        out[...] = dot(whole, caps[...]).astype(BF)

    (turn,) = call(
        turn_body, [(top_caps.shape, BF)], gram_pair, next_far, top_caps, cross_send, micros=0.1
    )
    turn_far = swap(turn, "top", 2)
    turn_near = swap(turn, "top", 1)
    def late_body(lb, rb, caps, tl, tr, seen, seen2, out):
        for i, basis in enumerate((tl[0], tr[0])):
            out[:, span(i)] = (dot_t(lb[0, 0], basis) * s1).astype(BF)
            out[:, span(4 + i)] = (dot_t(lb[1, 0], basis) * s2).astype(BF)
        gram = (dot_t(lb[0, 0], rb[1, 0]) * s1).astype(BF)
        out[:, span(2, 2)] = dot(gram, caps[1, 0]).astype(BF)

    (late,) = call(
        late_body,
        [((rank, 6 * rank), BF)],
        lb,
        rb,
        caps,
        tl,
        tr,
        cross_send,
        next_far,
        micros=5,
    )

    late_sib = swap(late, "leaf", 1)

    def column_body(send, keep2, far, nexts, nexts_far, seen, out):
        out[...] = (
            keep2[...]
            + far[:, cols:]
            - dot(nexts[:, span(1)], far[:, :cols])
            - dot(nexts_far[:, span(0)], send[:, :cols])
        ).astype(BF)

    (top_send,) = call(
        column_body,
        [(wide, BF)],
        cross_send,
        cross_keep,
        cross_in,
        next_keep,
        next_far,
        late,
        micros=0.2,
    )
    top_far = swap(top_send, "top", 2)

    def two_body(x1, send, far, lb, caps, lefts_t, seen, x2, z5, z, stack, both):
        put_rows(stack, tree_side(1), send[:, :cols], far[:, :cols])
        coef = dot(caps[1, 0], stack[...]).astype(BF)
        x2[...] = (x1[...] - dot(lb[1, 0], coef)).astype(BF)
        both[...] = dot(lefts_t[...], x2[...])
        z5[...] = both[span(0), :] * s2
        z[:, :cols] = z5[...].astype(BF)
        z[:, cols:] = (both[span(1), :] * s1).astype(BF)

    state2, down5, down_send = call(
        two_body,
        [(tall, BF), (wide, f32), ((rank, 2 * cols), BF)],
        state1,
        cross_send,
        cross_in,
        lb,
        caps,
        lefts_t,
        top_send,
        scratch=[pltpu.VMEM((2 * rank, cols), BF), pltpu.VMEM((2 * rank, cols), f32)],
        micros=0.1,
    )
    down_in = swap(down_send, "leaf", 1)
    top_near = swap(after(top_send, state2), "top", 1)
    top_parts = top_send, top_near, top_far, swap(top_far, "top", 1)

    turn_far_near = swap(after(turn_far, top_far), "top", 1)

    def order_body(a, b, c, d, caps, out, row):
        here = lax.axis_index("top")
        for k in range(4):
            for i, piece in enumerate((a, b, c, d)):
                out[span(i), span(k)] = piece[:, block(here ^ k, rank)]
            row[:, span(k)] = caps[:, block(here ^ k, rank)]

    turn_all, caps_row = call(
        order_body,
        [((4 * rank, 4 * rank), BF), ((rank, 4 * rank), BF)],
        turn,
        turn_near,
        turn_far,
        turn_far_near,
        top_caps,
        micros=0.1,
    )

    def under_body(x2, rb, tl, tr, inv, seen, out2, under):
        for c in range(blocks):
            column = inv[c * rank :, span(c)]
            out2[span(c), :] = dot_t(column, x2[c * rank :, :])
            for i, basis in enumerate((tl[0], tr[0], rb[1, 0], rb[0, 0])):
                under[span(c), span(i)] = dot_t(column, basis[c * rank :, :]).astype(BF)

    out2, under = call(
        under_body,
        [(tall, f32), ((rows, 4 * rank), BF)],
        state2,
        rb,
        tl,
        tr,
        inverse,
        late_sib,
        micros=3,
    )

    def top_body(a, b, c, d, turns, row, seen, out, up):
        for i, piece in enumerate((a, b, c, d)):
            up[span(i), :] = piece[...]
        turned = dot(turns[...], up[...]).astype(BF)
        out[:, :cols] = dot(row[...], up[...]).astype(BF)
        out[:, cols:] = dot(row[...], turned).astype(BF)

    (back_send,) = call(
        top_body,
        [((rank, 2 * cols), BF)],
        *top_parts,
        turn_all,
        caps_row,
        out2,
        scratch=[pltpu.VMEM((4 * rank, cols), BF)],
        micros=1,
    )
    back_in = swap(back_send, "leaf", 1)

    def down_body(back, back_sib, down5, z_sib, late, late_sib, both, send, pieces):
        side = column_side()
        pieces[side] = back[...]
        pieces[1 - side] = back_sib[...]
        both[span(0), :] = pieces[0, :, :cols]
        both[span(1), :] = (pieces[1, :, :cols].astype(f32) - pieces[0, :, cols:]).astype(BF)
        gram = (late[:, span(4, 2)].astype(f32) + late_sib[:, span(4, 2)]).astype(BF)
        send[...] = (down5[...] + z_sib[:, :cols] - dot(gram, both[...])).astype(BF)

    both, half5 = call(
        down_body,
        [((2 * rank, cols), BF), (wide, BF)],
        back_send,
        back_in,
        down5,
        down_in,
        late,
        late_sib,
        scratch=[pltpu.VMEM((2, rank, 2 * cols), BF)],
        micros=0.3,
    )
    half5_far = swap(half5, "leaf", 2)

    def part_body(out2, under, both, z, z_sib, late, late_sib, seen, proj, out3):
        def down(zs, gram):
            return zs[:, cols:] - dot(gram[:, span(0, 2)], both[...])

        put_rows(proj, tree_side(0), down(z, late), down(z_sib, late_sib))
        out3[...] = out2[...] - dot(under[:, span(0, 2)], both[...])

    proj6, out3 = call(
        part_body,
        [((2 * rank, cols), f32), (tall, f32)],
        out2,
        under,
        both,
        down_send,
        down_in,
        late,
        late_sib,
        half5,
        micros=0.3,
    )

    def last_body(
        out3, under, half5, half5_far, late, late_sib, proj6, caps, out,
        coefs, stack, grams, out_v, sems,
    ):
        put_rows(stack, tree_side(1), half5[...], half5_far[...])
        put_rows(grams, tree_side(0), late[:, span(2, 2)], late_sib[:, span(2, 2)])
        proj = (proj6[...] - dot(grams[...], stack[...])).astype(BF)
        coefs[span(0), :] = dot(caps[1, 0], stack[...]).astype(BF)
        coefs[span(1), :] = dot(caps[0, 0], proj).astype(BF)
        copies = []
        for c in range(0, blocks, 2):
            at = span(c, min(2, blocks - c))
            out_v[at, :] = out3[at, :] - dot(under[at, span(2, 2)], coefs[...])
            copy = pltpu.make_async_copy(out_v.at[at, :], out.at[0, at, :], sems.at[c])
            copy.start()
            copies.append(copy)
        for copy in copies:
            copy.wait()

    (out,) = call(
        last_body,
        [((1, rows, cols), f32)],
        out3,
        under,
        half5,
        half5_far,
        late,
        late_sib,
        proj6,
        caps,
        hbm_out=True,
        scratch=[
            pltpu.VMEM((2 * rank, cols), BF),
            pltpu.VMEM((2 * rank, cols), BF),
            pltpu.VMEM((2 * rank, 2 * rank), BF),
            pltpu.VMEM(tall, f32),
            pltpu.SemaphoreType.DMA((blocks,)),
        ],
    )
    return out


def on_device(*args):
    levels = args[2].shape[0]
    sizes = lax.axis_size("leaf"), lax.axis_size("top")
    if levels == 2 and sizes == (4, 4):
        return two_levels(*args)
    return step_by_step(*args)


def solution(mesh):
    rows = P(("parts", "top"), "leaf", None)
    level_rows = P(None, ("parts", "top"), "leaf", None)
    return jax.shard_map(
        on_device,
        mesh=mesh,
        in_specs=(
            rows,
            rows,
            level_rows,
            level_rows,
            level_rows,
            rows,
            rows,
            P(("parts", "top"), None),
        ),
        out_specs=rows,
        check_vma=False,
    )
```
